32 devices in a mesh: lat: 4 (over y, x), lon: 8 (over z, core).
Axes of the slice: x: 2, y: 2, z: 4, core: 2. Of those that a mesh axis runs over, the one named last changes fastest.
Arguments:
- grad_rows: bfloat16 [32768, 128], P(('lat', 'lon')), may hold values from -6 to 6
- owner: int32 [32768, 1], P(('lat', 'lon')), may hold values from 0 to 31; in each aligned block of 1024 rows (0 to 1023, 1024 to 2047, ...) at most 64 rows name the same one
- lat_offset: int32 [32768], P(('lat', 'lon')), may hold values from 0 to 63
- lon_offset: int32 [32768], P(('lat', 'lon')), may hold values from 0 to 127
- position: bfloat16 [32768, 2], P(('lat', 'lon')), may hold values from 0 to 1
- live_count: int32 [32], P(('lat', 'lon')), may hold values from 512 to 1024
- features: bfloat16 [256, 1024, 128], P('lat', 'lon'), may hold values from -6 to 6
- conv_weight: bfloat16 [3, 3, 128, 128], replicated, may hold values from -0.1875 to 0.1875
Outputs:
- input_grad: bfloat16 [256, 1024, 128], P('lat', 'lon')
- weight_grad: float32 [3, 3, 128, 128], replicated
The draws below stay inside these ranges and needn't reach their ends.
Inputs may be any that keep to these rules, and one draw needn't show every extreme that they name: `owner`: among the 1024 rows of one device no tile is named more than 64 times, a bound that some block reaches. `live_count`: entry k counts the real rows among the rows of device k, which come first.
All inputs are finite; a program needn't handle non-finite values.
Results may differ from the reference program's by a relative error of at most 0.012.
Values may be sent and summed in bfloat16 or wider, within the bound.
A program may use at most 128 MiB of HBM per device.

```python
import math
import jax
import jax.numpy as jnp
import numpy as np
from jax import lax

C = 128
CLAT = 64
CLON = 128
ROWS_DEV = 1024
CAP = 64
NLAT = 256
NLON = 1024
ROWS = 32768
N_LAT = 4
N_LON = 8


def with_ends(drawn, key, least, largest):
    longest = drawn.shape.index(max(drawn.shape))
    spots = []
    for shift in (0, 1):
        where = [jax.random.randint(jax.random.fold_in(key, axis), (), 0, length) for axis, length in enumerate(drawn.shape)]
        where[longest] = (where[longest] + shift) % drawn.shape[longest]
        spots.append(tuple(where))
    return drawn.at[spots[0]].set(least).at[spots[1]].set(largest)


def block_levels(own_key, shape, pieces, smallest, high):
    def one(dim, blocks):
        steps = jax.random.uniform(jax.random.fold_in(jax.random.fold_in(own_key, 6), dim), (blocks,), jnp.float32, smallest / len(pieces), high / len(pieces))
        return jnp.repeat(jnp.exp(steps), shape[dim] // blocks).reshape((-1,) + (1,) * (len(shape) - dim - 1))

    loudness = one(*pieces[0])
    for cut in pieces[1:]:
        loudness = loudness * one(*cut)
    return loudness


def deal_out(own_key, own, number, rows, number_of, top, limit, skew):
    order = jax.random.permutation(own_key, number_of)
    packed, usual = portions_of(number_of, rows * top, limit, skew, True), portions_of(number_of, rows * top, limit, skew, False)
    places = jnp.arange(number_of)

    def named(tallies, offset_by):
        used = int((tallies > 0).sum())
        fixed = max(1, used // 4)
        moved = fixed + (places - fixed + offset_by * (used - fixed)) % max(1, number_of - fixed)
        return jnp.zeros((number_of,), jnp.int32).at[order[jnp.where(places < fixed, places, moved)]].set(jnp.asarray(tallies, jnp.int32))

    tallies = jnp.where(number % 4 == 0, named(packed, number // 4), named(usual, number - number // 4 - 1))
    mixed = jax.random.permutation(jax.random.fold_in(own, 3), number_of)
    giver, receiver = mixed[0:number_of // 2 * 2:2], mixed[1:number_of // 2 * 2:2]
    room = jnp.minimum(tallies[giver] - 1, limit - tallies[receiver]) // 2
    room = jnp.where((giver == order[0]) | (receiver == order[0]) | (tallies[receiver] == 0), 0, jnp.maximum(room, 0))
    moved = jax.random.randint(jax.random.fold_in(own, 4), (number_of // 2,), 0, 1 << 20) % (room + 1)
    tallies = tallies.at[giver].add(-moved).at[receiver].add(moved)
    labels = jnp.searchsorted(jnp.cumsum(tallies), jnp.arange(rows * top), side="right").astype(jnp.int32)
    grid = labels.reshape(top, rows).T
    grid = grid[jax.random.permutation(jax.random.fold_in(own, 1), rows)]
    offset_by = jax.random.randint(jax.random.fold_in(own, 2), (rows, 1), 0, top)
    return jnp.take_along_axis(grid, (jnp.arange(top)[None, :] + offset_by) % top, axis=1)


def portions_of(number_of, total, reach, skew, full):
    portions = [(1 << 20) // math.isqrt(grade ** skew) + 1 for grade in range(1, number_of + 1)]
    largest = reach if full else min(reach, max(-(-total // number_of), total * portions[0] // sum(portions)))
    least = 1 if total - largest >= number_of - 1 else 0
    counts, rest = [largest] + [least] * (number_of - 1), total - largest - least * (number_of - 1)
    while rest > 0:
        movable = [i for i in range(1, number_of) if counts[i] < largest] or [i for i in range(1, number_of) if counts[i] < reach]
        whole, remaining = sum([portions[i] for i in movable]), rest
        for i in movable:
            more = min(reach - counts[i], max(1, remaining * portions[i] // whole), rest)
            counts[i] = counts[i] + more
            rest = rest - more
    return np.array(counts)


def noise(rng, extent, scale, reach, shards=(), kind=jnp.bfloat16):
    drawn = scale * jax.random.normal(rng, extent, jnp.float32)
    if shards:
        drawn = drawn * block_levels(rng, extent, shards, -0.22, 0.18)
    return jnp.clip(drawn, -reach, reach).astype(kind)


def setup_inputs(seed: int = 0) -> dict:
    key_list = jax.random.split(jax.random.key(seed), 9)
    grad_rows = noise(key_list[0], (ROWS, C), 1.0, 6.0, ((0, 32),))
    owner_keys = jax.random.split(jax.random.fold_in(key_list[1], 1), ROWS // ROWS_DEV)
    owner_turns = jax.random.permutation(jax.random.fold_in(key_list[1], 3), ROWS // ROWS_DEV)
    owner = jax.vmap(lambda own, number: deal_out(jax.random.fold_in(key_list[1], 2), own, number, ROWS_DEV, N_LAT * N_LON, 1, CAP, 2))(owner_keys, owner_turns).reshape((ROWS, 1))
    lat_offset = with_ends(jax.random.randint(key_list[2], (ROWS,), 0, CLAT), jax.random.fold_in(key_list[2], 1), 0, CLAT - 1).astype(jnp.int32)
    lon_offset = with_ends(jax.random.randint(key_list[3], (ROWS,), 0, CLON), jax.random.fold_in(key_list[3], 1), 0, CLON - 1).astype(jnp.int32)
    position = jnp.clip(1.0 * jax.random.uniform(key_list[4], (ROWS, 2), jnp.float32) ** block_levels(key_list[4], (ROWS, 2), ((0, 32),), -0.2, 0.2), 0.0, 1.0).astype(jnp.bfloat16)
    live_count = with_ends(jax.random.randint(key_list[5], (N_LAT * N_LON,), ROWS_DEV // 2, ROWS_DEV + 1), jax.random.fold_in(key_list[5], 1), ROWS_DEV // 2, ROWS_DEV).astype(jnp.int32)
    features = noise(key_list[6], (NLAT, NLON, C), 1.0, 6.0, ((0, 4), (1, 8)))
    conv_weight = noise(key_list[7], (3, 3, C, C), (9 * C) ** -0.5, 0.1875)
    return {"grad_rows": grad_rows, "owner": owner, "lat_offset": lat_offset, "lon_offset": lon_offset, "position": position, "live_count": live_count, "features": features, "conv_weight": conv_weight}


rbf_scale = 1.5


def profile(frac):
    tap_index = jnp.arange(8).astype(frac.dtype)
    return jnp.exp(-jnp.square(tap_index[None, :] - 3.0 - frac[:, None]) / (2.0 * rbf_scale * rbf_scale))


def reference(grad_rows, owner, lat_offset, lon_offset, position, live_count, features, conv_weight):
    row_total = grad_rows.shape[0]
    row_ids = jnp.arange(row_total, dtype=jnp.int32)
    is_live = (row_ids % ROWS_DEV) < live_count[row_ids // ROWS_DEV]
    owner_tile = owner[:, 0]
    base_lat = (owner_tile // N_LON) * CLAT + lat_offset - 3
    base_lon = (owner_tile % N_LON) * CLON + lon_offset - 3
    tap_ints = jnp.arange(8, dtype=jnp.int32)
    lat_cell = base_lat[:, None] + tap_ints[None, :]
    lon_cell = (base_lon[:, None] + tap_ints[None, :]) % NLON
    valid = (lat_cell >= 0) & (lat_cell < NLAT) & is_live[:, None]
    cell_index = jnp.where(valid[:, :, None], lat_cell[:, :, None] * NLON + lon_cell[:, None, :], NLAT * NLON).astype(jnp.int32)
    lat_weight = profile(position[:, 0].astype(jnp.float32)).astype(jnp.bfloat16)
    lon_weight = profile(position[:, 1].astype(jnp.float32)).astype(jnp.bfloat16)
    block_rows = math.gcd(row_total, 8192)
    blocks = row_total // block_rows

    def accumulate(canvas, payload):
        rows_blk, lat_blk, lon_blk, index_blk = payload
        spread = lon_blk[:, :, None] * rows_blk[:, None, :]
        updates = lat_blk.astype(jnp.float32)[:, :, None, None] * spread.astype(jnp.float32)[:, None, :, :]
        canvas = canvas.at[index_blk.reshape(-1)].add(updates.reshape(-1, C), mode="drop")
        return canvas, None

    canvas, _ = lax.scan(accumulate, jnp.zeros((NLAT * NLON, C), jnp.float32),
                         (grad_rows.reshape(blocks, block_rows, C), lat_weight.reshape(blocks, block_rows, 8),
                          lon_weight.reshape(blocks, block_rows, 8), cell_index.reshape(blocks, block_rows, 8, 8)))
    grid_grad = canvas.reshape(NLAT, NLON, C).astype(jnp.bfloat16)

    def pad_grid(field):
        padded = jnp.pad(field, ((1, 1), (0, 0), (0, 0)))
        return jnp.concatenate([padded[:, -1:], padded, padded[:, :1]], axis=1)

    grid_padded = pad_grid(grid_grad)
    input_padded = pad_grid(features)
    flat_grad = grid_grad.reshape(-1, C)
    input_grad = jnp.zeros((NLAT * NLON, C), jnp.float32)
    weight_parts = []
    for a in range(3):
        for b in range(3):
            shifted = grid_padded[2 - a:2 - a + NLAT, 2 - b:2 - b + NLON].reshape(-1, C)
            input_grad = input_grad + jnp.dot(shifted, conv_weight[a, b].T, preferred_element_type=jnp.float32)
            window = input_padded[a:a + NLAT, b:b + NLON].reshape(-1, C)
            weight_parts.append(jnp.dot(window.T, flat_grad, preferred_element_type=jnp.float32))
    weight_grad = jnp.stack(weight_parts).reshape(3, 3, C, C)
    return input_grad.reshape(NLAT, NLON, C).astype(jnp.bfloat16), weight_grad
```

```python
import functools
import math

import jax
import jax.numpy as jnp
from jax import lax
from jax.experimental import pallas as pl
from jax.experimental.pallas import tpu as pltpu
from jax.sharding import PartitionSpec as P

rbf_scale = 1.5
taps = 8
before = 3
after = taps - 1 - before
geom_rows = 8
f32 = jnp.float32
bf16 = jnp.bfloat16


def spread_kernel(
    capacity,
    lat_total,
    lon_total,
    tile_lat,
    tile_lon,
    live_ref,
    rows_ref,
    owner_ref,
    lat_ref,
    lon_ref,
    pos_ref,
    own_ref,
    up_ref,
    down_ref,
    left_ref,
    right_ref,
    ul_ref,
    ur_ref,
    dl_ref,
    dr_ref,
    held,
    inbox,
    sums,
    canvas,
    lat_taps,
    lon_taps,
    halves,
    send_sem,
    recv_sem,
):
    devices = inbox.shape[0]
    row_total, channels = rows_ref.shape
    lat, lon = lax.axis_index("lat"), lax.axis_index("lon")
    me = lon * lat_total + lat
    span = halves.shape[0]
    group = span // capacity
    groups = devices // group
    mine = me // group
    half = tile_lon // 2
    inv = 1.0 / (2.0 * rbf_scale * rbf_scale)

    def place(peer):
        return (peer % lat_total, peer // lat_total)

    barrier = pltpu.get_barrier_semaphore()

    def greet(k, _):
        pl.semaphore_signal(
            barrier, inc=1, device_id=place((me + k) % devices), device_id_type=pl.DeviceIdType.MESH
        )
        return 0

    lax.fori_loop(1, devices, greet, 0)

    live = lax.broadcasted_iota(jnp.int32, (1, row_total), 1) < live_ref[0]
    tile = owner_ref[...].astype(f32)
    tile_row = jnp.floor((tile + 0.5) * (1.0 / lon_total))
    owner = (tile - tile_row * lon_total) * lat_total + tile_row
    owner = jnp.where(live, owner, float(devices)).astype(jnp.int32)
    match = lax.broadcasted_iota(jnp.int32, (devices, row_total), 0) == owner
    match = jnp.where(match, 1.0, 0.0)
    blocks = row_total // 128
    upper = lax.broadcasted_iota(jnp.int32, (128, 128), 0) < lax.broadcasted_iota(
        jnp.int32, (128, 128), 1
    )
    upper = jnp.where(upper, 1.0, 0.0).astype(bf16)
    parts = [match[:, k * 128 : (k + 1) * 128] for k in range(blocks)]
    earlier = jnp.dot(
        jnp.concatenate(parts, axis=0).astype(bf16), upper, preferred_element_type=f32
    )
    before_block = jnp.zeros((devices, 1), f32)
    ranks = []
    for k, part in enumerate(parts):
        ahead = earlier[k * devices : (k + 1) * devices] + before_block
        ranks.append(jnp.sum(ahead * part, axis=0, keepdims=True))
        before_block = before_block + jnp.sum(part, axis=1, keepdims=True)
    rank = jnp.concatenate(ranks, axis=1).astype(jnp.int32)
    slot = owner * capacity + rank
    geometry = jnp.concatenate(
        [
            pos_ref[...].astype(f32),
            lat_ref[...].astype(f32),
            lon_ref[...].astype(f32),
            jnp.zeros((geom_rows - 4, row_total), f32),
        ],
        axis=0,
    ).astype(bf16)
    fold = 128 // capacity
    chunk = math.gcd(group, max(1, 256 // capacity))
    line = lax.broadcasted_iota(jnp.int32, (chunk * capacity, row_total), 0)
    lane_block = lax.broadcasted_iota(jnp.int32, (geom_rows, 128), 1) // capacity

    def build(first):
        hit = jnp.where(line == slot - first * capacity, 1.0, 0.0).astype(bf16)
        placed = jnp.dot(hit, rows_ref[...], preferred_element_type=f32).astype(bf16)
        info = lax.dot_general(
            geometry, hit, (((1,), (1,)), ((), ())), preferred_element_type=f32
        )
        for i in range(chunk):
            held[first + i, 0:capacity, :] = placed[i * capacity : (i + 1) * capacity]
        for v in range(chunk // fold):
            piece = info[:, v * 128 : (v + 1) * 128]
            rolled = [piece] + [pltpu.roll(piece, s * capacity, 1) for s in range(1, fold)]
            for i in range(fold):
                tiled = rolled[(fold - i) % fold]
                for t in range(1, fold):
                    tiled = jnp.where(lane_block == t, rolled[(t - i) % fold], tiled)
                held[first + v * fold + i, capacity : capacity + geom_rows, :] = tiled.astype(bf16)

    def copy_to(peer, slot_at):
        return pltpu.make_async_remote_copy(
            src_ref=held.at[peer],
            dst_ref=inbox.at[slot_at],
            send_sem=send_sem.at[peer],
            recv_sem=recv_sem.at[slot_at],
            device_id=place(peer),
            device_id_type=pl.DeviceIdType.MESH,
        )

    def send(first):
        for i in range(chunk):
            peer = first + i

            @pl.when(peer != me)
            def _():
                copy_to(peer, me).start()

    if groups == 4:
        order = [3 - mine, (mine + 2) % 4, mine + 1 - 2 * (mine % 2), mine]
    else:
        order = [(mine + groups // 2 + k) % groups for k in range(groups)]
    per = group // chunk
    steps = [(q, c) for q in order for c in range(per)]
    first_of = [q * group + c * chunk for q, c in steps]
    build(first_of[0])
    pl.semaphore_wait(barrier, devices - 1)
    send(first_of[0])
    for first in first_of[1:]:
        build(first)
        send(first)
    inbox[me] = held[me]

    sums[...] = jnp.zeros_like(sums)
    line_lat = lax.broadcasted_iota(jnp.int32, (lat_taps.shape[0], span), 0).astype(f32)
    line_lon = lax.broadcasted_iota(jnp.int32, (lon_taps.shape[0], span), 0).astype(f32)
    lanes = lax.broadcasted_iota(jnp.int32, (8, 128), 1) // capacity
    wide = sums.shape[1]
    deep = lon_taps.shape[0]
    stride = 8

    def taps_of(line, base, frac):
        tap = line - base
        d = tap - (frac + before)
        weight = jnp.exp(-(d * d) * inv)
        return jnp.where((tap >= 0.0) & (tap <= taps - 1.0), weight, 0.0)

    def collect(q):
        for i in range(group):
            peer = q * group + i

            @pl.when(peer != me)
            def _():
                copy_to(peer, peer).wait_recv()

        first = q * group
        infos = []
        for v in range(span // 128):
            at = first + v * fold
            info = inbox[at, capacity : capacity + geom_rows, :].astype(f32)
            for t in range(1, fold):
                info = jnp.where(
                    lanes == t, inbox[at + t, capacity : capacity + geom_rows, :].astype(f32), info
                )
            infos.append(info)
        info = jnp.concatenate(infos, axis=1)
        lat_frac, lon_frac, row_at, col_at = (info[k : k + 1] for k in range(4))
        right = jnp.where(col_at >= half, 1.0, 0.0)
        lat_taps[...] = taps_of(line_lat, row_at, lat_frac).astype(bf16).astype(f32)
        lon_taps[...] = taps_of(line_lon, col_at - right * half, lon_frac).astype(bf16)
        for v in range(span // 128):
            side = jnp.broadcast_to(right[:, v * 128 : (v + 1) * 128], (128, 128)).T.astype(bf16)
            rows = jnp.concatenate(
                [inbox[first + v * fold + t, 0:capacity, :] for t in range(fold)], axis=0
            )
            at = slice(v * 128, (v + 1) * 128)
            on_right = rows * side
            halves[at, 0:channels] = rows - on_right
            halves[at, channels : 2 * channels] = on_right

        def add(k, _):
            lhs = []
            for j in range(stride):
                row = jnp.broadcast_to(lat_taps[pl.ds(k * stride + j, 1), :], (16, span)).astype(bf16)
                for t in range(deep // 16):
                    lhs.append(row * lon_taps[t * 16 : (t + 1) * 16, :])
            out = jnp.dot(jnp.concatenate(lhs, axis=0), halves[...], preferred_element_type=f32)
            for j in range(stride):
                sums[k * stride + j] += out[j * deep : j * deep + wide]
            return 0

        lax.fori_loop(0, sums.shape[0] // stride, add, 0)

    for q in order[::-1]:
        collect(q)

    rows, cols = own_ref.shape[0], own_ref.shape[1]
    tall = canvas.shape[0]

    def join(i, _):
        canvas[i, 0:half, :] = sums[i, 0:half, 0:channels]
        canvas[i, half:wide, :] = (
            sums[i, half:wide, 0:channels] + sums[i, 0 : wide - half, channels : 2 * channels]
        )
        canvas[i, wide : wide + half, :] = sums[i, wide - half : wide, channels : 2 * channels]
        return 0

    lax.fori_loop(0, tall, join, 0)
    up, down = before + 1, after + 1
    inset = before - 1

    def emit(i, _):
        own_ref[i] = canvas[i + inset, inset : inset + cols, :].astype(bf16)
        left_ref[i] = canvas[i + inset, 0:up, :].astype(bf16)
        right_ref[i] = canvas[i + inset, inset + cols - 2 : inset + cols - 2 + down, :].astype(bf16)
        return 0

    lax.fori_loop(0, rows, emit, 0)
    spans = ((0, up), (inset, cols), (inset + cols - 2, down))
    for count, first, refs in (
        (up, 0, (ul_ref, up_ref, ur_ref)),
        (down, inset + rows - 2, (dl_ref, down_ref, dr_ref)),
    ):
        for i in range(count):
            for (start, width), ref in zip(spans, refs):
                ref[i] = canvas[first + i, start : start + width, :].astype(bf16)

    def each(fn):
        def body(k, _):
            fn((me + k) % devices)
            return 0

        lax.fori_loop(1, devices, body, 0)

    each(lambda peer: copy_to(peer, me).wait_send())


def conv_kernel(
    lat_total,
    lon_total,
    own_ref,
    *refs,
):
    strips, (feat_ref, weight_ref, ig_ref, wg_ref) = refs[:8], refs[8:12]
    landed = refs[12:20]
    (grid, windows, turned, total, flat, mixer, pieces, twin, parts, mine, gathered) = refs[20:31]
    halo_send, halo_recv, pair_send, pair_recv, part_send, part_recv, all_send, all_recv = refs[31:]
    rows, cols = own_ref.shape[0], own_ref.shape[1]
    tile_lat, tile_lon, channels = feat_ref.shape
    up, down = before + 1, after + 1
    devices = lat_total * lon_total
    lat, lon = lax.axis_index("lat"), lax.axis_index("lon")
    me = lat * lon_total + lon
    chips = devices // 2
    core, chip = me % 2, me // 2
    other = 1 - core

    def place(peer):
        return (peer // lon_total, peer % lon_total)

    barrier = pltpu.get_barrier_semaphore()

    def greet(k, _):
        pl.semaphore_signal(
            barrier, inc=1, device_id=place((me + k) % devices), device_id_type=pl.DeviceIdType.MESH
        )
        return 0

    lax.fori_loop(1, devices, greet, 0)

    def fill(i, _):
        grid[i, 0:cols, :] = own_ref[i].astype(f32)
        return 0

    lax.fori_loop(0, rows, fill, 0)
    pl.semaphore_wait(barrier, devices - 1)

    ways = ((-1, 0), (1, 0), (0, -1), (0, 1), (-1, -1), (-1, 1), (1, -1), (1, 1))
    halos = []
    for w, (da, db) in enumerate(ways):
        copy = pltpu.make_async_remote_copy(
            src_ref=strips[w],
            dst_ref=landed[w],
            send_sem=halo_send.at[w],
            recv_sem=halo_recv.at[w],
            device_id=((lat + da + lat_total) % lat_total, (lon + db + lon_total) % lon_total),
            device_id_type=pl.DeviceIdType.MESH,
        )
        sends = (lat + da >= 0) & (lat + da < lat_total)
        takes = (lat - da >= 0) & (lat - da < lat_total)
        halos.append((copy, sends, takes))

    def when(da, cond, fn):
        if da == 0:
            fn()
        else:
            pl.when(cond)(fn)

    for (copy, sends, _), (da, _) in zip(halos, ways):
        when(da, sends, copy.start)

    turned[:, 0 : 2 * tile_lon] = jnp.zeros((channels, 2 * tile_lon), bf16)
    turned[:, rows * tile_lon : (rows + 2) * tile_lon] = jnp.zeros((channels, 2 * tile_lon), bf16)

    def turn(p, _):
        turned[:, pl.ds(pl.multiple_of((p + 2) * tile_lon, tile_lon), tile_lon)] = feat_ref[p].T
        return 0

    lax.fori_loop(0, tile_lat, turn, 0)
    mixer[...] = jnp.zeros_like(mixer)
    for a in range(3):
        for b in range(3):
            tap = weight_ref[a, b].T
            for r in range(2):
                at = ((r + 2 - a) * 3 + b) * channels
                mixer[at : at + channels, r * channels : (r + 1) * channels] = tap
    total[...] = jnp.zeros_like(total)

    for (copy, _, takes), (da, db), ref in zip(halos, ways, landed):

        def take(copy=copy, da=da, db=db, ref=ref):
            copy.wait_recv()
            high = {-1: rows - up, 0: 0, 1: 0}[da]
            count = {-1: up, 0: rows, 1: down}[da]
            left = {-1: cols - up, 0: 0, 1: 0}[db]
            width = {-1: up, 0: cols, 1: down}[db]

            def add(i, _):
                grid[high + i, left : left + width, :] += ref[i].astype(f32)
                return 0

            lax.fori_loop(0, count, add, 0)

        when(da, takes, take)

    @pl.when(lat == 0)
    def _():
        grid[0] = jnp.zeros(grid.shape[1:], f32)

    @pl.when(lat == lat_total - 1)
    def _():
        grid[rows - 1] = jnp.zeros(grid.shape[1:], f32)

    def shift(i, _):
        at = pl.ds(pl.multiple_of(i * tile_lon, tile_lon), tile_lon)
        for b in range(3):
            windows[at, b * channels : (b + 1) * channels] = grid[
                i, 2 - b : 2 - b + tile_lon, :
            ].astype(bf16)
        return 0

    lax.fori_loop(0, rows, shift, 0)
    step = next(n for n in (11, 6, 3, 2, 1) if rows % n == 0)
    depth = step * tile_lon

    def weigh(k, _):
        start = k * depth
        lhs = jnp.concatenate(
            [
                turned[:, pl.ds(pl.multiple_of(start + a * tile_lon, tile_lon), depth)]
                for a in range(3)
            ],
            axis=0,
        )
        rhs = windows[pl.ds(pl.multiple_of(start, tile_lon), depth), :]
        total[...] += jnp.dot(lhs, rhs, preferred_element_type=f32)
        return 0

    lax.fori_loop(0, rows // step, weigh, 0)
    for a in range(3):
        for b in range(3):
            at = (a * 3 + b) * channels
            flat[at : at + channels, :] = total[
                a * channels : (a + 1) * channels, b * channels : (b + 1) * channels
            ]
    share = pieces.shape[1]

    def cut(d, _):
        pieces[d] = flat[pl.ds(d * share, share), :].astype(bf16)
        return 0

    lax.fori_loop(0, devices, cut, 0)
    part = math.gcd(tile_lat // 2, 8)
    strides = tile_lat // 2 // part
    first, second = strides // 4, strides * 3 // 4

    def apply(k, _):
        lhs = jnp.concatenate(
            [
                jnp.concatenate(
                    [
                        windows[
                            pl.ds(
                                pl.multiple_of((2 * (k * part + j) + r) * tile_lon, tile_lon),
                                tile_lon,
                            ),
                            :,
                        ]
                        for r in range(4)
                    ],
                    axis=1,
                )
                for j in range(part)
            ],
            axis=0,
        )
        acc = jnp.dot(lhs, mixer[...], preferred_element_type=f32).astype(bf16)
        for j in range(part):
            for r in range(2):
                ig_ref[2 * (k * part + j) + r] = acc[
                    j * tile_lon : (j + 1) * tile_lon, r * channels : (r + 1) * channels
                ]
        return 0

    def paired(src, dst, n):
        return pltpu.make_async_remote_copy(
            src_ref=src,
            dst_ref=dst,
            send_sem=pair_send.at[n],
            recv_sem=pair_recv.at[n],
            device_id=place(chip * 2 + other),
            device_id_type=pl.DeviceIdType.MESH,
        )

    def scattered(peer, slot):
        return pltpu.make_async_remote_copy(
            src_ref=pieces.at[core * chips + peer],
            dst_ref=parts.at[slot],
            send_sem=part_send.at[peer],
            recv_sem=part_recv.at[slot],
            device_id=place(peer * 2 + core),
            device_id_type=pl.DeviceIdType.MESH,
        )

    def shared(peer, slot):
        return pltpu.make_async_remote_copy(
            src_ref=mine,
            dst_ref=gathered.at[core * chips + slot],
            send_sem=all_send.at[peer],
            recv_sem=all_recv.at[slot],
            device_id=place(peer * 2 + core),
            device_id_type=pl.DeviceIdType.MESH,
        )

    def each(fn):
        def body(k, _):
            fn((chip + k) % chips)
            return 0

        lax.fori_loop(1, chips, body, 0)

    swap = paired(pieces.at[pl.ds(other * chips, chips)], twin, 0)
    swap.start()
    lax.fori_loop(0, first, apply, 0)
    swap.wait_recv()

    def merge(p, _):
        at = core * chips + p
        pieces[at] = (flat[pl.ds(at * share, share), :] + twin[p].astype(f32)).astype(bf16)
        return 0

    lax.fori_loop(0, chips, merge, 0)
    each(lambda peer: scattered(peer, chip).start())
    lax.fori_loop(first, second, apply, 0)
    parts[chip] = pieces[core * chips + chip]
    each(lambda peer: scattered(peer, peer).wait_recv())

    def gather_sum(p, acc):
        return acc + parts[p].astype(f32)

    mine[...] = lax.fori_loop(
        0, chips, gather_sum, jnp.zeros((share, channels), f32)
    ).astype(bf16)
    each(lambda peer: shared(peer, chip).start())
    gathered[core * chips + chip] = mine[...]
    lax.fori_loop(second, strides, apply, 0)
    each(lambda peer: shared(peer, peer).wait_recv())
    held = gathered.at[pl.ds(core * chips, chips)]
    back = paired(held, held, 1)
    back.start()

    def spill(d, _):
        wg_ref[pl.ds(d * share, share), :] = gathered[d].astype(f32)
        return 0

    lax.fori_loop(core * chips, (core + 1) * chips, spill, 0)
    back.wait_recv()
    lax.fori_loop(other * chips, (other + 1) * chips, spill, 0)
    for (copy, sends, _), (da, _) in zip(halos, ways):
        when(da, sends, copy.wait_send)
    swap.wait_send()
    back.wait_send()
    each(lambda peer: scattered(peer, chip).wait_send())
    each(lambda peer: shared(peer, chip).wait_send())


def shards(grad_rows, owner, lat_offset, lon_offset, position, live_count, features, conv_weight):
    lat_total = lax.axis_size("lat")
    lon_total = lax.axis_size("lon")
    device_total = lat_total * lon_total
    row_total, channels = grad_rows.shape
    tile_lat, tile_lon = features.shape[:2]
    capacity = max(2, 2 * row_total // device_total)
    smem = pl.BlockSpec(memory_space=pltpu.SMEM)
    vmem = pl.BlockSpec(memory_space=pltpu.VMEM)

    rows, cols = tile_lat + 2, tile_lon + 2
    tall = -(-(tile_lat + taps - 1) // 8) * 8
    wide = tile_lon // 2 + 8
    span = math.gcd(device_total, max(1, 512 // capacity)) * capacity
    up, down = before + 1, after + 1
    strip_shapes = [
        (up, cols),
        (down, cols),
        (rows, up),
        (rows, down),
        (up, up),
        (up, down),
        (down, up),
        (down, down),
    ]
    message = (device_total, capacity + geom_rows, channels)
    own, *strips = pl.pallas_call(
        functools.partial(spread_kernel, capacity, lat_total, lon_total, tile_lat, tile_lon),
        out_shape=[
            jax.ShapeDtypeStruct(shape + (channels,), bf16)
            for shape in [(rows, cols)] + strip_shapes
        ],
        in_specs=[smem] + [vmem] * 5,
        out_specs=[vmem] * 9,
        scratch_shapes=[
            pltpu.VMEM(message, bf16),
            pltpu.VMEM(message, bf16),
            pltpu.VMEM((tall, wide, 2 * channels), f32),
            pltpu.VMEM((tall, wide + tile_lon // 2, channels), f32),
            pltpu.VMEM((tall, span), f32),
            pltpu.VMEM((-(-wide // 16) * 16, span), bf16),
            pltpu.VMEM((span, 2 * channels), bf16),
            pltpu.SemaphoreType.DMA((device_total,)),
            pltpu.SemaphoreType.DMA((device_total,)),
        ],
        compiler_params=pltpu.CompilerParams(
            vmem_limit_bytes=40 * 2**20, collective_id=1, has_side_effects=True
        ),
        name="spread",
    )(
        live_count,
        grad_rows,
        owner.reshape(1, row_total),
        lat_offset.reshape(1, row_total),
        lon_offset.reshape(1, row_total),
        position.T,
    )
    flat_rows = 9 * channels
    share = flat_rows // device_total
    ring = pltpu.VMEM((device_total, share, channels), bf16)
    half_ring = pltpu.VMEM((device_total // 2, share, channels), bf16)
    input_grad, weight_grad = pl.pallas_call(
        functools.partial(conv_kernel, lat_total, lon_total),
        out_shape=[
            jax.ShapeDtypeStruct((tile_lat, tile_lon, channels), bf16),
            jax.ShapeDtypeStruct((flat_rows, channels), f32),
        ],
        in_specs=[vmem] * 11,
        out_specs=[vmem] * 2,
        scratch_shapes=[pltpu.VMEM(shape + (channels,), bf16) for shape in strip_shapes]
        + [
            pltpu.VMEM((rows, -(-cols // 8) * 8, channels), f32),
            pltpu.VMEM((rows * tile_lon, 3 * channels), bf16),
            pltpu.VMEM((channels, (rows + 2) * tile_lon), bf16),
            pltpu.VMEM((3 * channels, 3 * channels), f32),
            pltpu.VMEM((flat_rows, channels), f32),
            pltpu.VMEM((4 * 3 * channels, 2 * channels), bf16),
            ring,
            half_ring,
            half_ring,
            pltpu.VMEM((share, channels), bf16),
            ring,
            pltpu.SemaphoreType.DMA((8,)),
            pltpu.SemaphoreType.DMA((8,)),
            pltpu.SemaphoreType.DMA((2,)),
            pltpu.SemaphoreType.DMA((2,)),
            pltpu.SemaphoreType.DMA((device_total // 2,)),
            pltpu.SemaphoreType.DMA((device_total // 2,)),
            pltpu.SemaphoreType.DMA((device_total // 2,)),
            pltpu.SemaphoreType.DMA((device_total // 2,)),
        ],
        compiler_params=pltpu.CompilerParams(
            vmem_limit_bytes=36 * 2**20, collective_id=0, has_side_effects=True
        ),
        name="conv",
    )(own, *strips, features, conv_weight)
    return input_grad, weight_grad.reshape(3, 3, channels, channels)


def solution(mesh):
    placed = (
        P(("lat", "lon"), None),
        P(("lat", "lon"), None),
        P(("lat", "lon")),
        P(("lat", "lon")),
        P(("lat", "lon"), None),
        P(("lat", "lon")),
        P("lat", "lon", None),
        P(),
    )
    return jax.shard_map(
        shards, mesh=mesh, in_specs=placed, out_specs=(P("lat", "lon", None), P()), check_vma=False
    )
```

```python
import functools
import math

import jax
import jax.numpy as jnp
from jax import lax
from jax.experimental import pallas as pl
from jax.experimental.pallas import tpu as pltpu
from jax.sharding import PartitionSpec as P

rbf_scale = 1.5
taps = 8
before = 3
after = taps - 1 - before
geom_rows = 8
f32 = jnp.float32
bf16 = jnp.bfloat16


def solve_kernel(
    capacity,
    lat_total,
    lon_total,
    live_ref,
    rows_hbm,
    owner_hbm,
    lat_hbm,
    lon_hbm,
    pos_hbm,
    feat_hbm,
    weight_hbm,
    ig_ref,
    wg_ref,
    *refs,
):
    (rows_ref, owner_ref, lat_ref, lon_ref, pos_ref, feat_ref, weight_ref) = refs[:7]
    (held, inbox, sums, canvas, lat_taps, lon_taps, halves) = refs[7:14]
    strips, landed = refs[14:22], refs[22:30]
    (windows, turned, total, flat, mixer, pieces, twin, parts, mine, gathered) = refs[30:40]
    (load_sem, send_sem, recv_sem) = refs[40:43]
    halo_send, halo_recv, pair_send, pair_recv, part_send, part_recv, all_send, all_recv = refs[43:]
    devices = inbox.shape[0]
    row_total, channels = rows_ref.shape
    tile_lat, tile_lon = feat_ref.shape[:2]
    lat, lon = lax.axis_index("lat"), lax.axis_index("lon")
    me = lon * lat_total + lat
    span = halves.shape[0]
    group = span // capacity
    groups = devices // group
    ours = me // group
    half = tile_lon // 2
    inv = 1.0 / (2.0 * rbf_scale * rbf_scale)

    def place(peer):
        return (peer % lat_total, peer // lat_total)

    barrier = pltpu.get_barrier_semaphore()

    def greet(k, _):
        pl.semaphore_signal(
            barrier, inc=1, device_id=place((me + k) % devices), device_id_type=pl.DeviceIdType.MESH
        )
        return 0

    loads = [
        pltpu.make_async_copy(src, dst, load_sem.at[k])
        for k, (src, dst) in enumerate(
            zip(
                (rows_hbm, owner_hbm, lat_hbm, lon_hbm, pos_hbm, feat_hbm, weight_hbm),
                (rows_ref, owner_ref, lat_ref, lon_ref, pos_ref, feat_ref, weight_ref),
            )
        )
    ]
    for load in loads:
        load.start()
    lax.fori_loop(1, devices, greet, 0)
    sums[...] = jnp.zeros_like(sums)
    mixer[...] = jnp.zeros_like(mixer)
    total[...] = jnp.zeros_like(total)
    rows, cols = tile_lat + 2, tile_lon + 2
    turned[:, 0 : 2 * tile_lon] = jnp.zeros((channels, 2 * tile_lon), bf16)
    turned[:, rows * tile_lon : (rows + 2) * tile_lon] = jnp.zeros((channels, 2 * tile_lon), bf16)
    for load in loads[:5]:
        load.wait()

    live = lax.broadcasted_iota(jnp.int32, (1, row_total), 1) < live_ref[0]
    tile = owner_ref[...].astype(f32)
    tile_row = jnp.floor((tile + 0.5) * (1.0 / lon_total))
    owner = (tile - tile_row * lon_total) * lat_total + tile_row
    owner = jnp.where(live, owner, float(devices)).astype(jnp.int32)
    match = lax.broadcasted_iota(jnp.int32, (devices, row_total), 0) == owner
    match = jnp.where(match, 1.0, 0.0)
    blocks = row_total // 128
    upper = lax.broadcasted_iota(jnp.int32, (128, 128), 0) < lax.broadcasted_iota(
        jnp.int32, (128, 128), 1
    )
    upper = jnp.where(upper, 1.0, 0.0).astype(bf16)
    columns = [match[:, k * 128 : (k + 1) * 128] for k in range(blocks)]
    earlier = jnp.dot(
        jnp.concatenate(columns, axis=0).astype(bf16), upper, preferred_element_type=f32
    )
    before_block = jnp.zeros((devices, 1), f32)
    ranks = []
    for k, part in enumerate(columns):
        ahead = earlier[k * devices : (k + 1) * devices] + before_block
        ranks.append(jnp.sum(ahead * part, axis=0, keepdims=True))
        before_block = before_block + jnp.sum(part, axis=1, keepdims=True)
    rank = jnp.concatenate(ranks, axis=1).astype(jnp.int32)
    slot = owner * capacity + rank
    geometry = jnp.concatenate(
        [
            pos_ref[...].astype(f32),
            lat_ref[...].astype(f32),
            lon_ref[...].astype(f32),
            jnp.zeros((geom_rows - 4, row_total), f32),
        ],
        axis=0,
    ).astype(bf16)
    fold = 128 // capacity
    chunk = math.gcd(group, max(1, 256 // capacity))
    line = lax.broadcasted_iota(jnp.int32, (chunk * capacity, row_total), 0)
    lane_block = lax.broadcasted_iota(jnp.int32, (geom_rows, 128), 1) // capacity

    def build(first):
        hit = jnp.where(line == slot - first * capacity, 1.0, 0.0).astype(bf16)
        placed = jnp.dot(hit, rows_ref[...], preferred_element_type=f32).astype(bf16)
        info = lax.dot_general(
            geometry, hit, (((1,), (1,)), ((), ())), preferred_element_type=f32
        )
        for i in range(chunk):
            held[first + i, 0:capacity, :] = placed[i * capacity : (i + 1) * capacity]
        for v in range(chunk // fold):
            piece = info[:, v * 128 : (v + 1) * 128]
            rolled = [piece] + [pltpu.roll(piece, s * capacity, 1) for s in range(1, fold)]
            for i in range(fold):
                tiled = rolled[(fold - i) % fold]
                for t in range(1, fold):
                    tiled = jnp.where(lane_block == t, rolled[(t - i) % fold], tiled)
                held[first + v * fold + i, capacity : capacity + geom_rows, :] = tiled.astype(bf16)

    def copy_to(peer, slot_at):
        return pltpu.make_async_remote_copy(
            src_ref=held.at[peer],
            dst_ref=inbox.at[slot_at],
            send_sem=send_sem.at[peer],
            recv_sem=recv_sem.at[slot_at],
            device_id=place(peer),
            device_id_type=pl.DeviceIdType.MESH,
        )

    def send(first):
        for i in range(chunk):
            peer = first + i

            @pl.when(peer != me)
            def _():
                copy_to(peer, me).start()

    if groups == 4:
        order = [3 - ours, (ours + 2) % 4, ours + 1 - 2 * (ours % 2), ours]
    else:
        order = [(ours + groups // 2 + k) % groups for k in range(groups)]
    per = group // chunk
    steps = [(q, c) for q in order for c in range(per)]
    first_of = [q * group + c * chunk for q, c in steps]
    build(first_of[0])
    pl.semaphore_wait(barrier, devices - 1)
    send(first_of[0])
    for first in first_of[1:]:
        build(first)
        send(first)
    inbox[me] = held[me]

    loads[5].wait()

    def turn(p, _):
        turned[:, pl.ds(pl.multiple_of((p + 2) * tile_lon, tile_lon), tile_lon)] = feat_ref[p].T
        return 0

    lax.fori_loop(0, tile_lat, turn, 0)
    loads[6].wait()
    for a in range(3):
        for b in range(3):
            tap = weight_ref[a, b].T
            for r in range(2):
                at = ((r + 2 - a) * 3 + b) * channels
                mixer[at : at + channels, r * channels : (r + 1) * channels] = tap

    line_lat = lax.broadcasted_iota(jnp.int32, (lat_taps.shape[0], span), 0).astype(f32)
    line_lon = lax.broadcasted_iota(jnp.int32, (lon_taps.shape[0], span), 0).astype(f32)
    lanes = lax.broadcasted_iota(jnp.int32, (8, 128), 1) // capacity
    wide = sums.shape[1]
    deep = lon_taps.shape[0]
    stride = 8

    def taps_of(line, base, frac):
        tap = line - base
        d = tap - (frac + before)
        weight = jnp.exp(-(d * d) * inv)
        return jnp.where((tap >= 0.0) & (tap <= taps - 1.0), weight, 0.0)

    def collect(q):
        for i in range(group):
            peer = q * group + i

            @pl.when(peer != me)
            def _():
                copy_to(peer, peer).wait_recv()

        first = q * group
        infos = []
        for v in range(span // 128):
            at = first + v * fold
            info = inbox[at, capacity : capacity + geom_rows, :].astype(f32)
            for t in range(1, fold):
                info = jnp.where(
                    lanes == t, inbox[at + t, capacity : capacity + geom_rows, :].astype(f32), info
                )
            infos.append(info)
        info = jnp.concatenate(infos, axis=1)
        lat_frac, lon_frac, row_at, col_at = (info[k : k + 1] for k in range(4))
        right = jnp.where(col_at >= half, 1.0, 0.0)
        lat_taps[...] = taps_of(line_lat, row_at, lat_frac).astype(bf16).astype(f32)
        lon_taps[...] = taps_of(line_lon, col_at - right * half, lon_frac).astype(bf16)
        for v in range(span // 128):
            side = jnp.broadcast_to(right[:, v * 128 : (v + 1) * 128], (128, 128)).T.astype(bf16)
            rows = jnp.concatenate(
                [inbox[first + v * fold + t, 0:capacity, :] for t in range(fold)], axis=0
            )
            at = slice(v * 128, (v + 1) * 128)
            on_right = rows * side
            halves[at, 0:channels] = rows - on_right
            halves[at, channels : 2 * channels] = on_right

        def add(k, _):
            lhs = []
            for j in range(stride):
                row = jnp.broadcast_to(lat_taps[pl.ds(k * stride + j, 1), :], (16, span)).astype(bf16)
                for t in range(deep // 16):
                    lhs.append(row * lon_taps[t * 16 : (t + 1) * 16, :])
            out = jnp.dot(jnp.concatenate(lhs, axis=0), halves[...], preferred_element_type=f32)
            for j in range(stride):
                sums[k * stride + j] += out[j * deep : j * deep + wide]
            return 0

        lax.fori_loop(0, sums.shape[0] // stride, add, 0)

    for q in order[::-1]:
        collect(q)

    tall = canvas.shape[0]

    def join(i, _):
        canvas[i, 0:half, :] = sums[i, 0:half, 0:channels]
        canvas[i, half:wide, :] = (
            sums[i, half:wide, 0:channels] + sums[i, 0 : wide - half, channels : 2 * channels]
        )
        canvas[i, wide : wide + half, :] = sums[i, wide - half : wide, channels : 2 * channels]
        return 0

    lax.fori_loop(0, tall, join, 0)
    up, down = before + 1, after + 1
    inset = before - 1
    spans = ((0, up), (inset, cols), (inset + cols - 2, down))
    for count, first, refs in (
        (up, 0, (strips[4], strips[0], strips[5])),
        (down, inset + rows - 2, (strips[6], strips[1], strips[7])),
    ):
        for i in range(count):
            for (start, width), ref in zip(spans, refs):
                ref[i] = canvas[first + i, start : start + width, :].astype(bf16)

    def emit(i, _):
        strips[2][i] = canvas[i + inset, 0:up, :].astype(bf16)
        strips[3][i] = canvas[i + inset, inset + cols - 2 : inset + cols - 2 + down, :].astype(bf16)
        return 0

    lax.fori_loop(0, rows, emit, 0)

    ways = ((-1, 0), (1, 0), (0, -1), (0, 1), (-1, -1), (-1, 1), (1, -1), (1, 1))
    chips = devices // 2
    at = lat * lon_total + lon
    core, chip = at % 2, at // 2
    other = 1 - core

    def seat(peer):
        return (peer // lon_total, peer % lon_total)

    halos = []
    for w, (da, db) in enumerate(ways):
        copy = pltpu.make_async_remote_copy(
            src_ref=strips[w],
            dst_ref=landed[w],
            send_sem=halo_send.at[w],
            recv_sem=halo_recv.at[w],
            device_id=((lat + da + lat_total) % lat_total, (lon + db + lon_total) % lon_total),
            device_id_type=pl.DeviceIdType.MESH,
        )
        sends = (lat + da >= 0) & (lat + da < lat_total)
        takes = (lat - da >= 0) & (lat - da < lat_total)
        halos.append((copy, sends, takes))

    def when(da, cond, fn):
        if da == 0:
            fn()
        else:
            pl.when(cond)(fn)

    for (copy, sends, _), (da, _) in zip(halos, ways):
        when(da, sends, copy.start)

    for (copy, _, takes), (da, db), ref in zip(halos, ways, landed):

        def take(copy=copy, da=da, db=db, ref=ref):
            copy.wait_recv()
            high = {-1: rows - up, 0: 0, 1: 0}[da]
            count = {-1: up, 0: rows, 1: down}[da]
            left = {-1: cols - up, 0: 0, 1: 0}[db]
            width = {-1: up, 0: cols, 1: down}[db]

            def add(i, _):
                canvas[inset + high + i, inset + left : inset + left + width, :] += ref[i].astype(f32)
                return 0

            lax.fori_loop(0, count, add, 0)

        when(da, takes, take)

    @pl.when(lat == 0)
    def _():
        canvas[inset] = jnp.zeros(canvas.shape[1:], f32)

    @pl.when(lat == lat_total - 1)
    def _():
        canvas[inset + rows - 1] = jnp.zeros(canvas.shape[1:], f32)

    def shift(i, _):
        at = pl.ds(pl.multiple_of(i * tile_lon, tile_lon), tile_lon)
        for b in range(3):
            windows[at, b * channels : (b + 1) * channels] = canvas[
                i + inset, inset + 2 - b : inset + 2 - b + tile_lon, :
            ].astype(bf16)
        return 0

    lax.fori_loop(0, rows, shift, 0)
    step = next(n for n in (11, 6, 3, 2, 1) if rows % n == 0)
    depth = step * tile_lon

    def weigh(k, _):
        start = k * depth
        lhs = jnp.concatenate(
            [
                turned[:, pl.ds(pl.multiple_of(start + a * tile_lon, tile_lon), depth)]
                for a in range(3)
            ],
            axis=0,
        )
        rhs = windows[pl.ds(pl.multiple_of(start, tile_lon), depth), :]
        total[...] += jnp.dot(lhs, rhs, preferred_element_type=f32)
        return 0

    lax.fori_loop(0, rows // step, weigh, 0)
    for a in range(3):
        for b in range(3):
            at = (a * 3 + b) * channels
            flat[at : at + channels, :] = total[
                a * channels : (a + 1) * channels, b * channels : (b + 1) * channels
            ]
    share = pieces.shape[1]

    def cut(d, _):
        pieces[d] = flat[pl.ds(d * share, share), :].astype(bf16)
        return 0

    lax.fori_loop(0, devices, cut, 0)
    part = math.gcd(tile_lat // 2, 8)
    strides = tile_lat // 2 // part
    first, second = strides // 4, strides * 3 // 4

    def apply(k, _):
        lhs = jnp.concatenate(
            [
                jnp.concatenate(
                    [
                        windows[
                            pl.ds(
                                pl.multiple_of((2 * (k * part + j) + r) * tile_lon, tile_lon),
                                tile_lon,
                            ),
                            :,
                        ]
                        for r in range(4)
                    ],
                    axis=1,
                )
                for j in range(part)
            ],
            axis=0,
        )
        acc = jnp.dot(lhs, mixer[...], preferred_element_type=f32).astype(bf16)
        for j in range(part):
            for r in range(2):
                ig_ref[2 * (k * part + j) + r] = acc[
                    j * tile_lon : (j + 1) * tile_lon, r * channels : (r + 1) * channels
                ]
        return 0

    def paired(src, dst, n):
        return pltpu.make_async_remote_copy(
            src_ref=src,
            dst_ref=dst,
            send_sem=pair_send.at[n],
            recv_sem=pair_recv.at[n],
            device_id=seat(chip * 2 + other),
            device_id_type=pl.DeviceIdType.MESH,
        )

    def scattered(peer, slot):
        return pltpu.make_async_remote_copy(
            src_ref=pieces.at[core * chips + peer],
            dst_ref=parts.at[slot],
            send_sem=part_send.at[peer],
            recv_sem=part_recv.at[slot],
            device_id=seat(peer * 2 + core),
            device_id_type=pl.DeviceIdType.MESH,
        )

    def shared(peer, slot):
        return pltpu.make_async_remote_copy(
            src_ref=mine,
            dst_ref=gathered.at[core * chips + slot],
            send_sem=all_send.at[peer],
            recv_sem=all_recv.at[slot],
            device_id=seat(peer * 2 + core),
            device_id_type=pl.DeviceIdType.MESH,
        )

    def each_chip(fn):
        def body(k, _):
            fn((chip + k) % chips)
            return 0

        lax.fori_loop(1, chips, body, 0)

    swap = paired(pieces.at[pl.ds(other * chips, chips)], twin, 0)
    swap.start()
    lax.fori_loop(0, first, apply, 0)
    swap.wait_recv()

    def merge(p, _):
        at = core * chips + p
        pieces[at] = (flat[pl.ds(at * share, share), :] + twin[p].astype(f32)).astype(bf16)
        return 0

    lax.fori_loop(0, chips, merge, 0)
    each_chip(lambda peer: scattered(peer, chip).start())
    lax.fori_loop(first, second, apply, 0)
    parts[chip] = pieces[core * chips + chip]
    each_chip(lambda peer: scattered(peer, peer).wait_recv())

    def gather_sum(p, acc):
        return acc + parts[p].astype(f32)

    mine[...] = lax.fori_loop(
        0, chips, gather_sum, jnp.zeros((share, channels), f32)
    ).astype(bf16)
    each_chip(lambda peer: shared(peer, chip).start())
    gathered[core * chips + chip] = mine[...]
    lax.fori_loop(second, strides, apply, 0)
    each_chip(lambda peer: shared(peer, peer).wait_recv())
    kept = gathered.at[pl.ds(core * chips, chips)]
    back = paired(kept, kept, 1)
    back.start()

    def spill(d, _):
        wg_ref[pl.ds(d * share, share), :] = gathered[d].astype(f32)
        return 0

    lax.fori_loop(core * chips, (core + 1) * chips, spill, 0)
    back.wait_recv()
    lax.fori_loop(other * chips, (other + 1) * chips, spill, 0)
    for (copy, sends, _), (da, _) in zip(halos, ways):
        when(da, sends, copy.wait_send)
    swap.wait_send()
    back.wait_send()
    each_chip(lambda peer: scattered(peer, chip).wait_send())
    each_chip(lambda peer: shared(peer, chip).wait_send())

    def each(fn):
        def body(k, _):
            fn((me + k) % devices)
            return 0

        lax.fori_loop(1, devices, body, 0)

    each(lambda peer: copy_to(peer, me).wait_send())


def shards(grad_rows, owner, lat_offset, lon_offset, position, live_count, features, conv_weight):
    lat_total = lax.axis_size("lat")
    lon_total = lax.axis_size("lon")
    device_total = lat_total * lon_total
    row_total, channels = grad_rows.shape
    tile_lat, tile_lon = features.shape[:2]
    capacity = max(2, 2 * row_total // device_total)
    smem = pl.BlockSpec(memory_space=pltpu.SMEM)
    vmem = pl.BlockSpec(memory_space=pltpu.VMEM)

    rows, cols = tile_lat + 2, tile_lon + 2
    tall = -(-(tile_lat + taps - 1) // 8) * 8
    wide = tile_lon // 2 + 8
    span = math.gcd(device_total, max(1, 512 // capacity)) * capacity
    up, down = before + 1, after + 1
    strip_shapes = [
        (up, cols),
        (down, cols),
        (rows, up),
        (rows, down),
        (up, up),
        (up, down),
        (down, up),
        (down, down),
    ]
    message = (device_total, capacity + geom_rows, channels)
    flat_rows = 9 * channels
    share = flat_rows // device_total
    ring = pltpu.VMEM((device_total, share, channels), bf16)
    half_ring = pltpu.VMEM((device_total // 2, share, channels), bf16)
    dma = pltpu.SemaphoreType.DMA
    places = [pltpu.VMEM(shape + (channels,), bf16) for shape in strip_shapes]
    operands = (
        grad_rows,
        owner.reshape(1, row_total),
        lat_offset.reshape(1, row_total),
        lon_offset.reshape(1, row_total),
        position.T,
        features,
        conv_weight,
    )
    input_grad, weight_grad = pl.pallas_call(
        functools.partial(solve_kernel, capacity, lat_total, lon_total),
        out_shape=[
            jax.ShapeDtypeStruct((tile_lat, tile_lon, channels), bf16),
            jax.ShapeDtypeStruct((flat_rows, channels), f32),
        ],
        in_specs=[smem] + [pl.BlockSpec(memory_space=pltpu.HBM)] * 7,
        out_specs=[vmem] * 2,
        scratch_shapes=[pltpu.VMEM(x.shape, x.dtype) for x in operands]
        + [
            pltpu.VMEM(message, bf16),
            pltpu.VMEM(message, bf16),
            pltpu.VMEM((tall, wide, 2 * channels), f32),
            pltpu.VMEM((tall, wide + tile_lon // 2, channels), f32),
            pltpu.VMEM((tall, span), f32),
            pltpu.VMEM((-(-wide // 16) * 16, span), bf16),
            pltpu.VMEM((span, 2 * channels), bf16),
        ]
        + places
        + places
        + [
            pltpu.VMEM((rows * tile_lon, 3 * channels), bf16),
            pltpu.VMEM((channels, (rows + 2) * tile_lon), bf16),
            pltpu.VMEM((3 * channels, 3 * channels), f32),
            pltpu.VMEM((flat_rows, channels), f32),
            pltpu.VMEM((4 * 3 * channels, 2 * channels), bf16),
            ring,
            half_ring,
            half_ring,
            pltpu.VMEM((share, channels), bf16),
            ring,
            dma((7,)),
            dma((device_total,)),
            dma((device_total,)),
            dma((8,)),
            dma((8,)),
            dma((2,)),
            dma((2,)),
            dma((device_total // 2,)),
            dma((device_total // 2,)),
            dma((device_total // 2,)),
            dma((device_total // 2,)),
        ],
        compiler_params=pltpu.CompilerParams(
            vmem_limit_bytes=44 * 2**20, collective_id=0, has_side_effects=True
        ),
        name="solve",
    )(live_count, *[pltpu.with_memory_space_constraint(x, pltpu.HBM) for x in operands])
    return input_grad, weight_grad.reshape(3, 3, channels, channels)


def solution(mesh):
    placed = (
        P(("lat", "lon"), None),
        P(("lat", "lon"), None),
        P(("lat", "lon")),
        P(("lat", "lon")),
        P(("lat", "lon"), None),
        P(("lat", "lon")),
        P("lat", "lon", None),
        P(),
    )
    return jax.shard_map(
        shards, mesh=mesh, in_specs=placed, out_specs=(P("lat", "lon", None), P()), check_vma=False
    )
```

```python
import functools
import math

import jax
import jax.numpy as jnp
from jax import lax
from jax.experimental import pallas as pl
from jax.experimental.pallas import tpu as pltpu
from jax.sharding import PartitionSpec as P

rbf_scale = 1.5
taps = 8
before = 3
after = taps - 1 - before
geom_rows = 8
f32 = jnp.float32
bf16 = jnp.bfloat16


def solve_kernel(
    capacity,
    lat_total,
    lon_total,
    live_ref,
    rows_hbm,
    owner_hbm,
    lat_hbm,
    lon_hbm,
    pos_hbm,
    feat_hbm,
    weight_hbm,
    ig_ref,
    wg_ref,
    *refs,
):
    (rows_ref, owner_ref, lat_ref, lon_ref, pos_ref, weight_ref) = refs[:6]
    (field, beside_left, beside_right, beside, edges) = refs[6:11]
    (held, inbox, sums, canvas, lat_taps, lon_taps, halves) = refs[11:18]
    strips, landed = refs[18:26], refs[26:34]
    (windows, turned, total, flat, mixer, pieces, twin, parts, mine, gathered) = refs[34:44]
    (load_sem, send_sem, recv_sem, field_send, field_recv) = refs[44:49]
    halo_send, halo_recv, pair_send, pair_recv, part_send, part_recv, all_send, all_recv = refs[49:]
    devices = inbox.shape[0]
    row_total, channels = rows_ref.shape
    tile_lat, tile_lon = ig_ref.shape[:2]
    up, down = before + 1, after + 1
    tall = canvas.shape[0]
    own_field = field.at[up : up + tile_lat]
    lat, lon = lax.axis_index("lat"), lax.axis_index("lon")
    me = lon * lat_total + lat
    span = halves.shape[0]
    group = span // capacity
    groups = devices // group
    ours = me // group
    half = tile_lon // 2
    inv = 1.0 / (2.0 * rbf_scale * rbf_scale)

    def place(peer):
        return (peer % lat_total, peer // lat_total)

    barrier = pltpu.get_barrier_semaphore()

    def greet(k, _):
        pl.semaphore_signal(
            barrier, inc=1, device_id=place((me + k) % devices), device_id_type=pl.DeviceIdType.MESH
        )
        return 0

    loads = [
        pltpu.make_async_copy(src, dst, load_sem.at[k])
        for k, (src, dst) in enumerate(
            zip(
                (rows_hbm, owner_hbm, lat_hbm, lon_hbm, pos_hbm, feat_hbm, weight_hbm),
                (rows_ref, owner_ref, lat_ref, lon_ref, pos_ref, own_field, weight_ref),
            )
        )
    ]
    for load in loads:
        load.start()
    lax.fori_loop(1, devices, greet, 0)
    sums[...] = jnp.zeros_like(sums)
    mixer[...] = jnp.zeros_like(mixer)
    total[...] = jnp.zeros_like(total)
    rows, cols = tile_lat + 2, tile_lon + 2
    field[tall + 1] = jnp.zeros(field.shape[1:], bf16)
    for ref in (beside_left, beside_right):
        ref[tall + 1] = jnp.zeros(ref.shape[1:], bf16)

    @pl.when(lat == 0)
    def _():
        for ref in (field, beside_left, beside_right):
            ref[0:up] = jnp.zeros((up,) + ref.shape[1:], bf16)

    @pl.when(lat == lat_total - 1)
    def _():
        for ref in (field, beside_left, beside_right):
            ref[up + tile_lat : tall + 1] = jnp.zeros((down,) + ref.shape[1:], bf16)

    for load in loads[:5]:
        load.wait()

    live = lax.broadcasted_iota(jnp.int32, (1, row_total), 1) < live_ref[0]
    tile = owner_ref[...].astype(f32)
    tile_row = jnp.floor((tile + 0.5) * (1.0 / lon_total))
    owner = (tile - tile_row * lon_total) * lat_total + tile_row
    owner = jnp.where(live, owner, float(devices)).astype(jnp.int32)
    match = lax.broadcasted_iota(jnp.int32, (devices, row_total), 0) == owner
    match = jnp.where(match, 1.0, 0.0)
    blocks = row_total // 128
    upper = lax.broadcasted_iota(jnp.int32, (128, 128), 0) < lax.broadcasted_iota(
        jnp.int32, (128, 128), 1
    )
    upper = jnp.where(upper, 1.0, 0.0).astype(bf16)
    columns = [match[:, k * 128 : (k + 1) * 128] for k in range(blocks)]
    earlier = jnp.dot(
        jnp.concatenate(columns, axis=0).astype(bf16), upper, preferred_element_type=f32
    )
    before_block = jnp.zeros((devices, 1), f32)
    ranks = []
    for k, part in enumerate(columns):
        ahead = earlier[k * devices : (k + 1) * devices] + before_block
        ranks.append(jnp.sum(ahead * part, axis=0, keepdims=True))
        before_block = before_block + jnp.sum(part, axis=1, keepdims=True)
    rank = jnp.concatenate(ranks, axis=1).astype(jnp.int32)
    slot = owner * capacity + rank
    geometry = jnp.concatenate(
        [
            pos_ref[...].astype(f32),
            lat_ref[...].astype(f32),
            lon_ref[...].astype(f32),
            jnp.zeros((geom_rows - 4, row_total), f32),
        ],
        axis=0,
    ).astype(bf16)
    fold = 128 // capacity
    chunk = math.gcd(group, max(1, 256 // capacity))
    line = lax.broadcasted_iota(jnp.int32, (chunk * capacity, row_total), 0)
    lane_block = lax.broadcasted_iota(jnp.int32, (geom_rows, 128), 1) // capacity

    def build(first):
        hit = jnp.where(line == slot - first * capacity, 1.0, 0.0).astype(bf16)
        placed = jnp.dot(hit, rows_ref[...], preferred_element_type=f32).astype(bf16)
        info = lax.dot_general(
            geometry, hit, (((1,), (1,)), ((), ())), preferred_element_type=f32
        )
        for i in range(chunk):
            held[first + i, 0:capacity, :] = placed[i * capacity : (i + 1) * capacity]
        for v in range(chunk // fold):
            piece = info[:, v * 128 : (v + 1) * 128]
            rolled = [piece] + [pltpu.roll(piece, s * capacity, 1) for s in range(1, fold)]
            for i in range(fold):
                tiled = rolled[(fold - i) % fold]
                for t in range(1, fold):
                    tiled = jnp.where(lane_block == t, rolled[(t - i) % fold], tiled)
                held[first + v * fold + i, capacity : capacity + geom_rows, :] = tiled.astype(bf16)

    def copy_to(peer, slot_at):
        return pltpu.make_async_remote_copy(
            src_ref=held.at[peer],
            dst_ref=inbox.at[slot_at],
            send_sem=send_sem.at[peer],
            recv_sem=recv_sem.at[slot_at],
            device_id=place(peer),
            device_id_type=pl.DeviceIdType.MESH,
        )

    def send(first):
        for i in range(chunk):
            peer = first + i

            @pl.when(peer != me)
            def _():
                copy_to(peer, me).start()

    if groups == 4:
        order = [3 - ours, (ours + 2) % 4, ours + 1 - 2 * (ours % 2), ours]
    else:
        order = [(ours + groups // 2 + k) % groups for k in range(groups)]
    per = group // chunk
    steps = [(q, c) for q in order for c in range(per)]
    first_of = [q * group + c * chunk for q, c in steps]
    build(first_of[0])
    pl.semaphore_wait(barrier, devices - 1)
    send(first_of[0])
    for first in first_of[1:]:
        build(first)
        send(first)
    inbox[me] = held[me]

    loads[5].wait()

    def when(da, cond, fn):
        if da == 0:
            fn()
        else:
            pl.when(cond)(fn)

    ways = ((-1, 0), (1, 0), (0, -1), (0, 1), (-1, -1), (-1, 1), (1, -1), (1, 1))
    reach = beside_left.shape[1]
    source_rows = {-1: slice(up, up + down), 0: slice(up, up + tile_lat), 1: slice(tile_lat, up + tile_lat)}
    target_rows = {-1: slice(up + tile_lat, tall + 1), 0: source_rows[0], 1: slice(0, up)}
    source_cols = {-1: slice(0, reach), 0: slice(0, tile_lon), 1: slice(tile_lon - reach, tile_lon)}
    target_of = {-1: beside_right, 0: field, 1: beside_left}
    borders = []
    for w, (da, db) in enumerate(ways):
        copy = pltpu.make_async_remote_copy(
            src_ref=field.at[source_rows[da], source_cols[db]],
            dst_ref=target_of[db].at[target_rows[da]],
            send_sem=field_send.at[w],
            recv_sem=field_recv.at[w],
            device_id=((lat + da + lat_total) % lat_total, (lon + db + lon_total) % lon_total),
            device_id_type=pl.DeviceIdType.MESH,
        )
        sends = (lat + da >= 0) & (lat + da < lat_total)
        takes = (lat - da >= 0) & (lat - da < lat_total)
        borders.append((copy, sends, takes))
    for (copy, sends, _), (da, _) in zip(borders, ways):
        when(da, sends, copy.start)

    def turn(p):
        at = p * tile_lon
        if not isinstance(p, int):
            at = pl.multiple_of(at, tile_lon)
        turned[:, pl.ds(at, tile_lon)] = field[p].T

    fast = math.gcd(tile_lat, 8)

    def turn_some(k, _):
        for j in range(fast):
            turn(up + k * fast + j)
        return 0

    lax.fori_loop(0, tile_lat // fast, turn_some, 0)
    loads[6].wait()
    for a in range(3):
        for b in range(3):
            tap = weight_ref[a, b].T
            for r in range(2):
                at = ((r + 2 - a) * 3 + b) * channels
                mixer[at : at + channels, r * channels : (r + 1) * channels] = tap

    line_lat = lax.broadcasted_iota(jnp.int32, (lat_taps.shape[0], span), 0).astype(f32)
    line_lon = lax.broadcasted_iota(jnp.int32, (lon_taps.shape[0], span), 0).astype(f32)
    lanes = lax.broadcasted_iota(jnp.int32, (8, 128), 1) // capacity
    wide = sums.shape[1]
    line_lon = jnp.where(line_lon >= wide, line_lon - wide, line_lon)
    stride = next(n for n in (24, 12, 8, 4, 2) if tall % n == 0)

    def taps_of(line, base, frac):
        tap = line - base
        d = tap - (frac + before)
        weight = jnp.exp(-(d * d) * inv)
        return jnp.where((tap >= 0.0) & (tap <= taps - 1.0), weight, 0.0)

    def collect(q):
        for i in range(group):
            peer = q * group + i

            @pl.when(peer != me)
            def _():
                copy_to(peer, peer).wait_recv()

        first = q * group
        infos = []
        for v in range(span // 128):
            at = first + v * fold
            info = inbox[at, capacity : capacity + geom_rows, :].astype(f32)
            for t in range(1, fold):
                info = jnp.where(
                    lanes == t, inbox[at + t, capacity : capacity + geom_rows, :].astype(f32), info
                )
            infos.append(info)
        info = jnp.concatenate(infos, axis=1)
        lat_frac, lon_frac, row_at, col_at = (info[k : k + 1] for k in range(4))
        right = jnp.where(col_at >= half, 1.0, 0.0)
        lat_taps[...] = taps_of(line_lat, row_at, lat_frac).astype(bf16).astype(f32)
        lon_taps[...] = taps_of(line_lon, col_at - right * half, lon_frac).astype(bf16)
        for v in range(span // 128):
            side = jnp.broadcast_to(right[:, v * 128 : (v + 1) * 128], (128, 128)).T.astype(bf16)
            rows = jnp.concatenate(
                [inbox[first + v * fold + t, 0:capacity, :] for t in range(fold)], axis=0
            )
            at = slice(v * 128, (v + 1) * 128)
            on_right = rows * side
            halves[at, 0:channels] = rows - on_right
            halves[at, channels : 2 * channels] = on_right

        def add(k, _):
            lhs = []
            for j in range(0, stride, 2):
                pair = [
                    jnp.broadcast_to(lat_taps[pl.ds(k * stride + j + n, 1), :], (8, span))
                    for n in range(2)
                ]
                for t in range(0, 2 * wide, 16):
                    row = jnp.concatenate([pair[t // wide], pair[(t + 8) // wide]], axis=0)
                    lhs.append(row.astype(bf16) * lon_taps[t : t + 16, :])
            out = jnp.dot(jnp.concatenate(lhs, axis=0), halves[...], preferred_element_type=f32)
            for j in range(stride):
                sums[k * stride + j] += out[j * wide : (j + 1) * wide]
            return 0

        lax.fori_loop(0, tall // stride, add, 0)

    def border():
        for (copy, _, takes), (da, _) in zip(borders, ways):
            when(da, takes, copy.wait_recv)
        for p in (*range(up), *range(up + tile_lat, tall + 2)):
            turn(p)
        slots = 2 * reach
        some = 128 // slots
        for a in range(3):
            for k in range(tall // some):
                at = slice(a + k * some, a + (k + 1) * some)
                both = jnp.concatenate([beside_left[at], beside_right[at]], axis=1)
                beside[a * channels : (a + 1) * channels, k * 128 : (k + 1) * 128] = both.reshape(
                    128, channels
                ).T

    for k, q in enumerate(order[::-1]):
        if k == groups - 1:
            border()
        collect(q)

    pad = reach

    def join(i, _):
        canvas[i, 0:pad, :] = jnp.zeros((pad, channels), f32)
        canvas[i, pad : pad + half, :] = sums[i, 0:half, 0:channels]
        canvas[i, pad + half : pad + wide, :] = (
            sums[i, half:wide, 0:channels] + sums[i, 0 : wide - half, channels : 2 * channels]
        )
        canvas[i, pad + wide : pad + wide + half, :] = sums[i, wide - half : wide, channels : 2 * channels]
        canvas[i, pad + wide + half : 2 * pad + wide + half, :] = jnp.zeros((pad, channels), f32)
        return 0

    lax.fori_loop(0, tall, join, 0)
    inset = before - 1
    edge = pad + inset
    spans = ((pad, up), (edge, cols), (edge + cols - 2, down))
    for count, first, refs in (
        (up, 0, (strips[4], strips[0], strips[5])),
        (down, inset + rows - 2, (strips[6], strips[1], strips[7])),
    ):
        for i in range(count):
            for (start, width), ref in zip(spans, refs):
                ref[i] = canvas[first + i, start : start + width, :].astype(bf16)

    def emit(i, _):
        strips[2][i] = canvas[i + inset, pad : pad + up, :].astype(bf16)
        strips[3][i] = canvas[i + inset, edge + cols - 2 : edge + cols - 2 + down, :].astype(bf16)
        return 0

    lax.fori_loop(0, rows, emit, 0)

    chips = devices // 2
    at = lat * lon_total + lon
    core, chip = at % 2, at // 2
    other = 1 - core

    def seat(peer):
        return (peer // lon_total, peer % lon_total)

    halos = []
    for w, (da, db) in enumerate(ways):
        copy = pltpu.make_async_remote_copy(
            src_ref=strips[w],
            dst_ref=landed[w],
            send_sem=halo_send.at[w],
            recv_sem=halo_recv.at[w],
            device_id=((lat + da + lat_total) % lat_total, (lon + db + lon_total) % lon_total),
            device_id_type=pl.DeviceIdType.MESH,
        )
        sends = (lat + da >= 0) & (lat + da < lat_total)
        takes = (lat - da >= 0) & (lat - da < lat_total)
        halos.append((copy, sends, takes))

    for (copy, sends, _), (da, _) in zip(halos, ways):
        when(da, sends, copy.start)

    @pl.when(lat == 0)
    def _():
        canvas[0:before] = jnp.zeros((before,) + canvas.shape[1:], f32)

    @pl.when(lat == lat_total - 1)
    def _():
        canvas[before + tile_lat : tall] = jnp.zeros((tall - before - tile_lat,) + canvas.shape[1:], f32)

    def shift(i, _):
        at = pl.ds(pl.multiple_of(i * tile_lon, tile_lon), tile_lon)
        for b in range(3):
            windows[at, b * channels : (b + 1) * channels] = canvas[
                i, edge + 2 - b : edge + 2 - b + tile_lon, :
            ].astype(bf16)
        return 0

    lax.fori_loop(0, tall, shift, 0)

    def shift_edges(i, _):
        at = pl.ds(pl.multiple_of(i * 2 * reach, 2 * reach), 2 * reach)
        for b in range(3):
            first = edge + 2 - b - reach
            second = edge + 2 - b + tile_lon
            both = [canvas[i, first : first + reach, :], canvas[i, second : second + reach, :]]
            edges[at, b * channels : (b + 1) * channels] = jnp.concatenate(both, axis=0).astype(bf16)
        return 0

    lax.fori_loop(0, tall, shift_edges, 0)
    step = next(n for n in (12, 8, 6, 4, 3, 2, 1) if tall % n == 0)
    depth = step * tile_lon

    def weigh(k, _):
        start = k * depth
        lhs = jnp.concatenate(
            [
                turned[:, pl.ds(pl.multiple_of(start + a * tile_lon, tile_lon), depth)]
                for a in range(3)
            ],
            axis=0,
        )
        rhs = windows[pl.ds(pl.multiple_of(start, tile_lon), depth), :]
        total[...] += jnp.dot(lhs, rhs, preferred_element_type=f32)
        return 0

    lax.fori_loop(0, tall // step, weigh, 0)
    total[...] += jnp.dot(beside[...], edges[...], preferred_element_type=f32)
    for a in range(3):
        for b in range(3):
            at = (a * 3 + b) * channels
            flat[at : at + channels, :] = total[
                a * channels : (a + 1) * channels, b * channels : (b + 1) * channels
            ]
    share = pieces.shape[1]

    def cut(d, _):
        pieces[d] = flat[pl.ds(d * share, share), :].astype(bf16)
        return 0

    lax.fori_loop(0, devices, cut, 0)
    part = math.gcd(tile_lat // 2, 8)
    strides = tile_lat // 2 // part
    first = strides // 2

    def apply(k, _):
        lhs = jnp.concatenate(
            [
                jnp.concatenate(
                    [
                        windows[
                            pl.ds(
                                pl.multiple_of(
                                    (inset + 2 * (k * part + j) + r) * tile_lon, tile_lon
                                ),
                                tile_lon,
                            ),
                            :,
                        ]
                        for r in range(4)
                    ],
                    axis=1,
                )
                for j in range(part)
            ],
            axis=0,
        )
        acc = jnp.dot(lhs, mixer[...], preferred_element_type=f32).astype(bf16)
        for j in range(part):
            for r in range(2):
                ig_ref[2 * (k * part + j) + r] = acc[
                    j * tile_lon : (j + 1) * tile_lon, r * channels : (r + 1) * channels
                ]
        return 0

    def settle():
        for (copy, _, takes), (da, db), ref in zip(halos, ways, landed):

            def take(copy=copy, da=da, db=db, ref=ref):
                copy.wait_recv()
                high = {-1: rows - up, 0: 0, 1: 0}[da]
                count = {-1: up, 0: rows, 1: down}[da]
                left = {-1: cols - up, 0: 0, 1: 0}[db]
                width = {-1: up, 0: cols, 1: down}[db]

                def add(i, _):
                    canvas[inset + high + i, edge + left : edge + left + width, :] += ref[i].astype(f32)
                    return 0

                lax.fori_loop(0, count, add, 0)

            when(da, takes, take)

        @pl.when(lat == 0)
        def _():
            canvas[inset] = jnp.zeros(canvas.shape[1:], f32)

        @pl.when(lat == lat_total - 1)
        def _():
            canvas[inset + rows - 1] = jnp.zeros(canvas.shape[1:], f32)
        lax.fori_loop(inset, inset + rows, shift, 0)

    def paired(src, dst, n):
        return pltpu.make_async_remote_copy(
            src_ref=src,
            dst_ref=dst,
            send_sem=pair_send.at[n],
            recv_sem=pair_recv.at[n],
            device_id=seat(chip * 2 + other),
            device_id_type=pl.DeviceIdType.MESH,
        )

    def scattered(peer, slot):
        return pltpu.make_async_remote_copy(
            src_ref=pieces.at[core * chips + peer],
            dst_ref=parts.at[slot],
            send_sem=part_send.at[peer],
            recv_sem=part_recv.at[slot],
            device_id=seat(peer * 2 + core),
            device_id_type=pl.DeviceIdType.MESH,
        )

    def shared(peer, slot):
        return pltpu.make_async_remote_copy(
            src_ref=mine,
            dst_ref=gathered.at[core * chips + slot],
            send_sem=all_send.at[peer],
            recv_sem=all_recv.at[slot],
            device_id=seat(peer * 2 + core),
            device_id_type=pl.DeviceIdType.MESH,
        )

    def each_chip(fn):
        def body(k, _):
            fn((chip + k) % chips)
            return 0

        lax.fori_loop(1, chips, body, 0)

    swap = paired(pieces.at[pl.ds(other * chips, chips)], twin, 0)
    swap.start()
    swap.wait_recv()

    def merge(p, _):
        at = core * chips + p
        pieces[at] = (flat[pl.ds(at * share, share), :] + twin[p].astype(f32)).astype(bf16)
        return 0

    lax.fori_loop(0, chips, merge, 0)
    each_chip(lambda peer: scattered(peer, chip).start())
    settle()
    lax.fori_loop(0, first, apply, 0)
    parts[chip] = pieces[core * chips + chip]
    each_chip(lambda peer: scattered(peer, peer).wait_recv())

    def gather_sum(p, acc):
        return acc + parts[p].astype(f32)

    mine[...] = lax.fori_loop(
        0, chips, gather_sum, jnp.zeros((share, channels), f32)
    ).astype(bf16)
    each_chip(lambda peer: shared(peer, chip).start())
    gathered[core * chips + chip] = mine[...]
    lax.fori_loop(first, strides, apply, 0)
    each_chip(lambda peer: shared(peer, peer).wait_recv())
    kept = gathered.at[pl.ds(core * chips, chips)]
    back = paired(kept, kept, 1)
    back.start()

    def spill(d, _):
        wg_ref[pl.ds(d * share, share), :] = gathered[d].astype(f32)
        return 0

    lax.fori_loop(core * chips, (core + 1) * chips, spill, 0)
    back.wait_recv()
    lax.fori_loop(other * chips, (other + 1) * chips, spill, 0)
    for (copy, sends, _), (da, _) in zip(halos + borders, ways + ways):
        when(da, sends, copy.wait_send)
    swap.wait_send()
    back.wait_send()
    each_chip(lambda peer: scattered(peer, chip).wait_send())
    each_chip(lambda peer: shared(peer, chip).wait_send())

    def each(fn):
        def body(k, _):
            fn((me + k) % devices)
            return 0

        lax.fori_loop(1, devices, body, 0)

    each(lambda peer: copy_to(peer, me).wait_send())


def shards(grad_rows, owner, lat_offset, lon_offset, position, live_count, features, conv_weight):
    lat_total = lax.axis_size("lat")
    lon_total = lax.axis_size("lon")
    device_total = lat_total * lon_total
    row_total, channels = grad_rows.shape
    tile_lat, tile_lon = features.shape[:2]
    capacity = max(2, 2 * row_total // device_total)
    smem = pl.BlockSpec(memory_space=pltpu.SMEM)
    vmem = pl.BlockSpec(memory_space=pltpu.VMEM)

    rows, cols = tile_lat + 2, tile_lon + 2
    tall = -(-(tile_lat + taps - 1) // 8) * 8
    wide = tile_lon // 2 + 8
    span = math.gcd(device_total, max(1, 512 // capacity)) * capacity
    up, down = before + 1, after + 1
    strip_shapes = [
        (up, cols),
        (down, cols),
        (rows, up),
        (rows, down),
        (up, up),
        (up, down),
        (down, up),
        (down, down),
    ]
    message = (device_total, capacity + geom_rows, channels)
    flat_rows = 9 * channels
    share = flat_rows // device_total
    ring = pltpu.VMEM((device_total, share, channels), bf16)
    half_ring = pltpu.VMEM((device_total // 2, share, channels), bf16)
    dma = pltpu.SemaphoreType.DMA
    places = [pltpu.VMEM(shape + (channels,), bf16) for shape in strip_shapes]
    operands = (
        grad_rows,
        owner.reshape(1, row_total),
        lat_offset.reshape(1, row_total),
        lon_offset.reshape(1, row_total),
        position.T,
        features,
        conv_weight,
    )
    input_grad, weight_grad = pl.pallas_call(
        functools.partial(solve_kernel, capacity, lat_total, lon_total),
        out_shape=[
            jax.ShapeDtypeStruct((tile_lat, tile_lon, channels), bf16),
            jax.ShapeDtypeStruct((flat_rows, channels), f32),
        ],
        in_specs=[smem] + [pl.BlockSpec(memory_space=pltpu.HBM)] * 7,
        out_specs=[vmem] * 2,
        scratch_shapes=[pltpu.VMEM(x.shape, x.dtype) for x in operands if x is not features]
        + [
            pltpu.VMEM((tall + 2, tile_lon, channels), bf16),
            pltpu.VMEM((tall + 2, 8, channels), bf16),
            pltpu.VMEM((tall + 2, 8, channels), bf16),
            pltpu.VMEM((3 * channels, tall * 16), bf16),
            pltpu.VMEM((tall * 16, 3 * channels), bf16),
            pltpu.VMEM(message, bf16),
            pltpu.VMEM(message, bf16),
            pltpu.VMEM((tall, wide, 2 * channels), f32),
            pltpu.VMEM((tall, wide + tile_lon // 2 + 16, channels), f32),
            pltpu.VMEM((tall, span), f32),
            pltpu.VMEM((2 * wide, span), bf16),
            pltpu.VMEM((span, 2 * channels), bf16),
        ]
        + places
        + places
        + [
            pltpu.VMEM((tall * tile_lon, 3 * channels), bf16),
            pltpu.VMEM((channels, (tall + 2) * tile_lon), bf16),
            pltpu.VMEM((3 * channels, 3 * channels), f32),
            pltpu.VMEM((flat_rows, channels), f32),
            pltpu.VMEM((4 * 3 * channels, 2 * channels), bf16),
            ring,
            half_ring,
            half_ring,
            pltpu.VMEM((share, channels), bf16),
            ring,
            dma((7,)),
            dma((device_total,)),
            dma((device_total,)),
            dma((8,)),
            dma((8,)),
            dma((8,)),
            dma((8,)),
            dma((2,)),
            dma((2,)),
            dma((device_total // 2,)),
            dma((device_total // 2,)),
            dma((device_total // 2,)),
            dma((device_total // 2,)),
        ],
        compiler_params=pltpu.CompilerParams(
            vmem_limit_bytes=44 * 2**20, collective_id=0, has_side_effects=True
        ),
        name="solve",
    )(live_count, *[pltpu.with_memory_space_constraint(x, pltpu.HBM) for x in operands])
    return input_grad, weight_grad.reshape(3, 3, channels, channels)


def solution(mesh):
    placed = (
        P(("lat", "lon"), None),
        P(("lat", "lon"), None),
        P(("lat", "lon")),
        P(("lat", "lon")),
        P(("lat", "lon"), None),
        P(("lat", "lon")),
        P("lat", "lon", None),
        P(),
    )
    return jax.shard_map(
        shards, mesh=mesh, in_specs=placed, out_specs=(P("lat", "lon", None), P()), check_vma=False
    )
```

```python
import functools
import math

import jax
import jax.numpy as jnp
from jax import lax
from jax.experimental import pallas as pl
from jax.experimental.pallas import tpu as pltpu
from jax.sharding import PartitionSpec as P

rbf_scale = 1.5
taps = 8
before = 3
after = taps - 1 - before
geom_rows = 8
f32 = jnp.float32
bf16 = jnp.bfloat16


def solve_kernel(
    capacity,
    lat_total,
    lon_total,
    live_ref,
    rows_hbm,
    owner_hbm,
    lat_hbm,
    lon_hbm,
    pos_hbm,
    feat_hbm,
    weight_hbm,
    ig_ref,
    wg_ref,
    *refs,
):
    (rows_ref, owner_ref, lat_ref, lon_ref, pos_ref, weight_ref) = refs[:6]
    (field, stage, beside, edges) = refs[6:10]
    (held, inbox, sums, canvas, lat_taps, lon_taps, halves) = refs[10:17]
    strips, landed = refs[17:25], refs[25:33]
    (windows, turned, total, flat, mixer, pieces, twin, parts, mine, gathered) = refs[33:43]
    (load_sem, send_sem, recv_sem, field_send, field_recv) = refs[43:48]
    halo_send, halo_recv, pair_send, pair_recv, part_send, part_recv, all_send, all_recv = refs[48:]
    devices = inbox.shape[0]
    row_total, channels = rows_ref.shape
    tile_lat, tile_lon = ig_ref.shape[:2]
    up, down = before + 1, after + 1
    tall = canvas.shape[0]
    own_field = field.at[up : up + tile_lat]
    lat, lon = lax.axis_index("lat"), lax.axis_index("lon")
    me = lon * lat_total + lat
    span = halves.shape[0]
    group = span // capacity
    groups = devices // group
    ours = me // group
    half = tile_lon // 2
    inv = 1.0 / (2.0 * rbf_scale * rbf_scale)

    def place(peer):
        return (peer % lat_total, peer // lat_total)

    barrier = pltpu.get_barrier_semaphore()

    def greet(k, _):
        pl.semaphore_signal(
            barrier, inc=1, device_id=place((me + k) % devices), device_id_type=pl.DeviceIdType.MESH
        )
        return 0

    loads = [
        pltpu.make_async_copy(src, dst, load_sem.at[k])
        for k, (src, dst) in enumerate(
            zip(
                (rows_hbm, owner_hbm, lat_hbm, lon_hbm, pos_hbm, feat_hbm, weight_hbm),
                (rows_ref, owner_ref, lat_ref, lon_ref, pos_ref, own_field, weight_ref),
            )
        )
    ]
    for load in loads:
        load.start()
    lax.fori_loop(1, devices, greet, 0)
    sums[...] = jnp.zeros_like(sums)
    mixer[...] = jnp.zeros_like(mixer)
    total[...] = jnp.zeros_like(total)
    rows, cols = tile_lat + 2, tile_lon + 2
    stage[...] = jnp.zeros_like(stage)
    field[tall + 1] = jnp.zeros(field.shape[1:], bf16)

    @pl.when(lat == 0)
    def _():
        field[0:up] = jnp.zeros((up,) + field.shape[1:], bf16)

    @pl.when(lat == lat_total - 1)
    def _():
        field[up + tile_lat : tall + 1] = jnp.zeros((down,) + field.shape[1:], bf16)

    for load in loads[:5]:
        load.wait()

    live = lax.broadcasted_iota(jnp.int32, (1, row_total), 1) < live_ref[0]
    tile = owner_ref[...].astype(f32)
    tile_row = jnp.floor((tile + 0.5) * (1.0 / lon_total))
    owner = (tile - tile_row * lon_total) * lat_total + tile_row
    owner = jnp.where(live, owner, float(devices)).astype(jnp.int32)
    match = lax.broadcasted_iota(jnp.int32, (devices, row_total), 0) == owner
    match = jnp.where(match, 1.0, 0.0)
    blocks = row_total // 128
    upper = lax.broadcasted_iota(jnp.int32, (128, 128), 0) < lax.broadcasted_iota(
        jnp.int32, (128, 128), 1
    )
    upper = jnp.where(upper, 1.0, 0.0).astype(bf16)
    columns = [match[:, k * 128 : (k + 1) * 128] for k in range(blocks)]
    earlier = jnp.dot(
        jnp.concatenate(columns, axis=0).astype(bf16), upper, preferred_element_type=f32
    )
    before_block = jnp.zeros((devices, 1), f32)
    ranks = []
    for k, part in enumerate(columns):
        ahead = earlier[k * devices : (k + 1) * devices] + before_block
        ranks.append(jnp.sum(ahead * part, axis=0, keepdims=True))
        before_block = before_block + jnp.sum(part, axis=1, keepdims=True)
    rank = jnp.concatenate(ranks, axis=1).astype(jnp.int32)
    slot = owner * capacity + rank
    geometry = jnp.concatenate(
        [
            pos_ref[...].astype(f32),
            lat_ref[...].astype(f32),
            lon_ref[...].astype(f32),
            jnp.zeros((geom_rows - 4, row_total), f32),
        ],
        axis=0,
    ).astype(bf16)
    fold = 128 // capacity
    chunk = math.gcd(group, max(1, 256 // capacity))
    line = lax.broadcasted_iota(jnp.int32, (chunk * capacity, row_total), 0)
    lane_block = lax.broadcasted_iota(jnp.int32, (geom_rows, 128), 1) // capacity

    def build(first):
        hit = jnp.where(line == slot - first * capacity, 1.0, 0.0).astype(bf16)
        placed = jnp.dot(hit, rows_ref[...], preferred_element_type=f32).astype(bf16)
        info = lax.dot_general(
            geometry, hit, (((1,), (1,)), ((), ())), preferred_element_type=f32
        )
        for i in range(chunk):
            held[first + i, 0:capacity, :] = placed[i * capacity : (i + 1) * capacity]
        for v in range(chunk // fold):
            piece = info[:, v * 128 : (v + 1) * 128]
            rolled = [piece] + [pltpu.roll(piece, s * capacity, 1) for s in range(1, fold)]
            for i in range(fold):
                tiled = rolled[(fold - i) % fold]
                for t in range(1, fold):
                    tiled = jnp.where(lane_block == t, rolled[(t - i) % fold], tiled)
                held[first + v * fold + i, capacity : capacity + geom_rows, :] = tiled.astype(bf16)

    def copy_to(peer, slot_at):
        return pltpu.make_async_remote_copy(
            src_ref=held.at[peer],
            dst_ref=inbox.at[slot_at],
            send_sem=send_sem.at[peer],
            recv_sem=recv_sem.at[slot_at],
            device_id=place(peer),
            device_id_type=pl.DeviceIdType.MESH,
        )

    def send(first):
        for i in range(chunk):
            peer = first + i

            @pl.when(peer != me)
            def _():
                copy_to(peer, me).start()

    if groups == 4:
        order = [3 - ours, (ours + 2) % 4, ours + 1 - 2 * (ours % 2), ours]
    else:
        order = [(ours + groups // 2 + k) % groups for k in range(groups)]
    per = group // chunk
    steps = [(q, c) for q in order for c in range(per)]
    first_of = [q * group + c * chunk for q, c in steps]
    early = len(first_of) // 2
    for first in first_of[:early]:
        build(first)
    pl.semaphore_wait(barrier, devices - 1)
    for first in first_of[:early]:
        send(first)
    for first in first_of[early:]:
        build(first)
        send(first)
    inbox[me] = held[me]

    loads[5].wait()

    def when(da, cond, fn):
        if da == 0:
            fn()
        else:
            pl.when(cond)(fn)

    ways = ((-1, 0), (1, 0), (0, -1), (0, 1), (-1, -1), (-1, 1), (1, -1), (1, 1))
    reach = 8
    borders = []
    for w, (da, source, target) in enumerate(
        (
            (-1, slice(up, up + down), slice(up + tile_lat, tall + 1)),
            (1, slice(tile_lat, up + tile_lat), slice(0, up)),
        )
    ):
        copy = pltpu.make_async_remote_copy(
            src_ref=field.at[source],
            dst_ref=field.at[target],
            send_sem=field_send.at[w],
            recv_sem=field_recv.at[w],
            device_id=((lat + da + lat_total) % lat_total, lon),
            device_id_type=pl.DeviceIdType.MESH,
        )
        sends = (lat + da >= 0) & (lat + da < lat_total)
        takes = (lat - da >= 0) & (lat - da < lat_total)
        borders.append((copy, sends, takes))
    for (copy, sends, _), (da, _) in zip(borders, ways):
        when(da, sends, copy.start)

    def turn(p):
        at = p * tile_lon
        if not isinstance(p, int):
            at = pl.multiple_of(at, tile_lon)
        turned[:, pl.ds(at, tile_lon)] = field[p].T

    fast = math.gcd(tile_lat, 8)

    def turn_some(k, _):
        for j in range(fast):
            turn(up + k * fast + j)
        return 0

    lax.fori_loop(0, tile_lat // fast, turn_some, 0)
    loads[6].wait()
    for a in range(3):
        for b in range(3):
            tap = weight_ref[a, b].T
            for r in range(2):
                at = ((r + 2 - a) * 3 + b) * channels
                mixer[at : at + channels, r * channels : (r + 1) * channels] = tap

    line_lat = lax.broadcasted_iota(jnp.int32, (lat_taps.shape[0], span), 0).astype(f32)
    line_lon = lax.broadcasted_iota(jnp.int32, (lon_taps.shape[0], span), 0).astype(f32)
    lanes = lax.broadcasted_iota(jnp.int32, (8, 128), 1) // capacity
    wide = sums.shape[1]
    line_lon = jnp.where(line_lon >= wide, line_lon - wide, line_lon)
    stride = next(n for n in (24, 12, 8, 4, 2) if tall % n == 0)

    def taps_of(line, base, frac):
        tap = line - base
        d = tap - (frac + before)
        weight = jnp.exp(-(d * d) * inv)
        return jnp.where((tap >= 0.0) & (tap <= taps - 1.0), weight, 0.0)

    def collect(q):
        for i in range(group):
            peer = q * group + i

            @pl.when(peer != me)
            def _():
                copy_to(peer, peer).wait_recv()

        first = q * group
        infos = []
        for v in range(span // 128):
            at = first + v * fold
            info = inbox[at, capacity : capacity + geom_rows, :].astype(f32)
            for t in range(1, fold):
                info = jnp.where(
                    lanes == t, inbox[at + t, capacity : capacity + geom_rows, :].astype(f32), info
                )
            infos.append(info)
        info = jnp.concatenate(infos, axis=1)
        lat_frac, lon_frac, row_at, col_at = (info[k : k + 1] for k in range(4))
        right = jnp.where(col_at >= half, 1.0, 0.0)
        lat_taps[...] = taps_of(line_lat, row_at, lat_frac).astype(bf16).astype(f32)
        lon_taps[...] = taps_of(line_lon, col_at - right * half, lon_frac).astype(bf16)
        for v in range(span // 128):
            side = jnp.broadcast_to(right[:, v * 128 : (v + 1) * 128], (128, 128)).T.astype(bf16)
            rows = jnp.concatenate(
                [inbox[first + v * fold + t, 0:capacity, :] for t in range(fold)], axis=0
            )
            at = slice(v * 128, (v + 1) * 128)
            on_right = rows * side
            halves[at, 0:channels] = rows - on_right
            halves[at, channels : 2 * channels] = on_right

        def add(k, _):
            lhs = []
            for j in range(0, stride, 2):
                pair = [
                    jnp.broadcast_to(lat_taps[pl.ds(k * stride + j + n, 1), :], (8, span))
                    for n in range(2)
                ]
                for t in range(0, 2 * wide, 16):
                    row = jnp.concatenate([pair[t // wide], pair[(t + 8) // wide]], axis=0)
                    lhs.append(row.astype(bf16) * lon_taps[t : t + 16, :])
            out = jnp.dot(jnp.concatenate(lhs, axis=0), halves[...], preferred_element_type=f32)
            for j in range(stride):
                sums[k * stride + j] += out[j * wide : (j + 1) * wide]
            return 0

        lax.fori_loop(0, tall // stride, add, 0)

    def border():
        for (copy, _, takes), (da, _) in zip(borders, ways):
            when(da, takes, copy.wait_recv)
        for p in (*range(up), *range(up + tile_lat, tall + 2)):
            turn(p)
        slots = 2 * reach
        some = 128 // slots
        for a in range(3):
            for k in range(tall // some):
                at = slice(a + k * some, a + (k + 1) * some)
                both = jnp.concatenate(
                    [field[at, 0:reach], field[at, tile_lon - reach : tile_lon]], axis=1
                )
                beside[a * channels : (a + 1) * channels, k * 128 : (k + 1) * 128] = both.reshape(
                    128, channels
                ).T

    for k, q in enumerate([order[3], order[2], order[0], order[1]] if groups == 4 else order[::-1]):
        if k == groups - 1:
            border()
        collect(q)

    pad = reach

    def join(i, _):
        canvas[i, 0:pad, :] = jnp.zeros((pad, channels), f32)
        canvas[i, pad : pad + half, :] = sums[i, 0:half, 0:channels]
        canvas[i, pad + half : pad + wide, :] = (
            sums[i, half:wide, 0:channels] + sums[i, 0 : wide - half, channels : 2 * channels]
        )
        canvas[i, pad + wide : pad + wide + half, :] = sums[i, wide - half : wide, channels : 2 * channels]
        canvas[i, pad + wide + half : 2 * pad + wide + half, :] = jnp.zeros((pad, channels), f32)
        return 0

    lax.fori_loop(0, tall, join, 0)
    inset = before - 1
    edge = pad + inset

    @pl.when(lat == 0)
    def _():
        canvas[0:before] = jnp.zeros((before,) + canvas.shape[1:], f32)

    @pl.when(lat == lat_total - 1)
    def _():
        canvas[before + tile_lat : tall] = jnp.zeros((tall - before - tile_lat,) + canvas.shape[1:], f32)

    some = math.gcd(tall, 4)

    def emit(k, _):
        for j in range(some):
            i = k * some + j
            strips[2][i] = canvas[i, pad : pad + up, :].astype(bf16)
            strips[3][i] = canvas[i, edge + cols - 2 : edge + cols - 2 + down, :].astype(bf16)
        return 0

    lax.fori_loop(0, tall // some, emit, 0)
    halos = []
    for w, (da, db) in enumerate(ways):
        copy = pltpu.make_async_remote_copy(
            src_ref=strips[w],
            dst_ref=landed[w],
            send_sem=halo_send.at[w],
            recv_sem=halo_recv.at[w],
            device_id=((lat + da + lat_total) % lat_total, (lon + db + lon_total) % lon_total),
            device_id_type=pl.DeviceIdType.MESH,
        )
        sends = (lat + da >= 0) & (lat + da < lat_total)
        takes = (lat - da >= 0) & (lat - da < lat_total)
        halos.append((copy, sends, takes))
    beside_halos = halos[2:4]
    for copy, _, _ in beside_halos:
        copy.start()
    spans = ((pad, up), (edge, cols), (edge + cols - 2, down))
    for count, first, refs in (
        (up, 0, (strips[4], strips[0], strips[5])),
        (down, inset + rows - 2, (strips[6], strips[1], strips[7])),
    ):
        for i in range(count):
            for (start, width), ref in zip(spans, refs):
                ref[i] = canvas[first + i, start : start + width, :].astype(bf16)
    for (copy, sends, _), (da, _) in zip(halos, ways):
        if da != 0:
            pl.when(sends)(copy.start)
    chips = devices // 2
    at = lat * lon_total + lon
    core, chip = at % 2, at // 2
    other = 1 - core

    def seat(peer):
        return (peer // lon_total, peer % lon_total)

    def shift(i, _):
        at = pl.ds(pl.multiple_of(i * tile_lon, tile_lon), tile_lon)
        for b in range(3):
            windows[at, b * channels : (b + 1) * channels] = canvas[
                i, edge + 2 - b : edge + 2 - b + tile_lon, :
            ].astype(bf16)
        return 0

    lax.fori_loop(0, tall, shift, 0)

    def shift_edges(k, _):
        for j in range(some):
            i = k * some + j
            stage[i, 0:down] = landed[3][i].astype(f32)
            stage[i, 3 * reach : 3 * reach + up] = landed[2][i].astype(f32)
            at = pl.ds(pl.multiple_of(i * 2 * reach, 2 * reach), 2 * reach)
            for b in range(3):
                first, second = 2 - b, 2 * reach + up - b
                both = [stage[i, first : first + reach, :], stage[i, second : second + reach, :]]
                edges[at, b * channels : (b + 1) * channels] = jnp.concatenate(
                    both, axis=0
                ).astype(bf16)
        return 0

    step = next(n for n in (12, 8, 6, 4, 3, 2, 1) if tall % n == 0)
    depth = step * tile_lon

    def weigh(k, _):
        start = k * depth
        lhs = jnp.concatenate(
            [
                turned[:, pl.ds(pl.multiple_of(start + a * tile_lon, tile_lon), depth)]
                for a in range(3)
            ],
            axis=0,
        )
        rhs = windows[pl.ds(pl.multiple_of(start, tile_lon), depth), :]
        total[...] += jnp.dot(lhs, rhs, preferred_element_type=f32)
        return 0

    lax.fori_loop(0, tall // step, weigh, 0)
    for copy, _, _ in beside_halos:
        copy.wait_recv()
    lax.fori_loop(0, tall // some, shift_edges, 0)
    total[...] += jnp.dot(beside[...], edges[...], preferred_element_type=f32)
    for a in range(3):
        for b in range(3):
            at = (a * 3 + b) * channels
            flat[at : at + channels, :] = total[
                a * channels : (a + 1) * channels, b * channels : (b + 1) * channels
            ]
    share = pieces.shape[1]

    def cut(d, _):
        pieces[d] = flat[pl.ds(d * share, share), :].astype(bf16)
        return 0

    lax.fori_loop(0, devices, cut, 0)
    part = math.gcd(tile_lat // 2, 8)
    strides = tile_lat // 2 // part
    first = strides // 2

    def apply(k, _):
        lhs = jnp.concatenate(
            [
                jnp.concatenate(
                    [
                        windows[
                            pl.ds(
                                pl.multiple_of(
                                    (inset + 2 * (k * part + j) + r) * tile_lon, tile_lon
                                ),
                                tile_lon,
                            ),
                            :,
                        ]
                        for r in range(4)
                    ],
                    axis=1,
                )
                for j in range(part)
            ],
            axis=0,
        )
        acc = jnp.dot(lhs, mixer[...], preferred_element_type=f32).astype(bf16)
        for j in range(part):
            for r in range(2):
                ig_ref[2 * (k * part + j) + r] = acc[
                    j * tile_lon : (j + 1) * tile_lon, r * channels : (r + 1) * channels
                ]
        return 0

    def settle():
        for (copy, _, takes), (da, db), ref in zip(halos, ways, landed):

            def take(copy=copy, da=da, db=db, ref=ref):
                if da != 0:
                    copy.wait_recv()
                high = {-1: inset + rows - up, 0: 0, 1: inset}[da]
                count = {-1: up, 0: tall, 1: down}[da]
                left = {-1: cols - up, 0: 0, 1: 0}[db]
                width = {-1: up, 0: cols, 1: down}[db]

                def add(i, _):
                    canvas[high + i, edge + left : edge + left + width, :] += ref[i].astype(f32)
                    return 0

                lax.fori_loop(0, count, add, 0)

            when(da, takes, take)

        lax.fori_loop(inset, inset + rows, shift, 0)

    def paired(src, dst, n):
        return pltpu.make_async_remote_copy(
            src_ref=src,
            dst_ref=dst,
            send_sem=pair_send.at[n],
            recv_sem=pair_recv.at[n],
            device_id=seat(chip * 2 + other),
            device_id_type=pl.DeviceIdType.MESH,
        )

    def scattered(peer, slot):
        return pltpu.make_async_remote_copy(
            src_ref=pieces.at[core * chips + peer],
            dst_ref=parts.at[slot],
            send_sem=part_send.at[peer],
            recv_sem=part_recv.at[slot],
            device_id=seat(peer * 2 + core),
            device_id_type=pl.DeviceIdType.MESH,
        )

    def shared(peer, slot):
        return pltpu.make_async_remote_copy(
            src_ref=mine,
            dst_ref=gathered.at[core * chips + slot],
            send_sem=all_send.at[peer],
            recv_sem=all_recv.at[slot],
            device_id=seat(peer * 2 + core),
            device_id_type=pl.DeviceIdType.MESH,
        )

    def each_chip(fn):
        def body(k, _):
            fn((chip + k) % chips)
            return 0

        lax.fori_loop(1, chips, body, 0)

    swap = paired(pieces.at[pl.ds(other * chips, chips)], twin, 0)
    swap.start()
    swap.wait_recv()

    def merge(p, _):
        at = core * chips + p
        pieces[at] = (flat[pl.ds(at * share, share), :] + twin[p].astype(f32)).astype(bf16)
        return 0

    lax.fori_loop(0, chips, merge, 0)
    each_chip(lambda peer: scattered(peer, chip).start())
    settle()
    lax.fori_loop(0, first, apply, 0)
    parts[chip] = pieces[core * chips + chip]
    each_chip(lambda peer: scattered(peer, peer).wait_recv())

    def gather_sum(p, acc):
        return acc + parts[p].astype(f32)

    mine[...] = lax.fori_loop(
        0, chips, gather_sum, jnp.zeros((share, channels), f32)
    ).astype(bf16)
    each_chip(lambda peer: shared(peer, chip).start())
    gathered[core * chips + chip] = mine[...]
    lax.fori_loop(first, strides, apply, 0)
    each_chip(lambda peer: shared(peer, peer).wait_recv())
    kept = gathered.at[pl.ds(core * chips, chips)]
    back = paired(kept, kept, 1)
    back.start()

    def spill(d, _):
        wg_ref[pl.ds(d * share, share), :] = gathered[d].astype(f32)
        return 0

    lax.fori_loop(core * chips, (core + 1) * chips, spill, 0)
    back.wait_recv()
    lax.fori_loop(other * chips, (other + 1) * chips, spill, 0)
    for (copy, sends, _), (da, _) in zip(halos + borders, ways + ways[:2]):
        when(da, sends, copy.wait_send)
    swap.wait_send()
    back.wait_send()
    each_chip(lambda peer: scattered(peer, chip).wait_send())
    each_chip(lambda peer: shared(peer, chip).wait_send())

    def each(fn):
        def body(k, _):
            fn((me + k) % devices)
            return 0

        lax.fori_loop(1, devices, body, 0)

    each(lambda peer: copy_to(peer, me).wait_send())


def shards(grad_rows, owner, lat_offset, lon_offset, position, live_count, features, conv_weight):
    lat_total = lax.axis_size("lat")
    lon_total = lax.axis_size("lon")
    device_total = lat_total * lon_total
    row_total, channels = grad_rows.shape
    tile_lat, tile_lon = features.shape[:2]
    capacity = max(2, 2 * row_total // device_total)
    smem = pl.BlockSpec(memory_space=pltpu.SMEM)
    vmem = pl.BlockSpec(memory_space=pltpu.VMEM)

    rows, cols = tile_lat + 2, tile_lon + 2
    tall = -(-(tile_lat + taps - 1) // 8) * 8
    wide = tile_lon // 2 + 8
    span = math.gcd(device_total, max(1, 512 // capacity)) * capacity
    up, down = before + 1, after + 1
    strip_shapes = [
        (up, cols),
        (down, cols),
        (tall, up),
        (tall, down),
        (up, up),
        (up, down),
        (down, up),
        (down, down),
    ]
    message = (device_total, capacity + geom_rows, channels)
    flat_rows = 9 * channels
    share = flat_rows // device_total
    ring = pltpu.VMEM((device_total, share, channels), bf16)
    half_ring = pltpu.VMEM((device_total // 2, share, channels), bf16)
    dma = pltpu.SemaphoreType.DMA
    places = [pltpu.VMEM(shape + (channels,), bf16) for shape in strip_shapes]
    operands = (
        grad_rows,
        owner.reshape(1, row_total),
        lat_offset.reshape(1, row_total),
        lon_offset.reshape(1, row_total),
        position.T,
        features,
        conv_weight,
    )
    input_grad, weight_grad = pl.pallas_call(
        functools.partial(solve_kernel, capacity, lat_total, lon_total),
        out_shape=[
            jax.ShapeDtypeStruct((tile_lat, tile_lon, channels), bf16),
            jax.ShapeDtypeStruct((flat_rows, channels), f32),
        ],
        in_specs=[smem] + [pl.BlockSpec(memory_space=pltpu.HBM)] * 7,
        out_specs=[vmem] * 2,
        scratch_shapes=[pltpu.VMEM(x.shape, x.dtype) for x in operands if x is not features]
        + [
            pltpu.VMEM((tall + 2, tile_lon, channels), bf16),
            pltpu.VMEM((tall, 32, channels), f32),
            pltpu.VMEM((3 * channels, tall * 16), bf16),
            pltpu.VMEM((tall * 16, 3 * channels), bf16),
            pltpu.VMEM(message, bf16),
            pltpu.VMEM(message, bf16),
            pltpu.VMEM((tall, wide, 2 * channels), f32),
            pltpu.VMEM((tall, wide + tile_lon // 2 + 16, channels), f32),
            pltpu.VMEM((tall, span), f32),
            pltpu.VMEM((2 * wide, span), bf16),
            pltpu.VMEM((span, 2 * channels), bf16),
        ]
        + places
        + places
        + [
            pltpu.VMEM((tall * tile_lon, 3 * channels), bf16),
            pltpu.VMEM((channels, (tall + 2) * tile_lon), bf16),
            pltpu.VMEM((3 * channels, 3 * channels), f32),
            pltpu.VMEM((flat_rows, channels), f32),
            pltpu.VMEM((4 * 3 * channels, 2 * channels), bf16),
            ring,
            half_ring,
            half_ring,
            pltpu.VMEM((share, channels), bf16),
            ring,
            dma((7,)),
            dma((device_total,)),
            dma((device_total,)),
            dma((2,)),
            dma((2,)),
            dma((8,)),
            dma((8,)),
            dma((2,)),
            dma((2,)),
            dma((device_total // 2,)),
            dma((device_total // 2,)),
            dma((device_total // 2,)),
            dma((device_total // 2,)),
        ],
        compiler_params=pltpu.CompilerParams(
            vmem_limit_bytes=44 * 2**20, collective_id=0, has_side_effects=True
        ),
        name="solve",
    )(live_count, *[pltpu.with_memory_space_constraint(x, pltpu.HBM) for x in operands])
    return input_grad, weight_grad.reshape(3, 3, channels, channels)


def solution(mesh):
    placed = (
        P(("lat", "lon"), None),
        P(("lat", "lon"), None),
        P(("lat", "lon")),
        P(("lat", "lon")),
        P(("lat", "lon"), None),
        P(("lat", "lon")),
        P("lat", "lon", None),
        P(),
    )
    return jax.shard_map(
        shards, mesh=mesh, in_specs=placed, out_specs=(P("lat", "lon", None), P()), check_vma=False
    )
```

```python
import functools
import math

import jax
import jax.numpy as jnp
from jax import lax
from jax.experimental import pallas as pl
from jax.experimental.pallas import tpu as pltpu
from jax.sharding import PartitionSpec as P

rbf_scale = 1.5
taps = 8
before = 3
after = taps - 1 - before
geom_rows = 8
f32 = jnp.float32
bf16 = jnp.bfloat16


def solve_kernel(
    capacity,
    lat_total,
    lon_total,
    live_ref,
    rows_hbm,
    owner_hbm,
    lat_hbm,
    lon_hbm,
    pos_hbm,
    feat_hbm,
    weight_hbm,
    ig_ref,
    gathered,
    *refs,
):
    (rows_ref, owner_ref, lat_ref, lon_ref, pos_ref, weight_ref) = refs[:6]
    (field, stage, beside, edges) = refs[6:10]
    (held, inbox, sums, canvas, lat_taps, lon_taps, halves) = refs[10:17]
    strips, landed = refs[17:25], refs[25:33]
    (windows, turned, total, flat, mixer, pieces, twin, parts, mine) = refs[33:42]
    (load_sem, send_sem, recv_sem, field_send, field_recv) = refs[42:47]
    halo_send, halo_recv, pair_send, pair_recv, part_send, part_recv, all_send, all_recv = refs[47:]
    devices = inbox.shape[0]
    row_total, channels = rows_ref.shape
    tile_lat, tile_lon = ig_ref.shape[:2]
    up, down = before + 1, after + 1
    tall = canvas.shape[0]
    own_field = field.at[up : up + tile_lat]
    lat, lon = lax.axis_index("lat"), lax.axis_index("lon")
    me = lon * lat_total + lat
    span = halves.shape[0]
    group = span // capacity
    groups = devices // group
    ours = me // group
    half = tile_lon // 2
    inv = 1.0 / (2.0 * rbf_scale * rbf_scale)

    def place(peer):
        return (peer % lat_total, peer // lat_total)

    barrier = pltpu.get_barrier_semaphore()

    def greet(k, _):
        pl.semaphore_signal(
            barrier, inc=1, device_id=place((me + k) % devices), device_id_type=pl.DeviceIdType.MESH
        )
        return 0

    loads = [
        pltpu.make_async_copy(src, dst, load_sem.at[k])
        for k, (src, dst) in enumerate(
            zip(
                (rows_hbm, owner_hbm, lat_hbm, lon_hbm, pos_hbm, feat_hbm, weight_hbm),
                (rows_ref, owner_ref, lat_ref, lon_ref, pos_ref, own_field, weight_ref),
            )
        )
    ]
    for load in loads:
        load.start()
    lax.fori_loop(1, devices, greet, 0)
    sums[...] = jnp.zeros_like(sums)
    mixer[...] = jnp.zeros_like(mixer)
    total[...] = jnp.zeros_like(total)
    rows, cols = tile_lat + 2, tile_lon + 2
    stage[...] = jnp.zeros_like(stage)
    for margin in (slice(0, 8), slice(canvas.shape[1] - 8, canvas.shape[1])):
        canvas[:, margin, :] = jnp.zeros((tall, 8, channels), f32)
    field[tall + 1] = jnp.zeros(field.shape[1:], bf16)

    @pl.when(lat == 0)
    def _():
        field[0:up] = jnp.zeros((up,) + field.shape[1:], bf16)

    @pl.when(lat == lat_total - 1)
    def _():
        field[up + tile_lat : tall + 1] = jnp.zeros((down,) + field.shape[1:], bf16)

    for load in loads[:5]:
        load.wait()

    live = lax.broadcasted_iota(jnp.int32, (1, row_total), 1) < live_ref[0]
    tile = owner_ref[...].astype(f32)
    tile_row = jnp.floor((tile + 0.5) * (1.0 / lon_total))
    owner = (tile - tile_row * lon_total) * lat_total + tile_row
    owner = jnp.where(live, owner, float(devices)).astype(jnp.int32)
    match = lax.broadcasted_iota(jnp.int32, (devices, row_total), 0) == owner
    match = jnp.where(match, 1.0, 0.0)
    blocks = row_total // 128
    upper = lax.broadcasted_iota(jnp.int32, (128, 128), 0) < lax.broadcasted_iota(
        jnp.int32, (128, 128), 1
    )
    upper = jnp.where(upper, 1.0, 0.0).astype(bf16)
    columns = [match[:, k * 128 : (k + 1) * 128] for k in range(blocks)]
    earlier = jnp.dot(
        jnp.concatenate(columns, axis=0).astype(bf16), upper, preferred_element_type=f32
    )
    before_block = jnp.zeros((devices, 1), f32)
    ranks = []
    for k, part in enumerate(columns):
        ahead = earlier[k * devices : (k + 1) * devices] + before_block
        ranks.append(jnp.sum(ahead * part, axis=0, keepdims=True))
        before_block = before_block + jnp.sum(part, axis=1, keepdims=True)
    rank = jnp.concatenate(ranks, axis=1).astype(jnp.int32)
    slot = owner * capacity + rank
    geometry = jnp.concatenate(
        [
            pos_ref[...].astype(f32),
            lat_ref[...].astype(f32),
            lon_ref[...].astype(f32),
            jnp.zeros((geom_rows - 4, row_total), f32),
        ],
        axis=0,
    ).astype(bf16)
    fold = 128 // capacity
    chunk = math.gcd(group, max(1, 256 // capacity))
    line = lax.broadcasted_iota(jnp.int32, (chunk * capacity, row_total), 0)
    lane_block = lax.broadcasted_iota(jnp.int32, (geom_rows, 128), 1) // capacity

    def build(first):
        hit = jnp.where(line == slot - first * capacity, 1.0, 0.0).astype(bf16)
        placed = jnp.dot(hit, rows_ref[...], preferred_element_type=f32).astype(bf16)
        info = lax.dot_general(
            geometry, hit, (((1,), (1,)), ((), ())), preferred_element_type=f32
        )
        for i in range(chunk):
            held[first + i, 0:capacity, :] = placed[i * capacity : (i + 1) * capacity]
        for v in range(chunk // fold):
            piece = info[:, v * 128 : (v + 1) * 128]
            rolled = [piece] + [pltpu.roll(piece, s * capacity, 1) for s in range(1, fold)]
            for i in range(fold):
                tiled = rolled[(fold - i) % fold]
                for t in range(1, fold):
                    tiled = jnp.where(lane_block == t, rolled[(t - i) % fold], tiled)
                held[first + v * fold + i, capacity : capacity + geom_rows, :] = tiled.astype(bf16)

    def copy_to(peer, slot_at):
        return pltpu.make_async_remote_copy(
            src_ref=held.at[peer],
            dst_ref=inbox.at[slot_at],
            send_sem=send_sem.at[peer],
            recv_sem=recv_sem.at[slot_at],
            device_id=place(peer),
            device_id_type=pl.DeviceIdType.MESH,
        )

    def send(first):
        for i in range(chunk):
            peer = first + i

            @pl.when(peer != me)
            def _():
                copy_to(peer, me).start()

    if groups == 4:
        order = [3 - ours, (ours + 2) % 4, ours + 1 - 2 * (ours % 2), ours]
    else:
        order = [(ours + groups // 2 + k) % groups for k in range(groups)]
    per = group // chunk
    steps = [(q, c) for q in order for c in range(per)]
    first_of = [q * group + c * chunk for q, c in steps]
    early = len(first_of) // 2
    for first in first_of[:early]:
        build(first)
    pl.semaphore_wait(barrier, devices - 1)
    for first in first_of[:early]:
        send(first)
    for first in first_of[early:]:
        build(first)
        send(first)
    inbox[me] = held[me]

    loads[5].wait()

    def when(da, cond, fn):
        if da == 0:
            fn()
        else:
            pl.when(cond)(fn)

    ways = ((-1, 0), (1, 0), (0, -1), (0, 1), (-1, -1), (-1, 1), (1, -1), (1, 1))
    reach = 8
    borders = []
    for w, (da, source, target) in enumerate(
        (
            (-1, slice(up, up + down), slice(up + tile_lat, tall + 1)),
            (1, slice(tile_lat, up + tile_lat), slice(0, up)),
        )
    ):
        copy = pltpu.make_async_remote_copy(
            src_ref=field.at[source],
            dst_ref=field.at[target],
            send_sem=field_send.at[w],
            recv_sem=field_recv.at[w],
            device_id=((lat + da + lat_total) % lat_total, lon),
            device_id_type=pl.DeviceIdType.MESH,
        )
        sends = (lat + da >= 0) & (lat + da < lat_total)
        takes = (lat - da >= 0) & (lat - da < lat_total)
        borders.append((copy, sends, takes))
    for (copy, sends, _), (da, _) in zip(borders, ways):
        when(da, sends, copy.start)

    def aligned(start, size):
        if not isinstance(start, int):
            start = pl.multiple_of(start, tile_lon)
        return pl.ds(start, size)

    def turn(p):
        turned[:, aligned(p * tile_lon, tile_lon)] = field[p].T

    fast = math.gcd(tile_lat, 8)

    def turn_some(k, _):
        for j in range(fast):
            turn(up + k * fast + j)
        return 0

    lax.fori_loop(0, tile_lat // fast, turn_some, 0)
    loads[6].wait()
    for a in range(3):
        for b in range(3):
            tap = weight_ref[a, b].T
            for r in range(2):
                at = ((r + 2 - a) * 3 + b) * channels
                mixer[at : at + channels, r * channels : (r + 1) * channels] = tap

    line_lat = lax.broadcasted_iota(jnp.int32, (lat_taps.shape[0], span), 0).astype(f32)
    line_lon = lax.broadcasted_iota(jnp.int32, (lon_taps.shape[0], span), 0).astype(f32)
    lanes = lax.broadcasted_iota(jnp.int32, (8, 128), 1) // capacity
    wide = sums.shape[1]
    line_lon = jnp.where(line_lon >= wide, line_lon - wide, line_lon)
    stride = next(n for n in (24, 12, 8, 4, 2) if tall % n == 0)

    def taps_of(line, base, frac):
        tap = line - base
        d = tap - (frac + before)
        weight = jnp.exp(-(d * d) * inv)
        return jnp.where((tap >= 0.0) & (tap <= taps - 1.0), weight, 0.0)

    pad = reach

    def collect(q, last):
        for i in range(group):
            peer = q * group + i

            @pl.when(peer != me)
            def _():
                copy_to(peer, peer).wait_recv()

        first = q * group
        infos = []
        for v in range(span // 128):
            at = first + v * fold
            info = inbox[at, capacity : capacity + geom_rows, :].astype(f32)
            for t in range(1, fold):
                info = jnp.where(
                    lanes == t, inbox[at + t, capacity : capacity + geom_rows, :].astype(f32), info
                )
            infos.append(info)
        info = jnp.concatenate(infos, axis=1)
        lat_frac, lon_frac, row_at, col_at = (info[k : k + 1] for k in range(4))
        right = jnp.where(col_at >= half, 1.0, 0.0)
        lat_taps[...] = taps_of(line_lat, row_at, lat_frac).astype(bf16).astype(f32)
        lon_taps[...] = taps_of(line_lon, col_at - right * half, lon_frac).astype(bf16)
        for v in range(span // 128):
            side = jnp.broadcast_to(right[:, v * 128 : (v + 1) * 128], (128, 128)).T.astype(bf16)
            rows = jnp.concatenate(
                [inbox[first + v * fold + t, 0:capacity, :] for t in range(fold)], axis=0
            )
            at = slice(v * 128, (v + 1) * 128)
            on_right = rows * side
            halves[at, 0:channels] = rows - on_right
            halves[at, channels : 2 * channels] = on_right

        def add(k, _):
            lhs = []
            for j in range(0, stride, 2):
                pair = [
                    jnp.broadcast_to(lat_taps[pl.ds(k * stride + j + n, 1), :], (8, span))
                    for n in range(2)
                ]
                for t in range(0, 2 * wide, 16):
                    row = jnp.concatenate([pair[t // wide], pair[(t + 8) // wide]], axis=0)
                    lhs.append(row.astype(bf16) * lon_taps[t : t + 16, :])
            out = jnp.dot(jnp.concatenate(lhs, axis=0), halves[...], preferred_element_type=f32)
            for j in range(stride):
                i = k * stride + j
                row = sums[i] + out[j * wide : (j + 1) * wide]
                if not last:
                    sums[i] = row
                    continue
                left, right = row[:, 0:channels], row[:, channels : 2 * channels]
                canvas[i, pad : pad + half, :] = left[0:half]
                canvas[i, pad + half : pad + wide, :] = left[half:wide] + right[0 : wide - half]
                canvas[i, pad + wide : pad + wide + half, :] = right[wide - half : wide]
            return 0

        lax.fori_loop(0, tall // stride, add, 0)

    slots = 2 * reach
    rows_at_once = 128 // slots
    last_chunk = tall // rows_at_once - 1

    def flank(chunks):
        for a in range(3):
            for k in chunks:
                at = slice(a + k * rows_at_once, a + (k + 1) * rows_at_once)
                both = jnp.concatenate(
                    [field[at, 0:reach], field[at, tile_lon - reach : tile_lon]], axis=1
                )
                beside[a * channels : (a + 1) * channels, k * 128 : (k + 1) * 128] = both.reshape(
                    128, channels
                ).T

    def border():
        for (copy, _, takes), (da, _) in zip(borders, ways):
            when(da, takes, copy.wait_recv)
        for p in (*range(up), *range(up + tile_lat, tall + 2)):
            turn(p)
        flank((0, last_chunk))

    for k, q in enumerate([order[3], order[2], order[0], order[1]] if groups == 4 else order[::-1]):
        if k == groups - 1:
            flank(range(1, last_chunk))
        collect(q, k == groups - 1)

    inset = before - 1
    edge = pad + inset

    @pl.when(lat == 0)
    def _():
        canvas[0:before] = jnp.zeros((before,) + canvas.shape[1:], f32)

    @pl.when(lat == lat_total - 1)
    def _():
        canvas[before + tile_lat : tall] = jnp.zeros((tall - before - tile_lat,) + canvas.shape[1:], f32)

    some = math.gcd(tall, 4)

    def emit(k, _):
        for j in range(some):
            i = k * some + j
            strips[2][i] = canvas[i, pad : pad + up, :].astype(bf16)
            strips[3][i] = canvas[i, edge + cols - 2 : edge + cols - 2 + down, :].astype(bf16)
        return 0

    lax.fori_loop(0, tall // some, emit, 0)
    halos = []
    for w, (da, db) in enumerate(ways):
        copy = pltpu.make_async_remote_copy(
            src_ref=strips[w],
            dst_ref=landed[w],
            send_sem=halo_send.at[w],
            recv_sem=halo_recv.at[w],
            device_id=((lat + da + lat_total) % lat_total, (lon + db + lon_total) % lon_total),
            device_id_type=pl.DeviceIdType.MESH,
        )
        sends = (lat + da >= 0) & (lat + da < lat_total)
        takes = (lat - da >= 0) & (lat - da < lat_total)
        halos.append((copy, sends, takes))
    beside_halos = halos[2:4]
    for copy, _, _ in beside_halos:
        copy.start()
    spans = ((pad, up), (edge, cols), (edge + cols - 2, down))
    for count, first, refs in (
        (up, 0, (strips[4], strips[0], strips[5])),
        (down, inset + rows - 2, (strips[6], strips[1], strips[7])),
    ):
        for i in range(count):
            for (start, width), ref in zip(spans, refs):
                ref[i] = canvas[first + i, start : start + width, :].astype(bf16)
    for (copy, sends, _), (da, _) in zip(halos, ways):
        if da != 0:
            pl.when(sends)(copy.start)
    chips = devices // 2
    at = lat * lon_total + lon
    core, chip = at % 2, at // 2
    other = 1 - core

    def seat(peer):
        return (peer // lon_total, peer % lon_total)

    def shift(i, _):
        at = pl.ds(pl.multiple_of(i * tile_lon, tile_lon), tile_lon)
        for b in range(3):
            windows[at, b * channels : (b + 1) * channels] = canvas[
                i, edge + 2 - b : edge + 2 - b + tile_lon, :
            ].astype(bf16)
        return 0

    lax.fori_loop(0, tall, shift, 0)

    def shift_edges(k, _):
        for j in range(some):
            i = k * some + j
            stage[i, 0:down] = landed[3][i].astype(f32)
            stage[i, 3 * reach : 3 * reach + up] = landed[2][i].astype(f32)
            at = pl.ds(pl.multiple_of(i * 2 * reach, 2 * reach), 2 * reach)
            for b in range(3):
                first, second = 2 - b, 2 * reach + up - b
                both = [stage[i, first : first + reach, :], stage[i, second : second + reach, :]]
                edges[at, b * channels : (b + 1) * channels] = jnp.concatenate(
                    both, axis=0
                ).astype(bf16)
        return 0

    step = next(n for n in (12, 8, 6, 4, 3, 2, 1) if tall % n == 0)
    depth = step * tile_lon

    def weigh(k, _):
        start = k * depth
        lhs = jnp.concatenate(
            [
                turned[:, aligned(start + a * tile_lon, depth)]
                for a in range(3)
            ],
            axis=0,
        )
        rhs = windows[aligned(start, depth), :]
        total[...] += jnp.dot(lhs, rhs, preferred_element_type=f32)
        return 0

    last_step = tall // step - 1
    lax.fori_loop(1, last_step, weigh, 0)
    border()
    weigh(0, 0)
    weigh(last_step, 0)
    for copy, _, _ in beside_halos:
        copy.wait_recv()
    lax.fori_loop(0, tall // some, shift_edges, 0)
    total[...] += jnp.dot(beside[...], edges[...], preferred_element_type=f32)
    for a in range(3):
        for b in range(3):
            at = (a * 3 + b) * channels
            flat[at : at + channels, :] = total[
                a * channels : (a + 1) * channels, b * channels : (b + 1) * channels
            ]
    share = pieces.shape[1]

    def cut(d, _):
        pieces[d] = flat[pl.ds(d * share, share), :].astype(bf16)
        return 0

    lax.fori_loop(0, devices, cut, 0)
    part = math.gcd(tile_lat // 2, 8)
    strides = tile_lat // 2 // part
    first = strides // 2

    def apply(k, _):
        lhs = jnp.concatenate(
            [
                jnp.concatenate(
                    [
                        windows[
                            pl.ds(
                                pl.multiple_of(
                                    (inset + 2 * (k * part + j) + r) * tile_lon, tile_lon
                                ),
                                tile_lon,
                            ),
                            :,
                        ]
                        for r in range(4)
                    ],
                    axis=1,
                )
                for j in range(part)
            ],
            axis=0,
        )
        acc = jnp.dot(lhs, mixer[...], preferred_element_type=f32).astype(bf16)
        for j in range(part):
            for r in range(2):
                ig_ref[2 * (k * part + j) + r] = acc[
                    j * tile_lon : (j + 1) * tile_lon, r * channels : (r + 1) * channels
                ]
        return 0

    def settle():
        for (copy, _, takes), (da, db), ref in zip(halos, ways, landed):

            def take(copy=copy, da=da, db=db, ref=ref):
                if da != 0:
                    copy.wait_recv()
                high = {-1: inset + rows - up, 0: 0, 1: inset}[da]
                count = {-1: up, 0: tall, 1: down}[da]
                left = {-1: cols - up, 0: 0, 1: 0}[db]
                width = {-1: up, 0: cols, 1: down}[db]

                def add(i, _):
                    canvas[high + i, edge + left : edge + left + width, :] += ref[i].astype(f32)
                    return 0

                lax.fori_loop(0, count, add, 0)

            when(da, takes, take)

        lax.fori_loop(inset, inset + rows, shift, 0)

    def paired(src, dst, n):
        return pltpu.make_async_remote_copy(
            src_ref=src,
            dst_ref=dst,
            send_sem=pair_send.at[n],
            recv_sem=pair_recv.at[n],
            device_id=seat(chip * 2 + other),
            device_id_type=pl.DeviceIdType.MESH,
        )

    def scattered(peer, slot):
        return pltpu.make_async_remote_copy(
            src_ref=pieces.at[core * chips + peer],
            dst_ref=parts.at[slot],
            send_sem=part_send.at[peer],
            recv_sem=part_recv.at[slot],
            device_id=seat(peer * 2 + core),
            device_id_type=pl.DeviceIdType.MESH,
        )

    def shared(peer, slot):
        return pltpu.make_async_remote_copy(
            src_ref=mine,
            dst_ref=gathered.at[core * chips + slot],
            send_sem=all_send.at[peer],
            recv_sem=all_recv.at[slot],
            device_id=seat(peer * 2 + core),
            device_id_type=pl.DeviceIdType.MESH,
        )

    def each_chip(fn):
        def body(k, _):
            fn((chip + k) % chips)
            return 0

        lax.fori_loop(1, chips, body, 0)

    swap = paired(pieces.at[pl.ds(other * chips, chips)], twin, 0)
    swap.start()
    swap.wait_recv()

    def merge(p, _):
        at = core * chips + p
        pieces[at] = (flat[pl.ds(at * share, share), :] + twin[p].astype(f32)).astype(bf16)
        return 0

    lax.fori_loop(0, chips, merge, 0)
    each_chip(lambda peer: scattered(peer, chip).start())
    settle()
    lax.fori_loop(0, first, apply, 0)
    parts[chip] = pieces[core * chips + chip]
    each_chip(lambda peer: scattered(peer, peer).wait_recv())

    def gather_sum(p, acc):
        return acc + parts[p].astype(f32)

    mine[...] = lax.fori_loop(
        0, chips, gather_sum, jnp.zeros((share, channels), f32)
    ).astype(bf16)
    each_chip(lambda peer: shared(peer, chip).start())
    gathered[core * chips + chip] = mine[...]
    lax.fori_loop(first, strides, apply, 0)
    each_chip(lambda peer: shared(peer, peer).wait_recv())
    kept = gathered.at[pl.ds(core * chips, chips)]
    back = paired(kept, kept, 1)
    back.start()

    back.wait_recv()
    for (copy, sends, _), (da, _) in zip(halos + borders, ways + ways[:2]):
        when(da, sends, copy.wait_send)
    swap.wait_send()
    back.wait_send()
    each_chip(lambda peer: scattered(peer, chip).wait_send())
    each_chip(lambda peer: shared(peer, chip).wait_send())

    def each(fn):
        def body(k, _):
            fn((me + k) % devices)
            return 0

        lax.fori_loop(1, devices, body, 0)

    each(lambda peer: copy_to(peer, me).wait_send())


def finish_kernel(grad_ref, shares_ref, grad_out, weight_out, flat, sem):
    grad_copy = pltpu.make_async_copy(grad_ref, grad_out, sem.at[0])
    grad_copy.start()
    share = shares_ref.shape[1]
    for d in range(shares_ref.shape[0]):
        flat[d * share : (d + 1) * share, :] = shares_ref[d].astype(f32)
    weight_copy = pltpu.make_async_copy(flat, weight_out, sem.at[1])
    weight_copy.start()
    grad_copy.wait()
    weight_copy.wait()


def shards(grad_rows, owner, lat_offset, lon_offset, position, live_count, features, conv_weight):
    lat_total = lax.axis_size("lat")
    lon_total = lax.axis_size("lon")
    device_total = lat_total * lon_total
    row_total, channels = grad_rows.shape
    tile_lat, tile_lon = features.shape[:2]
    capacity = max(2, 2 * row_total // device_total)
    smem = pl.BlockSpec(memory_space=pltpu.SMEM)
    vmem = pl.BlockSpec(memory_space=pltpu.VMEM)

    rows, cols = tile_lat + 2, tile_lon + 2
    tall = -(-(tile_lat + taps - 1) // 8) * 8
    wide = tile_lon // 2 + 8
    span = math.gcd(device_total, max(1, 512 // capacity)) * capacity
    up, down = before + 1, after + 1
    strip_shapes = [
        (up, cols),
        (down, cols),
        (tall, up),
        (tall, down),
        (up, up),
        (up, down),
        (down, up),
        (down, down),
    ]
    message = (device_total, capacity + geom_rows, channels)
    flat_rows = 9 * channels
    share = flat_rows // device_total
    ring = pltpu.VMEM((device_total, share, channels), bf16)
    half_ring = pltpu.VMEM((device_total // 2, share, channels), bf16)
    dma = pltpu.SemaphoreType.DMA
    places = [pltpu.VMEM(shape + (channels,), bf16) for shape in strip_shapes]
    operands = (
        grad_rows,
        owner.reshape(1, row_total),
        lat_offset.reshape(1, row_total),
        lon_offset.reshape(1, row_total),
        position.T,
        features,
        conv_weight,
    )
    inner_grad, shares = pl.pallas_call(
        functools.partial(solve_kernel, capacity, lat_total, lon_total),
        out_shape=[
            jax.ShapeDtypeStruct((tile_lat, tile_lon, channels), bf16),
            jax.ShapeDtypeStruct((device_total, share, channels), bf16),
        ],
        in_specs=[smem] + [pl.BlockSpec(memory_space=pltpu.HBM)] * 7,
        out_specs=[vmem] * 2,
        scratch_shapes=[pltpu.VMEM(x.shape, x.dtype) for x in operands if x is not features]
        + [
            pltpu.VMEM((tall + 2, tile_lon, channels), bf16),
            pltpu.VMEM((tall, 32, channels), f32),
            pltpu.VMEM((3 * channels, tall * 16), bf16),
            pltpu.VMEM((tall * 16, 3 * channels), bf16),
            pltpu.VMEM(message, bf16),
            pltpu.VMEM(message, bf16),
            pltpu.VMEM((tall, wide, 2 * channels), f32),
            pltpu.VMEM((tall, wide + tile_lon // 2 + 16, channels), f32),
            pltpu.VMEM((tall, span), f32),
            pltpu.VMEM((2 * wide, span), bf16),
            pltpu.VMEM((span, 2 * channels), bf16),
        ]
        + places
        + places
        + [
            pltpu.VMEM((tall * tile_lon, 3 * channels), bf16),
            pltpu.VMEM((channels, (tall + 2) * tile_lon), bf16),
            pltpu.VMEM((3 * channels, 3 * channels), f32),
            pltpu.VMEM((flat_rows, channels), f32),
            pltpu.VMEM((4 * 3 * channels, 2 * channels), bf16),
            ring,
            half_ring,
            half_ring,
            pltpu.VMEM((share, channels), bf16),
            dma((7,)),
            dma((device_total,)),
            dma((device_total,)),
            dma((2,)),
            dma((2,)),
            dma((8,)),
            dma((8,)),
            dma((2,)),
            dma((2,)),
            dma((device_total // 2,)),
            dma((device_total // 2,)),
            dma((device_total // 2,)),
            dma((device_total // 2,)),
        ],
        compiler_params=pltpu.CompilerParams(
            vmem_limit_bytes=44 * 2**20, collective_id=0, has_side_effects=True
        ),
        name="solve",
    )(live_count, *[pltpu.with_memory_space_constraint(x, pltpu.HBM) for x in operands])
    input_grad, weight_grad = pl.pallas_call(
        finish_kernel,
        out_shape=[
            jax.ShapeDtypeStruct((tile_lat, tile_lon, channels), bf16),
            jax.ShapeDtypeStruct((flat_rows, channels), f32),
        ],
        in_specs=[vmem] * 2,
        out_specs=[pl.BlockSpec(memory_space=pltpu.HBM)] * 2,
        scratch_shapes=[pltpu.VMEM((flat_rows, channels), f32), dma((2,))],
        compiler_params=pltpu.CompilerParams(vmem_limit_bytes=8 * 2**20),
        name="finish",
    )(inner_grad, shares)
    return input_grad, weight_grad.reshape(3, 3, channels, channels)


def solution(mesh):
    placed = (
        P(("lat", "lon"), None),
        P(("lat", "lon"), None),
        P(("lat", "lon")),
        P(("lat", "lon")),
        P(("lat", "lon"), None),
        P(("lat", "lon")),
        P("lat", "lon", None),
        P(),
    )
    return jax.shard_map(
        shards, mesh=mesh, in_specs=placed, out_specs=(P("lat", "lon", None), P()), check_vma=False
    )
```

```python
import functools
import math

import jax
import jax.numpy as jnp
from jax import lax
from jax.experimental import pallas as pl
from jax.experimental.pallas import tpu as pltpu
from jax.sharding import PartitionSpec as P

rbf_scale = 1.5
taps = 8
before = 3
after = taps - 1 - before
geom_rows = 8
f32 = jnp.float32
bf16 = jnp.bfloat16


def solve_kernel(
    capacity,
    lat_total,
    lon_total,
    live_ref,
    rows_hbm,
    owner_hbm,
    lat_hbm,
    lon_hbm,
    pos_hbm,
    feat_hbm,
    weight_hbm,
    ig_ref,
    gathered,
    *refs,
):
    (rows_ref, owner_ref, lat_ref, lon_ref, pos_ref, weight_ref) = refs[:6]
    (field, stage, beside, edges) = refs[6:10]
    (held, inbox, sums, canvas, lat_taps, lon_taps, halves) = refs[10:17]
    strips, landed = refs[17:25], refs[25:33]
    (windows, turned, total, flat, mixer, pieces, twin, parts, mine) = refs[33:42]
    (load_sem, send_sem, recv_sem, field_send, field_recv) = refs[42:47]
    halo_send, halo_recv, pair_send, pair_recv, part_send, part_recv, all_send, all_recv = refs[47:]
    devices = inbox.shape[0]
    row_total, channels = rows_ref.shape
    tile_lat, tile_lon = ig_ref.shape[:2]
    up, down = before + 1, after + 1
    tall = canvas.shape[0]
    own_field = field.at[up : up + tile_lat]
    lat, lon = lax.axis_index("lat"), lax.axis_index("lon")
    me = lon * lat_total + lat
    span = halves.shape[0]
    group = span // capacity
    groups = devices // group
    ours = me // group
    half = tile_lon // 2
    inv = 1.0 / (2.0 * rbf_scale * rbf_scale)

    def place(peer):
        return (peer % lat_total, peer // lat_total)

    barrier = pltpu.get_barrier_semaphore()

    if groups == 4:
        order = [3 - ours, (ours + 2) % 4, ours + 1 - 2 * (ours % 2), ours]
    else:
        order = [(ours + groups // 2 + k) % groups for k in range(groups)]
    for q in order:
        for i in range(group):
            peer = q * group + i

            @pl.when(peer != me)
            def _():
                pl.semaphore_signal(
                    barrier, inc=1, device_id=place(peer), device_id_type=pl.DeviceIdType.MESH
                )

    loads = [
        pltpu.make_async_copy(src, dst, load_sem.at[k])
        for k, (src, dst) in enumerate(
            zip(
                (rows_hbm, owner_hbm, lat_hbm, lon_hbm, pos_hbm, feat_hbm, weight_hbm),
                (rows_ref, owner_ref, lat_ref, lon_ref, pos_ref, own_field, weight_ref),
            )
        )
    ]
    for load in loads:
        load.start()
    sums[...] = jnp.zeros_like(sums)
    mixer[...] = jnp.zeros_like(mixer)
    total[...] = jnp.zeros_like(total)
    rows, cols = tile_lat + 2, tile_lon + 2
    stage[...] = jnp.zeros_like(stage)
    for margin in (slice(0, 8), slice(canvas.shape[1] - 8, canvas.shape[1])):
        canvas[:, margin, :] = jnp.zeros((tall, 8, channels), f32)
    field[tall + 1] = jnp.zeros(field.shape[1:], bf16)

    @pl.when(lat == 0)
    def _():
        field[0:up] = jnp.zeros((up,) + field.shape[1:], bf16)

    @pl.when(lat == lat_total - 1)
    def _():
        field[up + tile_lat : tall + 1] = jnp.zeros((down,) + field.shape[1:], bf16)

    for load in loads[:5]:
        load.wait()

    live = lax.broadcasted_iota(jnp.int32, (1, row_total), 1) < live_ref[0]
    tile = owner_ref[...].astype(f32)
    tile_row = jnp.floor((tile + 0.5) * (1.0 / lon_total))
    owner = (tile - tile_row * lon_total) * lat_total + tile_row
    owner = jnp.where(live, owner, float(devices)).astype(jnp.int32)
    match = lax.broadcasted_iota(jnp.int32, (devices, row_total), 0) == owner
    match = jnp.where(match, 1.0, 0.0)
    blocks = row_total // 128
    upper = lax.broadcasted_iota(jnp.int32, (128, 128), 0) < lax.broadcasted_iota(
        jnp.int32, (128, 128), 1
    )
    upper = jnp.where(upper, 1.0, 0.0).astype(bf16)
    columns = [match[:, k * 128 : (k + 1) * 128] for k in range(blocks)]
    earlier = jnp.dot(
        jnp.concatenate(columns, axis=0).astype(bf16), upper, preferred_element_type=f32
    )
    before_block = jnp.zeros((devices, 1), f32)
    ranks = []
    for k, part in enumerate(columns):
        ahead = earlier[k * devices : (k + 1) * devices] + before_block
        ranks.append(jnp.sum(ahead * part, axis=0, keepdims=True))
        before_block = before_block + jnp.sum(part, axis=1, keepdims=True)
    rank = jnp.concatenate(ranks, axis=1).astype(jnp.int32)
    slot = owner * capacity + rank
    geometry = jnp.concatenate(
        [
            pos_ref[...].astype(f32),
            lat_ref[...].astype(f32),
            lon_ref[...].astype(f32),
            jnp.zeros((geom_rows - 4, row_total), f32),
        ],
        axis=0,
    ).astype(bf16)
    fold = 128 // capacity
    chunk = math.gcd(group, max(1, 256 // capacity))
    line = lax.broadcasted_iota(jnp.int32, (chunk * capacity, row_total), 0)
    lane_block = lax.broadcasted_iota(jnp.int32, (geom_rows, 128), 1) // capacity

    def build(first):
        hit = jnp.where(line == slot - first * capacity, 1.0, 0.0).astype(bf16)
        placed = jnp.dot(hit, rows_ref[...], preferred_element_type=f32).astype(bf16)
        info = lax.dot_general(
            geometry, hit, (((1,), (1,)), ((), ())), preferred_element_type=f32
        )
        for i in range(chunk):
            held[first + i, 0:capacity, :] = placed[i * capacity : (i + 1) * capacity]
        for v in range(chunk // fold):
            piece = info[:, v * 128 : (v + 1) * 128]
            rolled = [piece] + [pltpu.roll(piece, s * capacity, 1) for s in range(1, fold)]
            for i in range(fold):
                tiled = rolled[(fold - i) % fold]
                for t in range(1, fold):
                    tiled = jnp.where(lane_block == t, rolled[(t - i) % fold], tiled)
                held[first + v * fold + i, capacity : capacity + geom_rows, :] = tiled.astype(bf16)

    def copy_to(peer, slot_at):
        return pltpu.make_async_remote_copy(
            src_ref=held.at[peer],
            dst_ref=inbox.at[slot_at],
            send_sem=send_sem.at[peer],
            recv_sem=recv_sem.at[slot_at],
            device_id=place(peer),
            device_id_type=pl.DeviceIdType.MESH,
        )

    def send(first):
        for i in range(chunk):
            peer = first + i

            @pl.when(peer != me)
            def _():
                copy_to(peer, me).start()

    per = group // chunk
    first_of = [q * group + ((c + lon) % per) * chunk for q in order for c in range(per)]
    early = len(first_of) // 2
    for first in first_of[:early]:
        build(first)
    pl.semaphore_wait(barrier, devices - 1)
    for first in first_of[:early]:
        send(first)
    for first in first_of[early:]:
        build(first)
        send(first)
    inbox[me] = held[me]

    loads[5].wait()

    def when(da, cond, fn):
        if da == 0:
            fn()
        else:
            pl.when(cond)(fn)

    ways = ((-1, 0), (1, 0), (0, -1), (0, 1), (-1, -1), (-1, 1), (1, -1), (1, 1))
    reach = 8
    borders = []
    for w, (da, source, target) in enumerate(
        (
            (-1, slice(up, up + down), slice(up + tile_lat, tall + 1)),
            (1, slice(tile_lat, up + tile_lat), slice(0, up)),
        )
    ):
        copy = pltpu.make_async_remote_copy(
            src_ref=field.at[source],
            dst_ref=field.at[target],
            send_sem=field_send.at[w],
            recv_sem=field_recv.at[w],
            device_id=((lat + da + lat_total) % lat_total, lon),
            device_id_type=pl.DeviceIdType.MESH,
        )
        sends = (lat + da >= 0) & (lat + da < lat_total)
        takes = (lat - da >= 0) & (lat - da < lat_total)
        borders.append((copy, sends, takes))
    for (copy, sends, _), (da, _) in zip(borders, ways):
        when(da, sends, copy.start)

    def aligned(start, size):
        if not isinstance(start, int):
            start = pl.multiple_of(start, tile_lon)
        return pl.ds(start, size)

    def turn(p):
        turned[:, aligned(p * tile_lon, tile_lon)] = field[p].T

    fast = math.gcd(tile_lat, 8)

    def turn_some(k, _):
        for j in range(fast):
            turn(up + k * fast + j)
        return 0

    lax.fori_loop(0, tile_lat // fast, turn_some, 0)
    loads[6].wait()
    for a in range(3):
        for b in range(3):
            tap = weight_ref[a, b].T
            for r in range(2):
                at = ((r + 2 - a) * 3 + b) * channels
                mixer[at : at + channels, r * channels : (r + 1) * channels] = tap

    line_lat = lax.broadcasted_iota(jnp.int32, (lat_taps.shape[0], span), 0).astype(f32)
    line_lon = lax.broadcasted_iota(jnp.int32, (lon_taps.shape[0], span), 0).astype(f32)
    lanes = lax.broadcasted_iota(jnp.int32, (8, 128), 1) // capacity
    wide = sums.shape[1]
    line_lon = jnp.where(line_lon >= wide, line_lon - wide, line_lon)
    stride = next(n for n in (24, 12, 8, 4, 2) if tall % n == 0)

    def taps_of(line, base, frac):
        tap = line - base
        d = tap - (frac + before)
        weight = jnp.exp(-(d * d) * inv)
        return jnp.where((tap >= 0.0) & (tap <= taps - 1.0), weight, 0.0)

    pad = reach

    def collect(first, count, last):
        size = count * capacity
        for i in range(count):
            peer = first + i

            @pl.when(peer != me)
            def _():
                copy_to(peer, peer).wait_recv()

        infos = []
        for v in range(size // 128):
            at = first + v * fold
            info = inbox[at, capacity : capacity + geom_rows, :].astype(f32)
            for t in range(1, fold):
                info = jnp.where(
                    lanes == t, inbox[at + t, capacity : capacity + geom_rows, :].astype(f32), info
                )
            infos.append(info)
        info = jnp.concatenate(infos, axis=1)
        lat_frac, lon_frac, row_at, col_at = (info[k : k + 1] for k in range(4))
        right = jnp.where(col_at >= half, 1.0, 0.0)
        lat_taps[:, 0:size] = taps_of(line_lat[:, 0:size], row_at, lat_frac).astype(bf16).astype(f32)
        lon_taps[:, 0:size] = taps_of(line_lon[:, 0:size], col_at - right * half, lon_frac).astype(bf16)
        for v in range(size // 128):
            side = jnp.broadcast_to(right[:, v * 128 : (v + 1) * 128], (128, 128)).T.astype(bf16)
            rows = jnp.concatenate(
                [inbox[first + v * fold + t, 0:capacity, :] for t in range(fold)], axis=0
            )
            at = slice(v * 128, (v + 1) * 128)
            on_right = rows * side
            halves[at, 0:channels] = rows - on_right
            halves[at, channels : 2 * channels] = on_right

        def add(k, _):
            lhs = []
            for j in range(0, stride, 2):
                pair = [
                    jnp.broadcast_to(lat_taps[pl.ds(k * stride + j + n, 1), 0:size], (8, size))
                    for n in range(2)
                ]
                for t in range(0, 2 * wide, 16):
                    row = jnp.concatenate([pair[t // wide], pair[(t + 8) // wide]], axis=0)
                    lhs.append(row.astype(bf16) * lon_taps[t : t + 16, 0:size])
            out = jnp.dot(jnp.concatenate(lhs, axis=0), halves[0:size, :], preferred_element_type=f32)
            for j in range(stride):
                i = k * stride + j
                row = sums[i] + out[j * wide : (j + 1) * wide]
                if not last:
                    sums[i] = row
                    continue
                left, right = row[:, 0:channels], row[:, channels : 2 * channels]
                canvas[i, pad : pad + half, :] = left[0:half]
                canvas[i, pad + half : pad + wide, :] = left[half:wide] + right[0 : wide - half]
                canvas[i, pad + wide : pad + wide + half, :] = right[wide - half : wide]
            return 0

        lax.fori_loop(0, tall // stride, add, 0)

    slots = 2 * reach
    rows_at_once = 128 // slots
    last_chunk = tall // rows_at_once - 1

    def flank(chunks):
        for a in range(3):
            for k in chunks:
                at = slice(a + k * rows_at_once, a + (k + 1) * rows_at_once)
                both = jnp.concatenate(
                    [field[at, 0:reach], field[at, tile_lon - reach : tile_lon]], axis=1
                )
                beside[a * channels : (a + 1) * channels, k * 128 : (k + 1) * 128] = both.reshape(
                    128, channels
                ).T

    def border():
        for (copy, _, takes), (da, _) in zip(borders, ways):
            when(da, takes, copy.wait_recv)
        for p in (*range(up), *range(up + tile_lat, tall + 2)):
            turn(p)
        flank((0, last_chunk))

    arrival = [order[3], order[2], order[0], order[1]] if groups == 4 else order[::-1]
    for q in arrival[:-1]:
        collect(q * group, group, False)
    flank(range(1, last_chunk))
    for c in range(per):
        collect(arrival[-1] * group + ((c + lon) % per) * chunk, chunk, c == per - 1)

    inset = before - 1
    edge = pad + inset

    @pl.when(lat == 0)
    def _():
        canvas[0:before] = jnp.zeros((before,) + canvas.shape[1:], f32)

    @pl.when(lat == lat_total - 1)
    def _():
        canvas[before + tile_lat : tall] = jnp.zeros((tall - before - tile_lat,) + canvas.shape[1:], f32)

    some = math.gcd(tall, 4)

    def emit(k, _):
        for j in range(some):
            i = k * some + j
            strips[2][i] = canvas[i, pad : pad + up, :].astype(bf16)
            strips[3][i] = canvas[i, edge + cols - 2 : edge + cols - 2 + down, :].astype(bf16)
        return 0

    lax.fori_loop(0, tall // some, emit, 0)
    halos = []
    for w, (da, db) in enumerate(ways):
        copy = pltpu.make_async_remote_copy(
            src_ref=strips[w],
            dst_ref=landed[w],
            send_sem=halo_send.at[w],
            recv_sem=halo_recv.at[w],
            device_id=((lat + da + lat_total) % lat_total, (lon + db + lon_total) % lon_total),
            device_id_type=pl.DeviceIdType.MESH,
        )
        sends = (lat + da >= 0) & (lat + da < lat_total)
        takes = (lat - da >= 0) & (lat - da < lat_total)
        halos.append((copy, sends, takes))
    beside_halos = halos[2:4]
    for copy, _, _ in beside_halos:
        copy.start()
    spans = ((pad, up), (edge, cols), (edge + cols - 2, down))
    for count, first, refs in (
        (up, 0, (strips[4], strips[0], strips[5])),
        (down, inset + rows - 2, (strips[6], strips[1], strips[7])),
    ):
        for i in range(count):
            for (start, width), ref in zip(spans, refs):
                ref[i] = canvas[first + i, start : start + width, :].astype(bf16)
    for (copy, sends, _), (da, _) in zip(halos, ways):
        if da != 0:
            pl.when(sends)(copy.start)
    chips = devices // 2
    planes = lon_total // 2
    outer = planes // 4
    inner = planes - 2 * outer
    roots = lat_total * inner
    plane, core = lon // 2, lon % 2
    chip = lat * planes + plane
    other = 1 - core
    is_root = (plane >= outer) & (plane < planes - outer)
    root = lat * inner + plane - outer

    def seat(peer):
        return (peer // planes, (peer % planes) * 2 + core)

    def chip_of(r):
        return (r // inner) * planes + r % inner + outer

    def shift(i, _):
        at = pl.ds(pl.multiple_of(i * tile_lon, tile_lon), tile_lon)
        for b in range(3):
            windows[at, b * channels : (b + 1) * channels] = canvas[
                i, edge + 2 - b : edge + 2 - b + tile_lon, :
            ].astype(bf16)
        return 0

    lax.fori_loop(0, tall, shift, 0)

    def shift_edges(k, _):
        for j in range(some):
            i = k * some + j
            stage[i, 0:down] = landed[3][i].astype(f32)
            stage[i, 3 * reach : 3 * reach + up] = landed[2][i].astype(f32)
            at = pl.ds(pl.multiple_of(i * 2 * reach, 2 * reach), 2 * reach)
            for b in range(3):
                first, second = 2 - b, 2 * reach + up - b
                both = [stage[i, first : first + reach, :], stage[i, second : second + reach, :]]
                edges[at, b * channels : (b + 1) * channels] = jnp.concatenate(
                    both, axis=0
                ).astype(bf16)
        return 0

    step = next(n for n in (12, 8, 6, 4, 3, 2, 1) if tall % n == 0)
    depth = step * tile_lon

    def weigh(k, _):
        start = k * depth
        lhs = jnp.concatenate(
            [
                turned[:, aligned(start + a * tile_lon, depth)]
                for a in range(3)
            ],
            axis=0,
        )
        rhs = windows[aligned(start, depth), :]
        total[...] += jnp.dot(lhs, rhs, preferred_element_type=f32)
        return 0

    last_step = tall // step - 1
    lax.fori_loop(1, last_step, weigh, 0)
    border()
    weigh(0, 0)
    weigh(last_step, 0)
    for copy, _, _ in beside_halos:
        copy.wait_recv()
    lax.fori_loop(0, tall // some, shift_edges, 0)
    total[...] += jnp.dot(beside[...], edges[...], preferred_element_type=f32)
    for a in range(3):
        for b in range(3):
            at = (a * 3 + b) * channels
            flat[at : at + channels, :] = total[
                a * channels : (a + 1) * channels, b * channels : (b + 1) * channels
            ]
    share = pieces.shape[1]

    def cut(d, _):
        pieces[d] = flat[pl.ds(d * share, share), :].astype(bf16)
        return 0

    lax.fori_loop(0, 2 * roots, cut, 0)
    part = math.gcd(tile_lat // 2, 8)
    strides = tile_lat // 2 // part
    first = strides // 2

    def apply(k, _):
        lhs = jnp.concatenate(
            [
                jnp.concatenate(
                    [
                        windows[
                            pl.ds(
                                pl.multiple_of(
                                    (inset + 2 * (k * part + j) + r) * tile_lon, tile_lon
                                ),
                                tile_lon,
                            ),
                            :,
                        ]
                        for r in range(4)
                    ],
                    axis=1,
                )
                for j in range(part)
            ],
            axis=0,
        )
        acc = jnp.dot(lhs, mixer[...], preferred_element_type=f32).astype(bf16)
        for j in range(part):
            for r in range(2):
                ig_ref[2 * (k * part + j) + r] = acc[
                    j * tile_lon : (j + 1) * tile_lon, r * channels : (r + 1) * channels
                ]
        return 0

    def settle():
        for (copy, _, takes), (da, db), ref in zip(halos, ways, landed):

            def take(copy=copy, da=da, db=db, ref=ref):
                if da != 0:
                    copy.wait_recv()
                high = {-1: inset + rows - up, 0: 0, 1: inset}[da]
                count = {-1: up, 0: tall, 1: down}[da]
                left = {-1: cols - up, 0: 0, 1: 0}[db]
                width = {-1: up, 0: cols, 1: down}[db]

                def add(i, _):
                    canvas[high + i, edge + left : edge + left + width, :] += ref[i].astype(f32)
                    return 0

                lax.fori_loop(0, count, add, 0)

            when(da, takes, take)

        lax.fori_loop(inset, inset + rows, shift, 0)

    def paired(src, dst, n):
        return pltpu.make_async_remote_copy(
            src_ref=src,
            dst_ref=dst,
            send_sem=pair_send.at[n],
            recv_sem=pair_recv.at[n],
            device_id=(lat, plane * 2 + other),
            device_id_type=pl.DeviceIdType.MESH,
        )

    def scattered(r, slot):
        return pltpu.make_async_remote_copy(
            src_ref=pieces.at[core * roots + r],
            dst_ref=parts.at[slot],
            send_sem=part_send.at[r],
            recv_sem=part_recv.at[slot],
            device_id=seat(chip_of(r)),
            device_id_type=pl.DeviceIdType.MESH,
        )

    def shared(peer, r):
        return pltpu.make_async_remote_copy(
            src_ref=mine,
            dst_ref=gathered.at[core * roots + r],
            send_sem=all_send.at[peer],
            recv_sem=all_recv.at[r],
            device_id=seat(peer),
            device_id_type=pl.DeviceIdType.MESH,
        )

    def each_root(fn):
        def body(k, _):
            r = (chip + k) % roots

            @pl.when(chip_of(r) != chip)
            def _():
                fn(r)

            return 0

        lax.fori_loop(0, roots, body, 0)

    def each_chip(fn):
        def body(k, _):
            fn((chip + k) % chips)
            return 0

        lax.fori_loop(1, chips, body, 0)

    swap = paired(pieces.at[pl.ds(other * roots, roots)], twin, 0)
    swap.start()
    swap.wait_recv()

    def merge(p, _):
        at = core * roots + p
        pieces[at] = (flat[pl.ds(at * share, share), :] + twin[p].astype(f32)).astype(bf16)
        return 0

    lax.fori_loop(0, roots, merge, 0)
    each_root(lambda r: scattered(r, chip).start())
    settle()
    lax.fori_loop(0, first, apply, 0)

    @pl.when(is_root)
    def _():
        parts[chip] = pieces[core * roots + root]
        each_chip(lambda peer: scattered(root, peer).wait_recv())

        def gather_sum(p, acc):
            return acc + parts[p].astype(f32)

        mine[...] = lax.fori_loop(
            0, chips, gather_sum, jnp.zeros((share, channels), f32)
        ).astype(bf16)
        each_chip(lambda peer: shared(peer, root).start())
        gathered[core * roots + root] = mine[...]

    lax.fori_loop(first, strides, apply, 0)
    each_root(lambda r: shared(chip, r).wait_recv())
    kept = gathered.at[pl.ds(core * roots, roots)]
    back = paired(kept, kept, 1)
    back.start()
    back.wait_recv()
    for (copy, sends, _), (da, _) in zip(halos + borders, ways + ways[:2]):
        when(da, sends, copy.wait_send)
    swap.wait_send()
    back.wait_send()
    each_root(lambda r: scattered(r, chip).wait_send())

    @pl.when(is_root)
    def _():
        each_chip(lambda peer: shared(peer, root).wait_send())


    def each(fn):
        def body(k, _):
            fn((me + k) % devices)
            return 0

        lax.fori_loop(1, devices, body, 0)

    each(lambda peer: copy_to(peer, me).wait_send())


def finish_kernel(grad_ref, shares_ref, grad_out, weight_out, flat, sem):
    grad_copy = pltpu.make_async_copy(grad_ref, grad_out, sem.at[0])
    grad_copy.start()
    share = shares_ref.shape[1]
    for d in range(shares_ref.shape[0]):
        flat[d * share : (d + 1) * share, :] = shares_ref[d].astype(f32)
    weight_copy = pltpu.make_async_copy(flat, weight_out, sem.at[1])
    weight_copy.start()
    grad_copy.wait()
    weight_copy.wait()


def shards(grad_rows, owner, lat_offset, lon_offset, position, live_count, features, conv_weight):
    lat_total = lax.axis_size("lat")
    lon_total = lax.axis_size("lon")
    device_total = lat_total * lon_total
    row_total, channels = grad_rows.shape
    tile_lat, tile_lon = features.shape[:2]
    capacity = max(2, 2 * row_total // device_total)
    smem = pl.BlockSpec(memory_space=pltpu.SMEM)
    vmem = pl.BlockSpec(memory_space=pltpu.VMEM)

    rows, cols = tile_lat + 2, tile_lon + 2
    tall = -(-(tile_lat + taps - 1) // 8) * 8
    wide = tile_lon // 2 + 8
    span = math.gcd(device_total, max(1, 512 // capacity)) * capacity
    up, down = before + 1, after + 1
    strip_shapes = [
        (up, cols),
        (down, cols),
        (tall, up),
        (tall, down),
        (up, up),
        (up, down),
        (down, up),
        (down, down),
    ]
    message = (device_total, capacity + geom_rows, channels)
    flat_rows = 9 * channels
    chips = device_total // 2
    roots = lat_total * (lon_total // 2 - 2 * (lon_total // 8))
    share = flat_rows // (2 * roots)
    dma = pltpu.SemaphoreType.DMA
    places = [pltpu.VMEM(shape + (channels,), bf16) for shape in strip_shapes]
    operands = (
        grad_rows,
        owner.reshape(1, row_total),
        lat_offset.reshape(1, row_total),
        lon_offset.reshape(1, row_total),
        position.T,
        features,
        conv_weight,
    )
    inner_grad, shares = pl.pallas_call(
        functools.partial(solve_kernel, capacity, lat_total, lon_total),
        out_shape=[
            jax.ShapeDtypeStruct((tile_lat, tile_lon, channels), bf16),
            jax.ShapeDtypeStruct((2 * roots, share, channels), bf16),
        ],
        in_specs=[smem] + [pl.BlockSpec(memory_space=pltpu.HBM)] * 7,
        out_specs=[vmem] * 2,
        scratch_shapes=[pltpu.VMEM(x.shape, x.dtype) for x in operands if x is not features]
        + [
            pltpu.VMEM((tall + 2, tile_lon, channels), bf16),
            pltpu.VMEM((tall, 32, channels), f32),
            pltpu.VMEM((3 * channels, tall * 16), bf16),
            pltpu.VMEM((tall * 16, 3 * channels), bf16),
            pltpu.VMEM(message, bf16),
            pltpu.VMEM(message, bf16),
            pltpu.VMEM((tall, wide, 2 * channels), f32),
            pltpu.VMEM((tall, wide + tile_lon // 2 + 16, channels), f32),
            pltpu.VMEM((tall, span), f32),
            pltpu.VMEM((2 * wide, span), bf16),
            pltpu.VMEM((span, 2 * channels), bf16),
        ]
        + places
        + places
        + [
            pltpu.VMEM((tall * tile_lon, 3 * channels), bf16),
            pltpu.VMEM((channels, (tall + 2) * tile_lon), bf16),
            pltpu.VMEM((3 * channels, 3 * channels), f32),
            pltpu.VMEM((flat_rows, channels), f32),
            pltpu.VMEM((4 * 3 * channels, 2 * channels), bf16),
            pltpu.VMEM((2 * roots, share, channels), bf16),
            pltpu.VMEM((roots, share, channels), bf16),
            pltpu.VMEM((chips, share, channels), bf16),
            pltpu.VMEM((share, channels), bf16),
            dma((7,)),
            dma((device_total,)),
            dma((device_total,)),
            dma((2,)),
            dma((2,)),
            dma((8,)),
            dma((8,)),
            dma((2,)),
            dma((2,)),
            dma((roots,)),
            dma((chips,)),
            dma((chips,)),
            dma((roots,)),
        ],
        compiler_params=pltpu.CompilerParams(
            vmem_limit_bytes=44 * 2**20, collective_id=0, has_side_effects=True
        ),
        name="solve",
    )(live_count, *[pltpu.with_memory_space_constraint(x, pltpu.HBM) for x in operands])
    input_grad, weight_grad = pl.pallas_call(
        finish_kernel,
        out_shape=[
            jax.ShapeDtypeStruct((tile_lat, tile_lon, channels), bf16),
            jax.ShapeDtypeStruct((flat_rows, channels), f32),
        ],
        in_specs=[vmem] * 2,
        out_specs=[pl.BlockSpec(memory_space=pltpu.HBM)] * 2,
        scratch_shapes=[pltpu.VMEM((flat_rows, channels), f32), dma((2,))],
        compiler_params=pltpu.CompilerParams(vmem_limit_bytes=8 * 2**20),
        name="finish",
    )(inner_grad, shares)
    return input_grad, weight_grad.reshape(3, 3, channels, channels)


def solution(mesh):
    placed = (
        P(("lat", "lon"), None),
        P(("lat", "lon"), None),
        P(("lat", "lon")),
        P(("lat", "lon")),
        P(("lat", "lon"), None),
        P(("lat", "lon")),
        P("lat", "lon", None),
        P(),
    )
    return jax.shard_map(
        shards, mesh=mesh, in_specs=placed, out_specs=(P("lat", "lon", None), P()), check_vma=False
    )
```

```python
import functools
import math

import jax
import jax.numpy as jnp
from jax import lax
from jax.experimental import pallas as pl
from jax.experimental.pallas import tpu as pltpu
from jax.sharding import PartitionSpec as P

rbf_scale = 1.5
taps = 8
before = 3
after = taps - 1 - before
geom_rows = 8
f32 = jnp.float32
bf16 = jnp.bfloat16


def solve_kernel(
    capacity,
    lat_total,
    lon_total,
    live_ref,
    rows_hbm,
    owner_hbm,
    lat_hbm,
    lon_hbm,
    pos_hbm,
    feat_hbm,
    weight_hbm,
    ig_ref,
    gathered,
    *refs,
):
    (rows_ref, owner_ref, lat_ref, lon_ref, pos_ref, weight_ref) = refs[:6]
    (field, stage, beside, edges) = refs[6:10]
    (held, inbox, sums, canvas, lat_taps, lon_taps, halves) = refs[10:17]
    strips, landed = refs[17:25], refs[25:33]
    (windows, turned, total, flat, mixer, pieces, twin, parts, mine) = refs[33:42]
    (load_sem, send_sem, recv_sem, field_send, field_recv) = refs[42:47]
    halo_send, halo_recv, pair_send, pair_recv, part_send, part_recv, all_send, all_recv = refs[47:]
    devices = inbox.shape[0]
    row_total, channels = rows_ref.shape
    tile_lat, tile_lon = ig_ref.shape[:2]
    up, down = before + 1, after + 1
    tall = canvas.shape[0]
    own_field = field.at[up : up + tile_lat]
    lat, lon = lax.axis_index("lat"), lax.axis_index("lon")
    me = lon * lat_total + lat
    span = halves.shape[0]
    group = span // capacity
    groups = devices // group
    ours = me // group
    half = tile_lon // 2
    inv = 1.0 / (2.0 * rbf_scale * rbf_scale)

    def place(peer):
        return (peer % lat_total, peer // lat_total)

    barrier = pltpu.get_barrier_semaphore()

    def greet(k, _):
        pl.semaphore_signal(
            barrier, inc=1, device_id=place((me + k) % devices), device_id_type=pl.DeviceIdType.MESH
        )
        return 0

    loads = [
        pltpu.make_async_copy(src, dst, load_sem.at[k])
        for k, (src, dst) in enumerate(
            zip(
                (rows_hbm, owner_hbm, lat_hbm, lon_hbm, pos_hbm, feat_hbm, weight_hbm),
                (rows_ref, owner_ref, lat_ref, lon_ref, pos_ref, own_field, weight_ref),
            )
        )
    ]
    for load in loads:
        load.start()
    lax.fori_loop(1, devices, greet, 0)
    sums[...] = jnp.zeros_like(sums)
    mixer[...] = jnp.zeros_like(mixer)
    total[...] = jnp.zeros_like(total)
    rows, cols = tile_lat + 2, tile_lon + 2
    stage[...] = jnp.zeros_like(stage)
    for margin in (slice(0, 8), slice(canvas.shape[1] - 8, canvas.shape[1])):
        canvas[:, margin, :] = jnp.zeros((tall, 8, channels), f32)
    field[tall + 1] = jnp.zeros(field.shape[1:], bf16)

    @pl.when(lat == 0)
    def _():
        field[0:up] = jnp.zeros((up,) + field.shape[1:], bf16)

    @pl.when(lat == lat_total - 1)
    def _():
        field[up + tile_lat : tall + 1] = jnp.zeros((down,) + field.shape[1:], bf16)

    for load in loads[:5]:
        load.wait()

    live = lax.broadcasted_iota(jnp.int32, (1, row_total), 1) < live_ref[0]
    tile = owner_ref[...].astype(f32)
    tile_row = jnp.floor((tile + 0.5) * (1.0 / lon_total))
    owner = (tile - tile_row * lon_total) * lat_total + tile_row
    owner = jnp.where(live, owner, float(devices)).astype(jnp.int32)
    match = lax.broadcasted_iota(jnp.int32, (devices, row_total), 0) == owner
    match = jnp.where(match, 1.0, 0.0)
    blocks = row_total // 128
    upper = lax.broadcasted_iota(jnp.int32, (128, 128), 0) < lax.broadcasted_iota(
        jnp.int32, (128, 128), 1
    )
    upper = jnp.where(upper, 1.0, 0.0).astype(bf16)
    columns = [match[:, k * 128 : (k + 1) * 128] for k in range(blocks)]
    earlier = jnp.dot(
        jnp.concatenate(columns, axis=0).astype(bf16), upper, preferred_element_type=f32
    )
    before_block = jnp.zeros((devices, 1), f32)
    ranks = []
    for k, part in enumerate(columns):
        ahead = earlier[k * devices : (k + 1) * devices] + before_block
        ranks.append(jnp.sum(ahead * part, axis=0, keepdims=True))
        before_block = before_block + jnp.sum(part, axis=1, keepdims=True)
    rank = jnp.concatenate(ranks, axis=1).astype(jnp.int32)
    slot = owner * capacity + rank
    geometry = jnp.concatenate(
        [
            pos_ref[...].astype(f32),
            lat_ref[...].astype(f32),
            lon_ref[...].astype(f32),
            jnp.zeros((geom_rows - 4, row_total), f32),
        ],
        axis=0,
    ).astype(bf16)
    fold = 128 // capacity
    chunk = math.gcd(group, max(1, 256 // capacity))
    line = lax.broadcasted_iota(jnp.int32, (chunk * capacity, row_total), 0)
    lane_block = lax.broadcasted_iota(jnp.int32, (geom_rows, 128), 1) // capacity

    def build(first):
        hit = jnp.where(line == slot - first * capacity, 1.0, 0.0).astype(bf16)
        placed = jnp.dot(hit, rows_ref[...], preferred_element_type=f32).astype(bf16)
        info = lax.dot_general(
            geometry, hit, (((1,), (1,)), ((), ())), preferred_element_type=f32
        )
        for i in range(chunk):
            held[first + i, 0:capacity, :] = placed[i * capacity : (i + 1) * capacity]
        for v in range(chunk // fold):
            piece = info[:, v * 128 : (v + 1) * 128]
            rolled = [piece] + [pltpu.roll(piece, s * capacity, 1) for s in range(1, fold)]
            for i in range(fold):
                tiled = rolled[(fold - i) % fold]
                for t in range(1, fold):
                    tiled = jnp.where(lane_block == t, rolled[(t - i) % fold], tiled)
                held[first + v * fold + i, capacity : capacity + geom_rows, :] = tiled.astype(bf16)

    def copy_to(peer, slot_at):
        return pltpu.make_async_remote_copy(
            src_ref=held.at[peer],
            dst_ref=inbox.at[slot_at],
            send_sem=send_sem.at[peer],
            recv_sem=recv_sem.at[slot_at],
            device_id=place(peer),
            device_id_type=pl.DeviceIdType.MESH,
        )

    def send(first):
        for i in range(chunk):
            peer = first + i

            @pl.when(peer != me)
            def _():
                copy_to(peer, me).start()

    if groups == 4:
        order = [(ours + 2) % 4, 3 - ours, ours + 1 - 2 * (ours % 2), ours]
    else:
        order = [(ours + groups // 2 + k) % groups for k in range(groups)]
    per = group // chunk
    steps = [(q, c) for q in order for c in range(per)]
    first_of = [q * group + c * chunk for q, c in steps]
    early = len(first_of) // 2
    for first in first_of[:early]:
        build(first)
    pl.semaphore_wait(barrier, devices - 1)
    for first in first_of[:early]:
        send(first)
    for first in first_of[early:]:
        build(first)
        send(first)
    inbox[me] = held[me]

    loads[5].wait()

    def when(da, cond, fn):
        if da == 0:
            fn()
        else:
            pl.when(cond)(fn)

    ways = ((-1, 0), (1, 0), (0, -1), (0, 1), (-1, -1), (-1, 1), (1, -1), (1, 1))
    reach = 8
    borders = []
    for w, (da, source, target) in enumerate(
        (
            (-1, slice(up, up + down), slice(up + tile_lat, tall + 1)),
            (1, slice(tile_lat, up + tile_lat), slice(0, up)),
        )
    ):
        copy = pltpu.make_async_remote_copy(
            src_ref=field.at[source],
            dst_ref=field.at[target],
            send_sem=field_send.at[w],
            recv_sem=field_recv.at[w],
            device_id=((lat + da + lat_total) % lat_total, lon),
            device_id_type=pl.DeviceIdType.MESH,
        )
        sends = (lat + da >= 0) & (lat + da < lat_total)
        takes = (lat - da >= 0) & (lat - da < lat_total)
        borders.append((copy, sends, takes))
    for (copy, sends, _), (da, _) in zip(borders, ways):
        when(da, sends, copy.start)

    def aligned(start, size):
        if not isinstance(start, int):
            start = pl.multiple_of(start, tile_lon)
        return pl.ds(start, size)

    def turn(p):
        turned[:, aligned(p * tile_lon, tile_lon)] = field[p].T

    fast = math.gcd(tile_lat, 8)

    def turn_some(k, _):
        for j in range(fast):
            turn(up + k * fast + j)
        return 0

    lax.fori_loop(0, tile_lat // fast, turn_some, 0)
    loads[6].wait()
    for a in range(3):
        for b in range(3):
            tap = weight_ref[a, b].T
            for r in range(2):
                at = ((r + 2 - a) * 3 + b) * channels
                mixer[at : at + channels, r * channels : (r + 1) * channels] = tap

    line_lat = lax.broadcasted_iota(jnp.int32, (lat_taps.shape[0], span), 0).astype(f32)
    line_lon = lax.broadcasted_iota(jnp.int32, (lon_taps.shape[0], span), 0).astype(f32)
    lanes = lax.broadcasted_iota(jnp.int32, (8, 128), 1) // capacity
    wide = sums.shape[1]
    line_lon = jnp.where(line_lon >= wide, line_lon - wide, line_lon)
    stride = next(n for n in (36, 24, 12, 8, 4, 2) if tall % n == 0)

    def taps_of(line, base, frac):
        tap = line - base
        d = tap - (frac + before)
        weight = jnp.exp(-(d * d) * inv)
        return jnp.where((tap >= 0.0) & (tap <= taps - 1.0), weight, 0.0)

    pad = reach

    def collect(q, last):
        for i in range(group):
            peer = q * group + i

            @pl.when(peer != me)
            def _():
                copy_to(peer, peer).wait_recv()

        first = q * group
        infos = []
        for v in range(span // 128):
            at = first + v * fold
            info = inbox[at, capacity : capacity + geom_rows, :].astype(f32)
            for t in range(1, fold):
                info = jnp.where(
                    lanes == t, inbox[at + t, capacity : capacity + geom_rows, :].astype(f32), info
                )
            infos.append(info)
        info = jnp.concatenate(infos, axis=1)
        lat_frac, lon_frac, row_at, col_at = (info[k : k + 1] for k in range(4))
        right = jnp.where(col_at >= half, 1.0, 0.0)
        lat_taps[...] = taps_of(line_lat, row_at, lat_frac).astype(bf16).astype(f32)
        lon_taps[...] = taps_of(line_lon, col_at - right * half, lon_frac).astype(bf16)
        for v in range(span // 128):
            side = jnp.broadcast_to(right[:, v * 128 : (v + 1) * 128], (128, 128)).T.astype(bf16)
            rows = jnp.concatenate(
                [inbox[first + v * fold + t, 0:capacity, :] for t in range(fold)], axis=0
            )
            at = slice(v * 128, (v + 1) * 128)
            on_right = rows * side
            halves[at, 0:channels] = rows - on_right
            halves[at, channels : 2 * channels] = on_right

        def add(k, _):
            lhs = []
            for j in range(0, stride, 2):
                pair = [
                    jnp.broadcast_to(lat_taps[pl.ds(k * stride + j + n, 1), :], (8, span))
                    for n in range(2)
                ]
                for t in range(0, 2 * wide, 16):
                    row = jnp.concatenate([pair[t // wide], pair[(t + 8) // wide]], axis=0)
                    lhs.append(row.astype(bf16) * lon_taps[t : t + 16, :])
            out = jnp.dot(jnp.concatenate(lhs, axis=0), halves[...], preferred_element_type=f32)
            for j in range(stride):
                i = k * stride + j
                row = sums[i] + out[j * wide : (j + 1) * wide]
                if not last:
                    sums[i] = row
                    continue
                left, right = row[:, 0:channels], row[:, channels : 2 * channels]
                canvas[i, pad : pad + half, :] = left[0:half]
                canvas[i, pad + half : pad + wide, :] = left[half:wide] + right[0 : wide - half]
                canvas[i, pad + wide : pad + wide + half, :] = right[wide - half : wide]
            return 0

        lax.fori_loop(0, tall // stride, add, 0)

    slots = 2 * reach
    rows_at_once = 128 // slots
    last_chunk = tall // rows_at_once - 1

    def flank(chunks):
        for a in range(3):
            for k in chunks:
                at = slice(a + k * rows_at_once, a + (k + 1) * rows_at_once)
                both = jnp.concatenate(
                    [field[at, 0:reach], field[at, tile_lon - reach : tile_lon]], axis=1
                )
                beside[a * channels : (a + 1) * channels, k * 128 : (k + 1) * 128] = both.reshape(
                    128, channels
                ).T

    def border():
        for (copy, _, takes), (da, _) in zip(borders, ways):
            when(da, takes, copy.wait_recv)
        for p in (*range(up), *range(up + tile_lat, tall + 2)):
            turn(p)
        flank((0, last_chunk))

    for k, q in enumerate([order[3], order[2], order[0], order[1]] if groups == 4 else order[::-1]):
        if k == groups - 1:
            flank(range(1, last_chunk))
        collect(q, k == groups - 1)

    inset = before - 1
    edge = pad + inset

    @pl.when(lat == 0)
    def _():
        canvas[0:before] = jnp.zeros((before,) + canvas.shape[1:], f32)

    @pl.when(lat == lat_total - 1)
    def _():
        canvas[before + tile_lat : tall] = jnp.zeros((tall - before - tile_lat,) + canvas.shape[1:], f32)

    some = math.gcd(tall, 4)

    def emit(k, _):
        for j in range(some):
            i = k * some + j
            strips[2][i] = canvas[i, pad : pad + up, :].astype(bf16)
            strips[3][i] = canvas[i, edge + cols - 2 : edge + cols - 2 + down, :].astype(bf16)
        return 0

    lax.fori_loop(0, tall // some, emit, 0)
    halos = []
    for w, (da, db) in enumerate(ways):
        copy = pltpu.make_async_remote_copy(
            src_ref=strips[w],
            dst_ref=landed[w],
            send_sem=halo_send.at[w],
            recv_sem=halo_recv.at[w],
            device_id=((lat + da + lat_total) % lat_total, (lon + db + lon_total) % lon_total),
            device_id_type=pl.DeviceIdType.MESH,
        )
        sends = (lat + da >= 0) & (lat + da < lat_total)
        takes = (lat - da >= 0) & (lat - da < lat_total)
        halos.append((copy, sends, takes))
    beside_halos = halos[2:4]
    for copy, _, _ in beside_halos:
        copy.start()
    spans = ((pad, up), (edge, cols), (edge + cols - 2, down))
    for count, first, refs in (
        (up, 0, (strips[4], strips[0], strips[5])),
        (down, inset + rows - 2, (strips[6], strips[1], strips[7])),
    ):
        for i in range(count):
            for (start, width), ref in zip(spans, refs):
                ref[i] = canvas[first + i, start : start + width, :].astype(bf16)
    for (copy, sends, _), (da, _) in zip(halos, ways):
        if da != 0:
            pl.when(sends)(copy.start)
    chips = devices // 2
    planes = lon_total // 2
    outer = planes // 4
    inner = planes - 2 * outer
    roots = lat_total * inner
    plane, core = lon // 2, lon % 2
    chip = lat * planes + plane
    other = 1 - core
    is_root = (plane >= outer) & (plane < planes - outer)
    root = lat * inner + plane - outer

    def seat(peer):
        return (peer // planes, (peer % planes) * 2 + core)

    def chip_of(r):
        return (r // inner) * planes + r % inner + outer

    def shift(i, _):
        at = pl.ds(pl.multiple_of(i * tile_lon, tile_lon), tile_lon)
        for b in range(3):
            windows[at, b * channels : (b + 1) * channels] = canvas[
                i, edge + 2 - b : edge + 2 - b + tile_lon, :
            ].astype(bf16)
        return 0

    lax.fori_loop(0, tall, shift, 0)

    def shift_edges(k, _):
        for j in range(some):
            i = k * some + j
            stage[i, 0:down] = landed[3][i].astype(f32)
            stage[i, 3 * reach : 3 * reach + up] = landed[2][i].astype(f32)
            at = pl.ds(pl.multiple_of(i * 2 * reach, 2 * reach), 2 * reach)
            for b in range(3):
                first, second = 2 - b, 2 * reach + up - b
                both = [stage[i, first : first + reach, :], stage[i, second : second + reach, :]]
                edges[at, b * channels : (b + 1) * channels] = jnp.concatenate(
                    both, axis=0
                ).astype(bf16)
        return 0

    step = next(n for n in (12, 8, 6, 4, 3, 2, 1) if tall % n == 0)
    depth = step * tile_lon

    def weigh(k, _):
        start = k * depth
        lhs = jnp.concatenate(
            [
                turned[:, aligned(start + a * tile_lon, depth)]
                for a in range(3)
            ],
            axis=0,
        )
        rhs = windows[aligned(start, depth), :]
        total[...] += jnp.dot(lhs, rhs, preferred_element_type=f32)
        return 0

    last_step = tall // step - 1
    lax.fori_loop(1, last_step, weigh, 0)
    border()
    weigh(0, 0)
    weigh(last_step, 0)
    for copy, _, _ in beside_halos:
        copy.wait_recv()
    lax.fori_loop(0, tall // some, shift_edges, 0)
    total[...] += jnp.dot(beside[...], edges[...], preferred_element_type=f32)
    for a in range(3):
        for b in range(3):
            at = (a * 3 + b) * channels
            flat[at : at + channels, :] = total[
                a * channels : (a + 1) * channels, b * channels : (b + 1) * channels
            ]
    share = pieces.shape[1]

    def cut(d, _):
        pieces[d] = flat[pl.ds(d * share, share), :].astype(bf16)
        return 0

    lax.fori_loop(0, 2 * roots, cut, 0)
    part = math.gcd(tile_lat // 2, 8)
    strides = tile_lat // 2 // part
    first = strides // 4

    def apply(k, _):
        lhs = jnp.concatenate(
            [
                jnp.concatenate(
                    [
                        windows[
                            pl.ds(
                                pl.multiple_of(
                                    (inset + 2 * (k * part + j) + r) * tile_lon, tile_lon
                                ),
                                tile_lon,
                            ),
                            :,
                        ]
                        for r in range(4)
                    ],
                    axis=1,
                )
                for j in range(part)
            ],
            axis=0,
        )
        acc = jnp.dot(lhs, mixer[...], preferred_element_type=f32).astype(bf16)
        for j in range(part):
            for r in range(2):
                ig_ref[2 * (k * part + j) + r] = acc[
                    j * tile_lon : (j + 1) * tile_lon, r * channels : (r + 1) * channels
                ]
        return 0

    def settle():
        for (copy, _, takes), (da, db), ref in zip(halos, ways, landed):

            def take(copy=copy, da=da, db=db, ref=ref):
                if da != 0:
                    copy.wait_recv()
                high = {-1: inset + rows - up, 0: 0, 1: inset}[da]
                count = {-1: up, 0: tall, 1: down}[da]
                left = {-1: cols - up, 0: 0, 1: 0}[db]
                width = {-1: up, 0: cols, 1: down}[db]

                def add(i, _):
                    canvas[high + i, edge + left : edge + left + width, :] += ref[i].astype(f32)
                    return 0

                lax.fori_loop(0, count, add, 0)

            when(da, takes, take)

        lax.fori_loop(inset, inset + rows, shift, 0)

    def paired(src, dst, n):
        return pltpu.make_async_remote_copy(
            src_ref=src,
            dst_ref=dst,
            send_sem=pair_send.at[n],
            recv_sem=pair_recv.at[n],
            device_id=(lat, plane * 2 + other),
            device_id_type=pl.DeviceIdType.MESH,
        )

    def scattered(r, slot):
        return pltpu.make_async_remote_copy(
            src_ref=pieces.at[core * roots + r],
            dst_ref=parts.at[slot],
            send_sem=part_send.at[r],
            recv_sem=part_recv.at[slot],
            device_id=seat(chip_of(r)),
            device_id_type=pl.DeviceIdType.MESH,
        )

    def shared(peer, r):
        return pltpu.make_async_remote_copy(
            src_ref=mine,
            dst_ref=gathered.at[core * roots + r],
            send_sem=all_send.at[peer],
            recv_sem=all_recv.at[r],
            device_id=seat(peer),
            device_id_type=pl.DeviceIdType.MESH,
        )

    def each_root(fn):
        def body(k, _):
            r = (chip + k) % roots

            @pl.when(chip_of(r) != chip)
            def _():
                fn(r)

            return 0

        lax.fori_loop(0, roots, body, 0)

    def each_chip(fn):
        def body(k, _):
            fn((chip + k) % chips)
            return 0

        lax.fori_loop(1, chips, body, 0)

    swap = paired(pieces.at[pl.ds(other * roots, roots)], twin, 0)
    swap.start()
    swap.wait_recv()

    def merge(p, _):
        at = core * roots + p
        pieces[at] = (flat[pl.ds(at * share, share), :] + twin[p].astype(f32)).astype(bf16)
        return 0

    lax.fori_loop(0, roots, merge, 0)
    each_root(lambda r: scattered(r, chip).start())
    settle()
    lax.fori_loop(0, first, apply, 0)

    @pl.when(is_root)
    def _():
        parts[chip] = pieces[core * roots + root]
        each_chip(lambda peer: scattered(root, peer).wait_recv())

        def gather_sum(p, acc):
            return acc + parts[p].astype(f32)

        mine[...] = lax.fori_loop(
            0, chips, gather_sum, jnp.zeros((share, channels), f32)
        ).astype(bf16)
        each_chip(lambda peer: shared(peer, root).start())
        gathered[core * roots + root] = mine[...]

    lax.fori_loop(first, strides, apply, 0)
    each_root(lambda r: shared(chip, r).wait_recv())
    kept = gathered.at[pl.ds(core * roots, roots)]
    back = paired(kept, kept, 1)
    back.start()
    back.wait_recv()
    for (copy, sends, _), (da, _) in zip(halos + borders, ways + ways[:2]):
        when(da, sends, copy.wait_send)
    swap.wait_send()
    back.wait_send()
    each_root(lambda r: scattered(r, chip).wait_send())

    @pl.when(is_root)
    def _():
        each_chip(lambda peer: shared(peer, root).wait_send())


    def each(fn):
        def body(k, _):
            fn((me + k) % devices)
            return 0

        lax.fori_loop(1, devices, body, 0)

    each(lambda peer: copy_to(peer, me).wait_send())


def finish_kernel(grad_ref, shares_ref, grad_out, weight_out, flat, sem):
    grad_copy = pltpu.make_async_copy(grad_ref, grad_out, sem.at[0])
    grad_copy.start()
    share = shares_ref.shape[1]
    for d in range(shares_ref.shape[0]):
        flat[d * share : (d + 1) * share, :] = shares_ref[d].astype(f32)
    weight_copy = pltpu.make_async_copy(flat, weight_out, sem.at[1])
    weight_copy.start()
    grad_copy.wait()
    weight_copy.wait()


def shards(grad_rows, owner, lat_offset, lon_offset, position, live_count, features, conv_weight):
    lat_total = lax.axis_size("lat")
    lon_total = lax.axis_size("lon")
    device_total = lat_total * lon_total
    row_total, channels = grad_rows.shape
    tile_lat, tile_lon = features.shape[:2]
    capacity = max(2, 2 * row_total // device_total)
    smem = pl.BlockSpec(memory_space=pltpu.SMEM)
    vmem = pl.BlockSpec(memory_space=pltpu.VMEM)

    rows, cols = tile_lat + 2, tile_lon + 2
    tall = -(-(tile_lat + taps - 1) // 8) * 8
    wide = tile_lon // 2 + 8
    span = math.gcd(device_total, max(1, 512 // capacity)) * capacity
    up, down = before + 1, after + 1
    strip_shapes = [
        (up, cols),
        (down, cols),
        (tall, up),
        (tall, down),
        (up, up),
        (up, down),
        (down, up),
        (down, down),
    ]
    message = (device_total, capacity + geom_rows, channels)
    flat_rows = 9 * channels
    chips = device_total // 2
    roots = lat_total * (lon_total // 2 - 2 * (lon_total // 8))
    share = flat_rows // (2 * roots)
    dma = pltpu.SemaphoreType.DMA
    places = [pltpu.VMEM(shape + (channels,), bf16) for shape in strip_shapes]
    operands = (
        grad_rows,
        owner.reshape(1, row_total),
        lat_offset.reshape(1, row_total),
        lon_offset.reshape(1, row_total),
        position.T,
        features,
        conv_weight,
    )
    inner_grad, shares = pl.pallas_call(
        functools.partial(solve_kernel, capacity, lat_total, lon_total),
        out_shape=[
            jax.ShapeDtypeStruct((tile_lat, tile_lon, channels), bf16),
            jax.ShapeDtypeStruct((2 * roots, share, channels), bf16),
        ],
        in_specs=[smem] + [pl.BlockSpec(memory_space=pltpu.HBM)] * 7,
        out_specs=[vmem] * 2,
        scratch_shapes=[pltpu.VMEM(x.shape, x.dtype) for x in operands if x is not features]
        + [
            pltpu.VMEM((tall + 2, tile_lon, channels), bf16),
            pltpu.VMEM((tall, 32, channels), f32),
            pltpu.VMEM((3 * channels, tall * 16), bf16),
            pltpu.VMEM((tall * 16, 3 * channels), bf16),
            pltpu.VMEM(message, bf16),
            pltpu.VMEM(message, bf16),
            pltpu.VMEM((tall, wide, 2 * channels), f32),
            pltpu.VMEM((tall, wide + tile_lon // 2 + 16, channels), f32),
            pltpu.VMEM((tall, span), f32),
            pltpu.VMEM((2 * wide, span), bf16),
            pltpu.VMEM((span, 2 * channels), bf16),
        ]
        + places
        + places
        + [
            pltpu.VMEM((tall * tile_lon, 3 * channels), bf16),
            pltpu.VMEM((channels, (tall + 2) * tile_lon), bf16),
            pltpu.VMEM((3 * channels, 3 * channels), f32),
            pltpu.VMEM((flat_rows, channels), f32),
            pltpu.VMEM((4 * 3 * channels, 2 * channels), bf16),
            pltpu.VMEM((2 * roots, share, channels), bf16),
            pltpu.VMEM((roots, share, channels), bf16),
            pltpu.VMEM((chips, share, channels), bf16),
            pltpu.VMEM((share, channels), bf16),
            dma((7,)),
            dma((device_total,)),
            dma((device_total,)),
            dma((2,)),
            dma((2,)),
            dma((8,)),
            dma((8,)),
            dma((2,)),
            dma((2,)),
            dma((roots,)),
            dma((chips,)),
            dma((chips,)),
            dma((roots,)),
        ],
        compiler_params=pltpu.CompilerParams(
            vmem_limit_bytes=44 * 2**20, collective_id=0, has_side_effects=True
        ),
        name="solve",
    )(live_count, *[pltpu.with_memory_space_constraint(x, pltpu.HBM) for x in operands])
    input_grad, weight_grad = pl.pallas_call(
        finish_kernel,
        out_shape=[
            jax.ShapeDtypeStruct((tile_lat, tile_lon, channels), bf16),
            jax.ShapeDtypeStruct((flat_rows, channels), f32),
        ],
        in_specs=[vmem] * 2,
        out_specs=[pl.BlockSpec(memory_space=pltpu.HBM)] * 2,
        scratch_shapes=[pltpu.VMEM((flat_rows, channels), f32), dma((2,))],
        compiler_params=pltpu.CompilerParams(vmem_limit_bytes=8 * 2**20),
        name="finish",
    )(inner_grad, shares)
    return input_grad, weight_grad.reshape(3, 3, channels, channels)


def solution(mesh):
    placed = (
        P(("lat", "lon"), None),
        P(("lat", "lon"), None),
        P(("lat", "lon")),
        P(("lat", "lon")),
        P(("lat", "lon"), None),
        P(("lat", "lon")),
        P("lat", "lon", None),
        P(),
    )
    return jax.shard_map(
        shards, mesh=mesh, in_specs=placed, out_specs=(P("lat", "lon", None), P()), check_vma=False
    )
```

```python
import functools
import math

import jax
import jax.numpy as jnp
from jax import lax
from jax.experimental import pallas as pl
from jax.experimental.pallas import tpu as pltpu
from jax.sharding import PartitionSpec as P

rbf_scale = 1.5
taps = 8
before = 3
after = taps - 1 - before
geom_rows = 8
f32 = jnp.float32
bf16 = jnp.bfloat16


def solve_kernel(
    capacity,
    lat_total,
    lon_total,
    live_ref,
    rows_hbm,
    owner_hbm,
    lat_hbm,
    lon_hbm,
    pos_hbm,
    feat_hbm,
    weight_hbm,
    ig_ref,
    gathered,
    *refs,
):
    (rows_ref, owner_ref, lat_ref, lon_ref, pos_ref, weight_ref) = refs[:6]
    (field, stage, beside, edges) = refs[6:10]
    (held, inbox, sums, canvas, lat_taps, lon_taps, halves) = refs[10:17]
    strips, landed = refs[17:25], refs[25:33]
    (windows, turned, total, flat, mixer, pieces, twin, parts, mine) = refs[33:42]
    (load_sem, send_sem, recv_sem, field_send, field_recv) = refs[42:47]
    halo_send, halo_recv, pair_send, pair_recv, part_send, part_recv, all_send, all_recv = refs[47:]
    devices = inbox.shape[0]
    row_total, channels = rows_ref.shape
    tile_lat, tile_lon = ig_ref.shape[:2]
    up, down = before + 1, after + 1
    tall = canvas.shape[0]
    own_field = field.at[up : up + tile_lat]
    lat, lon = lax.axis_index("lat"), lax.axis_index("lon")
    me = lon * lat_total + lat
    span = halves.shape[0]
    group = span // capacity
    groups = devices // group
    ours = me // group
    half = tile_lon // 2
    inv = 1.0 / (2.0 * rbf_scale * rbf_scale)

    def place(peer):
        return (peer % lat_total, peer // lat_total)

    barrier = pltpu.get_barrier_semaphore()

    def greet(k, _):
        pl.semaphore_signal(
            barrier, inc=1, device_id=place((me + k) % devices), device_id_type=pl.DeviceIdType.MESH
        )
        return 0

    loads = [
        pltpu.make_async_copy(src, dst, load_sem.at[k])
        for k, (src, dst) in enumerate(
            zip(
                (rows_hbm, owner_hbm, lat_hbm, lon_hbm, pos_hbm, feat_hbm, weight_hbm),
                (rows_ref, owner_ref, lat_ref, lon_ref, pos_ref, own_field, weight_ref),
            )
        )
    ]
    for load in loads:
        load.start()
    lax.fori_loop(1, devices, greet, 0)
    sums[...] = jnp.zeros_like(sums)
    mixer[...] = jnp.zeros_like(mixer)
    total[...] = jnp.zeros_like(total)
    rows, cols = tile_lat + 2, tile_lon + 2
    stage[...] = jnp.zeros_like(stage)
    for margin in (slice(0, 8), slice(canvas.shape[1] - 8, canvas.shape[1])):
        canvas[:, margin, :] = jnp.zeros((tall, 8, channels), f32)
    field[tall + 1] = jnp.zeros(field.shape[1:], bf16)

    @pl.when(lat == 0)
    def _():
        field[0:up] = jnp.zeros((up,) + field.shape[1:], bf16)

    @pl.when(lat == lat_total - 1)
    def _():
        field[up + tile_lat : tall + 1] = jnp.zeros((down,) + field.shape[1:], bf16)

    for load in loads[:5]:
        load.wait()

    live = lax.broadcasted_iota(jnp.int32, (1, row_total), 1) < live_ref[0]
    tile = owner_ref[...].astype(f32)
    tile_row = jnp.floor((tile + 0.5) * (1.0 / lon_total))
    owner = (tile - tile_row * lon_total) * lat_total + tile_row
    owner = jnp.where(live, owner, float(devices)).astype(jnp.int32)
    match = lax.broadcasted_iota(jnp.int32, (devices, row_total), 0) == owner
    match = jnp.where(match, 1.0, 0.0)
    blocks = row_total // 128
    upper = lax.broadcasted_iota(jnp.int32, (128, 128), 0) < lax.broadcasted_iota(
        jnp.int32, (128, 128), 1
    )
    upper = jnp.where(upper, 1.0, 0.0).astype(bf16)
    columns = [match[:, k * 128 : (k + 1) * 128] for k in range(blocks)]
    earlier = jnp.dot(
        jnp.concatenate(columns, axis=0).astype(bf16), upper, preferred_element_type=f32
    )
    before_block = jnp.zeros((devices, 1), f32)
    ranks = []
    for k, part in enumerate(columns):
        ahead = earlier[k * devices : (k + 1) * devices] + before_block
        ranks.append(jnp.sum(ahead * part, axis=0, keepdims=True))
        before_block = before_block + jnp.sum(part, axis=1, keepdims=True)
    rank = jnp.concatenate(ranks, axis=1).astype(jnp.int32)
    slot = owner * capacity + rank
    geometry = jnp.concatenate(
        [
            pos_ref[...].astype(f32),
            lat_ref[...].astype(f32),
            lon_ref[...].astype(f32),
            jnp.zeros((geom_rows - 4, row_total), f32),
        ],
        axis=0,
    ).astype(bf16)
    fold = 128 // capacity
    chunk = math.gcd(group, max(1, 256 // capacity))
    line = lax.broadcasted_iota(jnp.int32, (chunk * capacity, row_total), 0)
    lane_block = lax.broadcasted_iota(jnp.int32, (geom_rows, 128), 1) // capacity

    def build(first):
        hit = jnp.where(line == slot - first * capacity, 1.0, 0.0).astype(bf16)
        placed = jnp.dot(hit, rows_ref[...], preferred_element_type=f32).astype(bf16)
        info = lax.dot_general(
            geometry, hit, (((1,), (1,)), ((), ())), preferred_element_type=f32
        )
        for i in range(chunk):
            held[first + i, 0:capacity, :] = placed[i * capacity : (i + 1) * capacity]
        for v in range(chunk // fold):
            piece = info[:, v * 128 : (v + 1) * 128]
            rolled = [piece] + [pltpu.roll(piece, s * capacity, 1) for s in range(1, fold)]
            for i in range(fold):
                tiled = rolled[(fold - i) % fold]
                for t in range(1, fold):
                    tiled = jnp.where(lane_block == t, rolled[(t - i) % fold], tiled)
                held[first + v * fold + i, capacity : capacity + geom_rows, :] = tiled.astype(bf16)

    def copy_to(peer, slot_at):
        return pltpu.make_async_remote_copy(
            src_ref=held.at[peer],
            dst_ref=inbox.at[slot_at],
            send_sem=send_sem.at[peer],
            recv_sem=recv_sem.at[slot_at],
            device_id=place(peer),
            device_id_type=pl.DeviceIdType.MESH,
        )

    def send(first):
        for i in range(chunk):
            peer = first + i

            @pl.when(peer != me)
            def _():
                copy_to(peer, me).start()

    if groups == 4:
        order = [(ours + 2) % 4, 3 - ours, ours + 1 - 2 * (ours % 2), ours]
    else:
        order = [(ours + groups // 2 + k) % groups for k in range(groups)]
    per = group // chunk
    steps = [(q, c) for q in order for c in range(per)]
    first_of = [q * group + c * chunk for q, c in steps]
    early = len(first_of) // 2
    for first in first_of[:early]:
        build(first)
    pl.semaphore_wait(barrier, devices - 1)
    for first in first_of[:early]:
        send(first)
    for first in first_of[early:]:
        build(first)
        send(first)
    inbox[me] = held[me]

    loads[5].wait()

    def when(da, cond, fn):
        if da == 0:
            fn()
        else:
            pl.when(cond)(fn)

    ways = ((-1, 0), (1, 0), (0, -1), (0, 1), (-1, -1), (-1, 1), (1, -1), (1, 1))
    reach = 8
    borders = []
    for w, (da, source, target) in enumerate(
        (
            (-1, slice(up, up + down), slice(up + tile_lat, tall + 1)),
            (1, slice(tile_lat, up + tile_lat), slice(0, up)),
        )
    ):
        copy = pltpu.make_async_remote_copy(
            src_ref=field.at[source],
            dst_ref=field.at[target],
            send_sem=field_send.at[w],
            recv_sem=field_recv.at[w],
            device_id=((lat + da + lat_total) % lat_total, lon),
            device_id_type=pl.DeviceIdType.MESH,
        )
        sends = (lat + da >= 0) & (lat + da < lat_total)
        takes = (lat - da >= 0) & (lat - da < lat_total)
        borders.append((copy, sends, takes))
    for (copy, sends, _), (da, _) in zip(borders, ways):
        when(da, sends, copy.start)

    def aligned(start, size):
        if not isinstance(start, int):
            start = pl.multiple_of(start, tile_lon)
        return pl.ds(start, size)

    def turn(p):
        turned[:, aligned(p * tile_lon, tile_lon)] = field[p].T

    fast = math.gcd(tile_lat, 8)

    def turn_some(k, _):
        for j in range(fast):
            turn(up + k * fast + j)
        return 0

    lax.fori_loop(0, tile_lat // fast, turn_some, 0)
    loads[6].wait()
    for a in range(3):
        for b in range(3):
            tap = weight_ref[a, b].T
            for r in range(2):
                at = ((r + 2 - a) * 3 + b) * channels
                mixer[at : at + channels, r * channels : (r + 1) * channels] = tap

    line_lat = lax.broadcasted_iota(jnp.int32, (lat_taps.shape[0], span), 0).astype(f32)
    line_lon = lax.broadcasted_iota(jnp.int32, (lon_taps.shape[0], span), 0).astype(f32)
    lanes = lax.broadcasted_iota(jnp.int32, (8, 128), 1) // capacity
    wide = sums.shape[1]
    line_lon = jnp.where(line_lon >= wide, line_lon - wide, line_lon)
    stride = next(n for n in (36, 24, 12, 8, 4, 2) if tall % n == 0)

    def taps_of(line, base, frac):
        tap = line - base
        d = tap - (frac + before)
        weight = jnp.exp(-(d * d) * inv)
        return jnp.where((tap >= 0.0) & (tap <= taps - 1.0), weight, 0.0)

    pad = reach

    def collect(q, last):
        for i in range(group):
            peer = q * group + i

            @pl.when(peer != me)
            def _():
                copy_to(peer, peer).wait_recv()

        first = q * group
        infos = []
        for v in range(span // 128):
            at = first + v * fold
            info = inbox[at, capacity : capacity + geom_rows, :].astype(f32)
            for t in range(1, fold):
                info = jnp.where(
                    lanes == t, inbox[at + t, capacity : capacity + geom_rows, :].astype(f32), info
                )
            infos.append(info)
        info = jnp.concatenate(infos, axis=1)
        lat_frac, lon_frac, row_at, col_at = (info[k : k + 1] for k in range(4))
        right = jnp.where(col_at >= half, 1.0, 0.0)
        lat_taps[...] = taps_of(line_lat, row_at, lat_frac).astype(bf16).astype(f32)
        lon_taps[...] = taps_of(line_lon, col_at - right * half, lon_frac).astype(bf16)
        for v in range(span // 128):
            side = jnp.broadcast_to(right[:, v * 128 : (v + 1) * 128], (128, 128)).T.astype(bf16)
            rows = jnp.concatenate(
                [inbox[first + v * fold + t, 0:capacity, :] for t in range(fold)], axis=0
            )
            at = slice(v * 128, (v + 1) * 128)
            on_right = rows * side
            halves[at, 0:channels] = rows - on_right
            halves[at, channels : 2 * channels] = on_right

        def add(k, _):
            lhs = []
            for j in range(0, stride, 2):
                pair = [
                    jnp.broadcast_to(lat_taps[pl.ds(k * stride + j + n, 1), :], (8, span))
                    for n in range(2)
                ]
                for t in range(0, 2 * wide, 16):
                    row = jnp.concatenate([pair[t // wide], pair[(t + 8) // wide]], axis=0)
                    lhs.append(row.astype(bf16) * lon_taps[t : t + 16, :])
            out = jnp.dot(jnp.concatenate(lhs, axis=0), halves[...], preferred_element_type=f32)
            for j in range(stride):
                i = k * stride + j
                row = sums[i] + out[j * wide : (j + 1) * wide]
                if not last:
                    sums[i] = row
                    continue
                left, right = row[:, 0:channels], row[:, channels : 2 * channels]
                canvas[i, pad : pad + half, :] = left[0:half]
                canvas[i, pad + half : pad + wide, :] = left[half:wide] + right[0 : wide - half]
                canvas[i, pad + wide : pad + wide + half, :] = right[wide - half : wide]
            return 0

        lax.fori_loop(0, tall // stride, add, 0)

    slots = 2 * reach
    rows_at_once = 128 // slots
    last_chunk = tall // rows_at_once - 1

    def flank(chunks):
        for a in range(3):
            for k in chunks:
                at = slice(a + k * rows_at_once, a + (k + 1) * rows_at_once)
                both = jnp.concatenate(
                    [field[at, 0:reach], field[at, tile_lon - reach : tile_lon]], axis=1
                )
                beside[a * channels : (a + 1) * channels, k * 128 : (k + 1) * 128] = both.reshape(
                    128, channels
                ).T

    def border():
        for (copy, _, takes), (da, _) in zip(borders, ways):
            when(da, takes, copy.wait_recv)
        for p in (*range(up), *range(up + tile_lat, tall + 2)):
            turn(p)
        flank((0, last_chunk))

    for k, q in enumerate([order[3], order[2], order[0], order[1]] if groups == 4 else order[::-1]):
        if k == groups - 1:
            flank(range(1, last_chunk))
        collect(q, k == groups - 1)

    inset = before - 1
    edge = pad + inset

    @pl.when(lat == 0)
    def _():
        canvas[0:before] = jnp.zeros((before,) + canvas.shape[1:], f32)

    @pl.when(lat == lat_total - 1)
    def _():
        canvas[before + tile_lat : tall] = jnp.zeros((tall - before - tile_lat,) + canvas.shape[1:], f32)

    some = math.gcd(tall, 4)

    def emit(k, _):
        for j in range(some):
            i = k * some + j
            strips[2][i] = canvas[i, pad : pad + up, :].astype(bf16)
            strips[3][i] = canvas[i, edge + cols - 2 : edge + cols - 2 + down, :].astype(bf16)
        return 0

    lax.fori_loop(0, tall // some, emit, 0)
    halos = []
    for w, (da, db) in enumerate(ways):
        copy = pltpu.make_async_remote_copy(
            src_ref=strips[w],
            dst_ref=landed[w],
            send_sem=halo_send.at[w],
            recv_sem=halo_recv.at[w],
            device_id=((lat + da + lat_total) % lat_total, (lon + db + lon_total) % lon_total),
            device_id_type=pl.DeviceIdType.MESH,
        )
        sends = (lat + da >= 0) & (lat + da < lat_total)
        takes = (lat - da >= 0) & (lat - da < lat_total)
        halos.append((copy, sends, takes))
    beside_halos = halos[2:4]
    for copy, _, _ in beside_halos:
        copy.start()
    spans = ((pad, up), (edge, cols), (edge + cols - 2, down))
    for count, first, refs in (
        (up, 0, (strips[4], strips[0], strips[5])),
        (down, inset + rows - 2, (strips[6], strips[1], strips[7])),
    ):
        for i in range(count):
            for (start, width), ref in zip(spans, refs):
                ref[i] = canvas[first + i, start : start + width, :].astype(bf16)
    for (copy, sends, _), (da, _) in zip(halos, ways):
        if da != 0:
            pl.when(sends)(copy.start)
    chips = devices // 2
    planes = lon_total // 2
    outer = planes // 4
    inner = planes - 2 * outer
    roots = lat_total * inner
    plane, core = lon // 2, lon % 2
    chip = lat * planes + plane
    other = 1 - core
    is_root = (plane >= outer) & (plane < planes - outer)
    root = lat * inner + plane - outer

    def seat(peer):
        return (peer // planes, (peer % planes) * 2 + core)

    def chip_of(r):
        return (r // inner) * planes + r % inner + outer

    def shift_row(i):
        at = pl.ds(pl.multiple_of(i * tile_lon, tile_lon), tile_lon)
        for b in range(3):
            windows[at, b * channels : (b + 1) * channels] = canvas[
                i, edge + 2 - b : edge + 2 - b + tile_lon, :
            ].astype(bf16)

    def shift(k, _):
        for j in range(2):
            shift_row(2 * k + j)
        return 0

    lax.fori_loop(0, tall // 2, shift, 0)

    def shift_edges(k, _):
        for j in range(some):
            i = k * some + j
            stage[i, 0:down] = landed[3][i].astype(f32)
            stage[i, 3 * reach : 3 * reach + up] = landed[2][i].astype(f32)
            at = pl.ds(pl.multiple_of(i * 2 * reach, 2 * reach), 2 * reach)
            for b in range(3):
                first, second = 2 - b, 2 * reach + up - b
                both = [stage[i, first : first + reach, :], stage[i, second : second + reach, :]]
                edges[at, b * channels : (b + 1) * channels] = jnp.concatenate(
                    both, axis=0
                ).astype(bf16)
        return 0

    step = next(n for n in (12, 8, 6, 4, 3, 2, 1) if tall % n == 0)
    depth = step * tile_lon

    def weigh(k, _):
        start = k * depth
        lhs = jnp.concatenate(
            [
                turned[:, aligned(start + a * tile_lon, depth)]
                for a in range(3)
            ],
            axis=0,
        )
        rhs = windows[aligned(start, depth), :]
        total[...] += jnp.dot(lhs, rhs, preferred_element_type=f32)
        return 0

    last_step = tall // step - 1
    lax.fori_loop(1, last_step, weigh, 0)
    border()
    weigh(0, 0)
    weigh(last_step, 0)
    for copy, _, _ in beside_halos:
        copy.wait_recv()
    lax.fori_loop(0, tall // some, shift_edges, 0)
    total[...] += jnp.dot(beside[...], edges[...], preferred_element_type=f32)
    for a in range(3):
        for b in range(3):
            at = (a * 3 + b) * channels
            flat[at : at + channels, :] = total[
                a * channels : (a + 1) * channels, b * channels : (b + 1) * channels
            ]
    share = pieces.shape[1]

    def cut(d, _):
        pieces[d] = flat[pl.ds(d * share, share), :].astype(bf16)
        return 0

    lax.fori_loop(0, 2 * roots, cut, 0, unroll=4)
    part = math.gcd(tile_lat // 2, 8)
    strides = tile_lat // 2 // part

    def apply(k, _):
        lhs = jnp.concatenate(
            [
                jnp.concatenate(
                    [
                        windows[
                            pl.ds(
                                pl.multiple_of(
                                    (inset + 2 * (k * part + j) + r) * tile_lon, tile_lon
                                ),
                                tile_lon,
                            ),
                            :,
                        ]
                        for r in range(4)
                    ],
                    axis=1,
                )
                for j in range(part)
            ],
            axis=0,
        )
        acc = jnp.dot(lhs, mixer[...], preferred_element_type=f32).astype(bf16)
        for j in range(part):
            for r in range(2):
                ig_ref[2 * (k * part + j) + r] = acc[
                    j * tile_lon : (j + 1) * tile_lon, r * channels : (r + 1) * channels
                ]
        return 0

    def settle():
        for (copy, _, takes), (da, db), ref in zip(halos, ways, landed):

            def take(copy=copy, da=da, db=db, ref=ref):
                if da != 0:
                    copy.wait_recv()
                high = {-1: inset + rows - up, 0: 0, 1: inset}[da]
                count = {-1: up, 0: tall, 1: down}[da]
                left = {-1: cols - up, 0: 0, 1: 0}[db]
                width = {-1: up, 0: cols, 1: down}[db]

                def add(i, _):
                    canvas[high + i, edge + left : edge + left + width, :] += ref[i].astype(f32)
                    return 0

                lax.fori_loop(0, count, add, 0)

            when(da, takes, take)

        lax.fori_loop(inset // 2, (inset + rows) // 2, shift, 0)

    def paired(src, dst, n):
        return pltpu.make_async_remote_copy(
            src_ref=src,
            dst_ref=dst,
            send_sem=pair_send.at[n],
            recv_sem=pair_recv.at[n],
            device_id=(lat, plane * 2 + other),
            device_id_type=pl.DeviceIdType.MESH,
        )

    def scattered(r, slot):
        return pltpu.make_async_remote_copy(
            src_ref=pieces.at[core * roots + r],
            dst_ref=parts.at[slot],
            send_sem=part_send.at[r],
            recv_sem=part_recv.at[slot],
            device_id=seat(chip_of(r)),
            device_id_type=pl.DeviceIdType.MESH,
        )

    def shared(peer, r):
        return pltpu.make_async_remote_copy(
            src_ref=mine,
            dst_ref=gathered.at[core * roots + r],
            send_sem=all_send.at[peer],
            recv_sem=all_recv.at[r],
            device_id=seat(peer),
            device_id_type=pl.DeviceIdType.MESH,
        )

    def each_root(fn):
        def body(k, _):
            r = (chip + k) % roots

            @pl.when(chip_of(r) != chip)
            def _():
                fn(r)

            return 0

        lax.fori_loop(0, roots, body, 0)

    def each_chip(fn):
        def body(k, _):
            fn((chip + k) % chips)
            return 0

        lax.fori_loop(1, chips, body, 0)

    swap = paired(pieces.at[pl.ds(other * roots, roots)], twin, 0)
    swap.start()
    swap.wait_recv()

    def merge(p, _):
        at = core * roots + p
        pieces[at] = (flat[pl.ds(at * share, share), :] + twin[p].astype(f32)).astype(bf16)
        return 0

    lax.fori_loop(0, roots, merge, 0, unroll=4)
    each_root(lambda r: scattered(r, chip).start())

    @pl.when(is_root)
    def _():
        parts[chip] = pieces[core * roots + root]
        each_chip(lambda peer: scattered(root, peer).wait_recv())

        def gather_sum(p, acc):
            return acc + parts[p].astype(f32)

        mine[...] = lax.fori_loop(
            0, chips, gather_sum, jnp.zeros((share, channels), f32), unroll=4
        ).astype(bf16)
        each_chip(lambda peer: shared(peer, root).start())
        gathered[core * roots + root] = mine[...]

    settle()
    lax.fori_loop(0, strides, apply, 0)
    each_root(lambda r: shared(chip, r).wait_recv())
    kept = gathered.at[pl.ds(core * roots, roots)]
    back = paired(kept, kept, 1)
    back.start()
    back.wait_recv()
    for (copy, sends, _), (da, _) in zip(halos + borders, ways + ways[:2]):
        when(da, sends, copy.wait_send)
    swap.wait_send()
    back.wait_send()
    each_root(lambda r: scattered(r, chip).wait_send())

    @pl.when(is_root)
    def _():
        each_chip(lambda peer: shared(peer, root).wait_send())


    def each(fn):
        def body(k, _):
            fn((me + k) % devices)
            return 0

        lax.fori_loop(1, devices, body, 0)

    each(lambda peer: copy_to(peer, me).wait_send())


def finish_kernel(grad_ref, shares_ref, grad_out, weight_out, flat, sem):
    grad_copy = pltpu.make_async_copy(grad_ref, grad_out, sem.at[0])
    grad_copy.start()
    share = shares_ref.shape[1]
    for d in range(shares_ref.shape[0]):
        flat[d * share : (d + 1) * share, :] = shares_ref[d].astype(f32)
    weight_copy = pltpu.make_async_copy(flat, weight_out, sem.at[1])
    weight_copy.start()
    grad_copy.wait()
    weight_copy.wait()


def shards(grad_rows, owner, lat_offset, lon_offset, position, live_count, features, conv_weight):
    lat_total = lax.axis_size("lat")
    lon_total = lax.axis_size("lon")
    device_total = lat_total * lon_total
    row_total, channels = grad_rows.shape
    tile_lat, tile_lon = features.shape[:2]
    capacity = max(2, 2 * row_total // device_total)
    smem = pl.BlockSpec(memory_space=pltpu.SMEM)
    vmem = pl.BlockSpec(memory_space=pltpu.VMEM)

    rows, cols = tile_lat + 2, tile_lon + 2
    tall = -(-(tile_lat + taps - 1) // 8) * 8
    wide = tile_lon // 2 + 8
    span = math.gcd(device_total, max(1, 512 // capacity)) * capacity
    up, down = before + 1, after + 1
    strip_shapes = [
        (up, cols),
        (down, cols),
        (tall, up),
        (tall, down),
        (up, up),
        (up, down),
        (down, up),
        (down, down),
    ]
    message = (device_total, capacity + geom_rows, channels)
    flat_rows = 9 * channels
    chips = device_total // 2
    roots = lat_total * (lon_total // 2 - 2 * (lon_total // 8))
    share = flat_rows // (2 * roots)
    dma = pltpu.SemaphoreType.DMA
    places = [pltpu.VMEM(shape + (channels,), bf16) for shape in strip_shapes]
    operands = (
        grad_rows,
        owner.reshape(1, row_total),
        lat_offset.reshape(1, row_total),
        lon_offset.reshape(1, row_total),
        position.T,
        features,
        conv_weight,
    )
    inner_grad, shares = pl.pallas_call(
        functools.partial(solve_kernel, capacity, lat_total, lon_total),
        out_shape=[
            jax.ShapeDtypeStruct((tile_lat, tile_lon, channels), bf16),
            jax.ShapeDtypeStruct((2 * roots, share, channels), bf16),
        ],
        in_specs=[smem] + [pl.BlockSpec(memory_space=pltpu.HBM)] * 7,
        out_specs=[vmem] * 2,
        scratch_shapes=[pltpu.VMEM(x.shape, x.dtype) for x in operands if x is not features]
        + [
            pltpu.VMEM((tall + 2, tile_lon, channels), bf16),
            pltpu.VMEM((tall, 32, channels), f32),
            pltpu.VMEM((3 * channels, tall * 16), bf16),
            pltpu.VMEM((tall * 16, 3 * channels), bf16),
            pltpu.VMEM(message, bf16),
            pltpu.VMEM(message, bf16),
            pltpu.VMEM((tall, wide, 2 * channels), f32),
            pltpu.VMEM((tall, wide + tile_lon // 2 + 16, channels), f32),
            pltpu.VMEM((tall, span), f32),
            pltpu.VMEM((2 * wide, span), bf16),
            pltpu.VMEM((span, 2 * channels), bf16),
        ]
        + places
        + places
        + [
            pltpu.VMEM((tall * tile_lon, 3 * channels), bf16),
            pltpu.VMEM((channels, (tall + 2) * tile_lon), bf16),
            pltpu.VMEM((3 * channels, 3 * channels), f32),
            pltpu.VMEM((flat_rows, channels), f32),
            pltpu.VMEM((4 * 3 * channels, 2 * channels), bf16),
            pltpu.VMEM((2 * roots, share, channels), bf16),
            pltpu.VMEM((roots, share, channels), bf16),
            pltpu.VMEM((chips, share, channels), bf16),
            pltpu.VMEM((share, channels), bf16),
            dma((7,)),
            dma((device_total,)),
            dma((device_total,)),
            dma((2,)),
            dma((2,)),
            dma((8,)),
            dma((8,)),
            dma((2,)),
            dma((2,)),
            dma((roots,)),
            dma((chips,)),
            dma((chips,)),
            dma((roots,)),
        ],
        compiler_params=pltpu.CompilerParams(
            vmem_limit_bytes=44 * 2**20, collective_id=0, has_side_effects=True
        ),
        name="solve",
    )(live_count, *[pltpu.with_memory_space_constraint(x, pltpu.HBM) for x in operands])
    input_grad, weight_grad = pl.pallas_call(
        finish_kernel,
        out_shape=[
            jax.ShapeDtypeStruct((tile_lat, tile_lon, channels), bf16),
            jax.ShapeDtypeStruct((flat_rows, channels), f32),
        ],
        in_specs=[vmem] * 2,
        out_specs=[pl.BlockSpec(memory_space=pltpu.HBM)] * 2,
        scratch_shapes=[pltpu.VMEM((flat_rows, channels), f32), dma((2,))],
        compiler_params=pltpu.CompilerParams(vmem_limit_bytes=8 * 2**20),
        name="finish",
    )(inner_grad, shares)
    return input_grad, weight_grad.reshape(3, 3, channels, channels)


def solution(mesh):
    placed = (
        P(("lat", "lon"), None),
        P(("lat", "lon"), None),
        P(("lat", "lon")),
        P(("lat", "lon")),
        P(("lat", "lon"), None),
        P(("lat", "lon")),
        P("lat", "lon", None),
        P(),
    )
    return jax.shard_map(
        shards, mesh=mesh, in_specs=placed, out_specs=(P("lat", "lon", None), P()), check_vma=False
    )
```
